128 devices in a mesh: gx: 16 (over x_lo, z, core), gy: 8 (over y, x_hi).
Axes of the slice: x: 4 (x_hi: 2, x_lo: 2; x = x_hi * 2 + x_lo), y: 4, z: 4, core: 2. Of those that a mesh axis runs over, the one named last changes fastest.
Arguments:
- features: bfloat16 [16, 8, 2048, 128], P('gx', 'gy'), may hold values from -96 to 96
- positions: float32 [16, 8, 3, 2048], P('gx', 'gy'), may hold values from 0 to 576, as said below
- counts: int32 [16, 8], P(None, 'gy'), may hold values from 769 to 2048, as said below
- neighbours: int32 [16, 8, 16, 4], P('gx', 'gy'), may hold values from 0 to 143, as said below
- w_query: bfloat16 [128, 128], replicated, may hold values from -0.5 to 0.5
- w_key: bfloat16 [128, 128], replicated, may hold values from -0.5 to 0.5
- w_value: bfloat16 [128, 128], replicated, may hold values from -0.5 to 0.5
- w_radial: bfloat16 [16, 64], replicated, may hold values from -1.5 to 1.5
- b_radial: float32 [64], replicated, may hold values from -4 to 4
- w_head: bfloat16 [64, 8], replicated, may hold values from -0.75 to 0.75
Outputs:
- messages: bfloat16 [16, 8, 2048, 128], P('gx', 'gy')
The draws below stay inside these ranges and needn't reach their ends.
Inputs may be any that keep to these rules, and one draw needn't show every extreme that they name: `counts`: in every line of bricks along the first box axis exactly one brick holds min(16, 23) * 128 atoms; every other holds more than max(6, 0) * 128 and at most (7) * 128. `positions`: the first two coordinates lie in 0 to 6. Along the third, all bricks span the same length, 576: live slot s of a brick with c live atoms lies between s and s + 1 times that length over c. `neighbours`: entry 0 of query block q is the block itself, 64 + q; the other entries are live blocks of distinct bricks of the neighbourhood other than the centre.
All inputs are finite; a program needn't handle non-finite values.
Results may differ from the reference program's by a relative error of at most 0.012.
Values may be sent and summed in bfloat16 or wider, within the bound.
No kernel may reach another device: no remote copies, remote signals or barrier semaphores. Data moves between devices by JAX's collectives and lax.ppermute only.
A program may use at most 128 MiB of HBM per device.

```python
import jax
import jax.numpy as jnp
from jax import lax

HEADS = 8
CHANNELS = 128
BASIS = 16
RADIAL = 64
ATOM_BLOCK = 128
KEY_BLOCKS = 4
BLOCKS = 16
SLOTS = 2048
HELPED = 8
ROWS_X = 16
ROWS_Y = 8


def count_law(key):
    dense_key, fill_key = jax.random.split(key)
    dense_row = jax.random.randint(dense_key, (ROWS_Y,), 0, ROWS_X)
    lowest = max(HELPED - 2, 0) * ATOM_BLOCK + 1
    highest = (HELPED - 1) * ATOM_BLOCK + 1
    others = jax.random.randint(fill_key, (ROWS_X, ROWS_Y), lowest, highest)
    dense_count = min(BLOCKS, HELPED + ROWS_X - 1) * ATOM_BLOCK
    row_ids = jnp.arange(ROWS_X)[:, None]
    return jnp.where(row_ids == dense_row[None, :], dense_count, others).astype(jnp.int32)


def draw_counts(key, part):
    return count_law(jax.random.fold_in(key, 7))


def draw_positions(key, part):
    counts_now = count_law(jax.random.fold_in(key, 7))
    plane_key, depth_key, dead_key = jax.random.split(jax.random.fold_in(key, 11), 3)
    plane = jax.random.uniform(plane_key, (ROWS_X, ROWS_Y, 2, SLOTS), jnp.float32, 0.0, 6.0)
    column = float(SLOTS * 9 // 32)
    slot_ids = jnp.arange(SLOTS, dtype=jnp.int32)
    jitter = jax.random.uniform(depth_key, (ROWS_X, ROWS_Y, SLOTS), jnp.float32, 0.0, 1.0)
    live_depth = (slot_ids.astype(jnp.float32)[None, None, :] + jitter) * column / counts_now[:, :, None].astype(jnp.float32)
    dead_depth = jax.random.uniform(dead_key, (ROWS_X, ROWS_Y, SLOTS), jnp.float32, 0.0, column)
    live = slot_ids[None, None, :] < counts_now[:, :, None]
    depth = jnp.minimum(jnp.where(live, live_depth, dead_depth), column)
    return jnp.concatenate([plane, depth[:, :, None, :]], 2).astype(jnp.float32)


def draw_neighbours(key, part):
    counts_now = count_law(jax.random.fold_in(key, 7))
    pick_key = jax.random.fold_in(key, 13)
    scores = jax.random.randint(pick_key, (ROWS_X, ROWS_Y, BLOCKS, 8), 0, 65536)
    distinct = scores * 16 + jnp.arange(8, dtype=jnp.int32)
    ranked = lax.top_k(distinct, KEY_BLOCKS - 1)[1].astype(jnp.int32)
    brick_no = ranked + (ranked >= 4).astype(jnp.int32)
    step_a = brick_no // 3
    step_b = brick_no % 3
    rows_x = jnp.arange(ROWS_X, dtype=jnp.int32)[:, None, None, None]
    rows_y = jnp.arange(ROWS_Y, dtype=jnp.int32)[None, :, None, None]
    other_x = (rows_x + step_a - 1) % ROWS_X
    other_y = (rows_y + step_b - 1) % ROWS_Y
    other_count = counts_now[other_x, other_y]
    own_count = counts_now[:, :, None, None]
    block_ids = jnp.arange(BLOCKS, dtype=jnp.int32)[None, None, :, None]
    centre = block_ids * ATOM_BLOCK + ATOM_BLOCK // 2
    target = centre * other_count // (own_count * ATOM_BLOCK)
    target = jnp.minimum(target, (other_count - 1) // ATOM_BLOCK)
    others = brick_no * BLOCKS + target
    self_block = 4 * BLOCKS + jnp.arange(BLOCKS, dtype=jnp.int32)
    self_full = jnp.broadcast_to(self_block[None, None, :, None], (ROWS_X, ROWS_Y, BLOCKS, 1))
    return jnp.concatenate([self_full, others], 3).astype(jnp.int32)


def draw_features(key, part):
    base_key = jax.random.fold_in(key, 0)
    shape_all = (ROWS_X, ROWS_Y, SLOTS, CHANNELS)
    values = jax.random.truncated_normal(base_key, -6.0, 6.0, shape_all, jnp.float32)
    return values.astype(jnp.bfloat16)


def scatter_about(stream_key, extent, scale, limit, kind=jnp.bfloat16):
    values = jax.random.normal(stream_key, extent, jnp.float32) * scale
    return jnp.minimum(jnp.maximum(values, -limit), limit).astype(kind)


def setup_inputs(seed: int = 0) -> dict:
    arg_keys = jax.random.split(jax.random.key(seed), 11)
    features = draw_features(jax.random.fold_in(arg_keys[10], 71), 0)
    positions = draw_positions(jax.random.fold_in(arg_keys[10], 71), 0)
    counts = draw_counts(jax.random.fold_in(arg_keys[10], 71), 0)
    neighbours = draw_neighbours(jax.random.fold_in(arg_keys[10], 71), 0)
    w_query = scatter_about(arg_keys[4], (CHANNELS, CHANNELS), CHANNELS ** -0.5, 0.5)
    w_key = scatter_about(arg_keys[5], (CHANNELS, CHANNELS), CHANNELS ** -0.5, 0.5)
    w_value = scatter_about(arg_keys[6], (CHANNELS, CHANNELS), CHANNELS ** -0.5, 0.5)
    w_radial = scatter_about(arg_keys[7], (BASIS, RADIAL), BASIS ** -0.5, 1.5)
    b_radial = scatter_about(arg_keys[8], (RADIAL,), 1.0, 4.0, jnp.float32)
    w_head = scatter_about(arg_keys[9], (RADIAL, HEADS), RADIAL ** -0.5, 0.75)
    return dict(features=features, positions=positions, counts=counts, neighbours=neighbours, w_query=w_query, w_key=w_key, w_value=w_value, w_radial=w_radial, b_radial=b_radial, w_head=w_head)


CUTOFF = 6.0
SHARPNESS = 4.0
MASKED = -1e+30

def attend(query_rows, query_pos, key_rows, key_pos, w_radial, b_radial, w_head):
    channel_count = query_rows.shape[1]
    head_size = channel_count // HEADS
    diff_x = query_pos[0][:, None] - key_pos[0][None, :]
    diff_y = query_pos[1][:, None] - key_pos[1][None, :]
    diff_z = query_pos[2][:, None] - key_pos[2][None, :]
    dist_sq = diff_x * diff_x + diff_y * diff_y + diff_z * diff_z
    valid = (dist_sq < CUTOFF * CUTOFF) & (key_pos[3][None, :] > 0.5) & (query_pos[3][:, None] > 0.5)
    inside = 1.0 - dist_sq / (CUTOFF * CUTOFF)
    envelope = 2.0 * jnp.log(jnp.where(valid, inside, 1.0))
    distance = jnp.sqrt(dist_sq)
    basis_count = w_radial.shape[0]
    centres = jnp.arange(basis_count, dtype=jnp.float32) * (CUTOFF / (basis_count - 1))
    basis_val = jnp.exp(-SHARPNESS * (distance[None] - centres[:, None, None]) ** 2).astype(jnp.bfloat16)
    radial_hidden = jnp.einsum('kaj,kh->haj', basis_val.astype(jnp.float32), w_radial.astype(jnp.float32))
    radial_hidden = jax.nn.silu(radial_hidden + b_radial[:, None, None]).astype(jnp.bfloat16)
    head_filter = jnp.einsum('haj,hn->naj', radial_hidden.astype(jnp.float32), w_head.astype(jnp.float32))
    queries = query_rows.reshape(-1, HEADS, head_size).astype(jnp.float32)
    keys_part = key_rows[:, :channel_count].reshape(-1, HEADS, head_size).astype(jnp.float32)
    values_part = key_rows[:, channel_count:].reshape(-1, HEADS, head_size).astype(jnp.float32)
    logits = jnp.einsum('ahd,jhd->haj', queries, keys_part) * head_size ** (-0.5)
    logits = jnp.where(valid[None], logits + envelope[None], MASKED)
    top_score = lax.optimization_barrier(jnp.max(logits, axis=2, keepdims=True))
    expo = jnp.where(valid[None], jnp.exp(logits - top_score), 0.0)
    total = jnp.maximum(lax.optimization_barrier(jnp.sum(expo, axis=2, keepdims=True)), 1.0)
    coeffs = (expo / total * head_filter).astype(jnp.bfloat16)
    merged = jnp.einsum('haj,jhd->ahd', coeffs.astype(jnp.float32), values_part)
    return merged.reshape(query_rows.shape[0], channel_count).astype(jnp.bfloat16)

def reference(features, positions, counts, neighbours, w_query, w_key, w_value, w_radial, b_radial, w_head):
    flat_rows = features.reshape(-1, CHANNELS)
    query_all = jnp.dot(flat_rows, w_query, preferred_element_type=jnp.float32).astype(jnp.bfloat16)
    query_all = query_all.reshape(ROWS_X, ROWS_Y, SLOTS, CHANNELS)
    key_all = jnp.dot(flat_rows, w_key, preferred_element_type=jnp.float32).astype(jnp.bfloat16)
    value_all = jnp.dot(flat_rows, w_value, preferred_element_type=jnp.float32).astype(jnp.bfloat16)
    pairs_all = jnp.concatenate([key_all, value_all], 1).reshape(ROWS_X, ROWS_Y, SLOTS, 2 * CHANNELS)
    live_flag = (jnp.arange(SLOTS, dtype=jnp.int32)[None, None, :] < counts[:, :, None]).astype(jnp.float32)
    pos_all = jnp.concatenate([positions, live_flag[:, :, None, :]], 2)

    def brick(brick_index):
        row_x = brick_index // ROWS_Y
        row_y = brick_index % ROWS_Y
        shell_pairs = []
        shell_pos = []
        for step_a in range(3):
            for step_b in range(3):
                other_x = (row_x + step_a - 1) % ROWS_X
                other_y = (row_y + step_b - 1) % ROWS_Y
                shell_pairs.append(pairs_all[other_x, other_y])
                shift = jnp.array([(step_a - 1) * CUTOFF, (step_b - 1) * CUTOFF, 0.0, 0.0], dtype=jnp.float32)
                shell_pos.append(pos_all[other_x, other_y] + shift[:, None])
        ext_pairs = jnp.stack(shell_pairs, 0).reshape(9 * BLOCKS, ATOM_BLOCK, 2 * CHANNELS)
        ext_pos = jnp.stack(shell_pos, 1).reshape(4, 9 * BLOCKS, ATOM_BLOCK)
        own_count = counts[row_x, row_y]
        lists = neighbours[row_x, row_y]
        own_query = query_all[row_x, row_y]
        own_pos = pos_all[row_x, row_y]

        def block(block_index):
            chosen = lists[block_index]
            key_rows = ext_pairs[chosen].reshape(KEY_BLOCKS * ATOM_BLOCK, 2 * CHANNELS)
            key_pos = ext_pos[:, chosen].reshape(4, KEY_BLOCKS * ATOM_BLOCK)
            start = (block_index * ATOM_BLOCK).astype(jnp.int32)
            query_rows = lax.dynamic_slice_in_dim(own_query, start, ATOM_BLOCK, 0)
            query_pos = lax.dynamic_slice_in_dim(own_pos, start, ATOM_BLOCK, 1)
            return lax.cond(start < own_count, lambda: attend(query_rows, query_pos, key_rows, key_pos, w_radial, b_radial, w_head), lambda: jnp.zeros((ATOM_BLOCK, CHANNELS), jnp.bfloat16))
        return lax.map(block, jnp.arange(BLOCKS, dtype=jnp.int32)).reshape(SLOTS, CHANNELS)
    result = lax.map(brick, jnp.arange(ROWS_X * ROWS_Y, dtype=jnp.int32))
    return result.reshape(ROWS_X, ROWS_Y, SLOTS, CHANNELS)
```

```python
import math

import jax
import jax.numpy as jnp
from jax import lax
from jax.experimental import pallas as pl
from jax.experimental.pallas import tpu as pltpu
from jax.sharding import PartitionSpec as P

HEADS = 8
ATOM_BLOCK = 128
KEY_BLOCKS = 4
CUTOFF = 6.0
SHARPNESS = 4.0
MASKED = -1e30
LENGTH = 576.0
FAR = float(2**20)
POS_ROWS = 16
ROWS = ATOM_BLOCK + POS_ROWS
CHUNK = 8
UNITS = 32
DUMMY = KEY_BLOCKS * ATOM_BLOCK


def make_payload(rows, pos, count):
    slots, channels = rows.shape
    blocks = slots // ATOM_BLOCK
    live = jnp.arange(slots, dtype=jnp.int32) < count
    pos = jnp.concatenate([pos[:2], jnp.where(live, pos[2], FAR)[None]], 0)
    hi = lax.reduce_precision(pos, 8, 7)
    rest = pos - hi
    mid = lax.reduce_precision(rest, 8, 7)
    low = rest - mid
    parts = jnp.stack([hi, mid, low], 1).reshape(9, blocks, ATOM_BLOCK).transpose(1, 0, 2)
    parts = jnp.pad(parts.astype(jnp.bfloat16), ((0, 0), (0, POS_ROWS - 9), (0, 0)))
    return jnp.concatenate([rows.reshape(blocks, ATOM_BLOCK, channels), parts], 1)


def make_units(counts9, own_count, lists):
    blocks = lists.shape[0]
    chunks = ATOM_BLOCK // CHUNK
    ck = counts9[lists // blocks].astype(jnp.float32)[:, None, :]
    t0 = (lists % blocks * ATOM_BLOCK)[:, None, :]
    first = (
        jnp.arange(blocks, dtype=jnp.int32)[:, None] * ATOM_BLOCK
        + jnp.arange(chunks, dtype=jnp.int32)[None, :] * CHUNK
    )[:, :, None]
    cq = own_count.astype(jnp.float32)
    reach = ck * (CUTOFF / LENGTH)
    below = first.astype(jnp.float32) * ck / cq - reach - 1.05
    above = (first + CHUNK).astype(jnp.float32) * ck / cq + reach + 0.05
    lo = jnp.floor(below).astype(jnp.int32) + 1 - t0
    hi = jnp.ceil(above).astype(jnp.int32) - 1 - t0
    lo = jnp.maximum(lo, 0)
    hi = jnp.minimum(hi, ATOM_BLOCK - 1)
    hi = jnp.minimum(hi, ck.astype(jnp.int32) - 1 - t0)
    size = jnp.where(first < own_count, jnp.maximum(hi - lo + 1, 0), 0)
    units = (size + 7) // 8
    start = jnp.minimum(lo, ATOM_BLOCK - 8 * units)
    ends = jnp.cumsum(units, axis=2)
    begins = ends - units
    index = jnp.arange(UNITS, dtype=jnp.int32)[None, None, None, :]
    inside = (index >= begins[..., None]) & (index < ends[..., None])
    base = jnp.arange(KEY_BLOCKS, dtype=jnp.int32)[None, None, :] * ATOM_BLOCK + start - 8 * begins
    rows = jnp.sum(jnp.where(inside, base[..., None] + 8 * index, 0), axis=2)
    rows = jnp.where(index[:, :, 0] < ends[:, :, -1:], rows, DUMMY)
    wide = (ends[:, :, -1] > 16).reshape(blocks, chunks // 2, 2).any(-1)
    return rows.reshape(-1), wide.astype(jnp.int32).reshape(-1)


def attend_kernel(
    count_ref, lists_ref, units_ref, wide_ref, *refs
):
    srcs = refs[:9]
    wq_ref, wkv_ref, w1_ref, b1_ref, w2_ref, out_ref = refs[9:15]
    xbuf, sems, k_s, v_s, p_s, q_s, qp_s, acc_s = refs[15:]
    blocks = srcs[0].shape[0]
    chunks = ATOM_BLOCK // CHUNK
    count = count_ref[0]
    live_blocks = (count + ATOM_BLOCK - 1) // ATOM_BLOCK
    bf16 = jnp.bfloat16
    f32 = jnp.float32

    def fetch(q, slot):
        for e in range(KEY_BLOCKS):
            item = lists_ref[q * KEY_BLOCKS + e]
            brick = item // blocks
            block = item % blocks
            for n in range(9):
                @pl.when(brick == n)
                def _():
                    pltpu.make_async_copy(
                        srcs[n].at[block], xbuf.at[slot, e], sems.at[slot, e]
                    ).start()

    def await_block(slot):
        for e in range(KEY_BLOCKS):
            pltpu.make_async_copy(srcs[0].at[0], xbuf.at[slot, e], sems.at[slot, e]).wait()

    lane = lax.broadcasted_iota(jnp.int32, (CHUNK, 128), 1)
    head_of = lane // 16
    key_terms = []
    query_mask = []
    for a in range(3):
        r = lane % 16
        is_key = (lane < 64) & ((r // 3 == a) & (r < 9) | (r == 9 + a) & (a < 2))
        key_terms.append(jnp.where(is_key, -1.0, 0.0).astype(f32))
        query_mask.append((lane >= 64 + 3 * a) & (lane < 67 + 3 * a))

    tail = lax.broadcasted_iota(jnp.int32, (8, 128), 1)
    k_s[pl.ds(DUMMY, 8), :] = jnp.zeros((8, 128), f32)
    v_s[pl.ds(DUMMY, 8), :] = jnp.zeros((8, 128), f32)
    p_s[pl.ds(DUMMY, 8), :] = jnp.where(
        tail == 6, FAR, jnp.where((tail >= 64) & (tail < 73), 1.0, 0.0)
    ).astype(f32)
    out_ref[...] = jnp.zeros_like(out_ref)

    def gathered(ref, base, groups):
        parts = [ref[pl.ds(units_ref[base + j], 8), :] for j in range(16 * groups)]
        return jnp.concatenate(parts, 0).astype(bf16)

    contract_last = (((1,), (1,)), ((), ()))

    def process(q, chunk_ids, groups):
        width = 128 * groups
        stage = []
        basis_parts = []
        for c in chunk_ids:
            base = (q * chunks + c) * UNITS
            p_g = gathered(p_s, base, groups)
            qp = qp_s[pl.ds(c * CHUNK, CHUNK), :]
            lhs = [jnp.where(query_mask[a], qp, key_terms[a]) for a in range(3)]
            lhs.append(jnp.zeros((8, 128), f32))
            diff = lax.dot_general(
                jnp.concatenate(lhs, 0).astype(bf16), p_g, contract_last,
                preferred_element_type=f32,
            )
            dx, dy, dz = diff[0:8], diff[8:16], diff[16:24]
            r2 = dx * dx + dy * dy + dz * dz
            valid = r2 < CUTOFF * CUTOFF
            inside = 1.0 - r2 * (1.0 / (CUTOFF * CUTOFF))
            env = jnp.where(valid, 2.0 * jnp.log(jnp.where(valid, inside, 1.0)), MASKED)
            scale = math.sqrt(SHARPNESS * math.log2(math.e))
            r = jnp.sqrt(r2) * scale
            basis = []
            for k in range(16):
                t = r - (CUTOFF / 15 * k) * scale
                basis.append(jnp.exp2(-(t * t)))
            basis_parts.append(jnp.concatenate(basis, 0).astype(bf16))
            stage.append((c, base, env))
        basis = basis_parts[0] if len(basis_parts) == 1 else jnp.concatenate(basis_parts, 1)
        hidden = jnp.dot(w1_ref[...], basis, preferred_element_type=f32)
        bias = b1_ref[...]
        hidden = hidden + jnp.concatenate([bias] * (hidden.shape[1] // 128), 1)
        hidden = (hidden + hidden * jnp.tanh(hidden)).astype(bf16)
        filt = jnp.dot(w2_ref[...], hidden, preferred_element_type=f32)
        for i, (c, base, env) in enumerate(stage):
            k_g = gathered(k_s, base, groups)
            v_g = gathered(v_s, base, groups)
            qc = q_s[pl.ds(c * CHUNK, CHUNK), :]
            q_exp = jnp.concatenate(
                [jnp.where(head_of == h, qc, 0.0) for h in range(HEADS)], 0
            ).astype(bf16)
            logit = lax.dot_general(q_exp, k_g, contract_last, preferred_element_type=f32)
            coefs = []
            dens = []
            for h in range(HEADS):
                row = logit[8 * h : 8 * h + 8] + env
                top = jnp.max(row, axis=1, keepdims=True)
                expo = jnp.exp(row - top)
                coefs.append(expo * filt[8 * h : 8 * h + 8, width * i : width * (i + 1)])
                dens.append(jnp.sum(expo, axis=1, keepdims=True))
            coef = jnp.concatenate(coefs, 0).astype(bf16)
            num = jnp.dot(coef, v_g, preferred_element_type=f32)
            res = num[0:8]
            den = jnp.broadcast_to(dens[0], (8, 128))
            for h in range(1, HEADS):
                res = jnp.where(head_of == h, num[8 * h : 8 * h + 8], res)
                den = jnp.where(head_of == h, dens[h], den)
            acc_s[pl.ds(c * CHUNK, CHUNK), :] = res / jnp.maximum(den, 1.0)

    fetch(0, 0)

    def block_body(q, carry):
        slot = q % 2
        await_block(slot)

        @pl.when(q + 1 < live_blocks)
        def _():
            fetch(q + 1, 1 - slot)

        mats = []
        sub = lax.broadcasted_iota(jnp.int32, (POS_ROWS, 128), 0)
        for e in range(KEY_BLOCKS):
            brick = lists_ref[q * KEY_BLOCKS + e] // blocks
            shift_x = ((brick // 3 - 1).astype(f32)) * CUTOFF
            shift_y = ((brick % 3 - 1).astype(f32)) * CUTOFF
            m = xbuf[slot, e, ATOM_BLOCK:, :].astype(f32)
            mats.append(jnp.where(sub == 9, shift_x, jnp.where(sub == 10, shift_y, m)))
        mats.append(xbuf[slot, 0, ATOM_BLOCK:, :].astype(f32))
        mats.append(jnp.zeros((48, 128), f32))
        turned = jnp.transpose(jnp.concatenate(mats, 0))
        wide_lane = lax.broadcasted_iota(jnp.int32, (128, 128), 1)
        ones = jnp.where((wide_lane >= 64) & (wide_lane < 73), 1.0, 0.0).astype(f32)
        qp_s[...] = turned
        for e in range(KEY_BLOCKS):
            p_s[pl.ds(e * ATOM_BLOCK, ATOM_BLOCK), :] = jnp.where(
                wide_lane // 16 == e, turned, ones
            )
            x = xbuf[slot, e, :ATOM_BLOCK, :]
            kv = jnp.dot(x, wkv_ref[...], preferred_element_type=f32)
            kv = kv.astype(bf16).astype(f32)
            k_s[pl.ds(e * ATOM_BLOCK, ATOM_BLOCK), :] = kv[:, :128]
            v_s[pl.ds(e * ATOM_BLOCK, ATOM_BLOCK), :] = kv[:, 128:]
        query = jnp.dot(xbuf[slot, 0, :ATOM_BLOCK, :], wq_ref[...], preferred_element_type=f32)
        q_s[...] = query.astype(bf16).astype(f32) * 0.25

        left = count - q * ATOM_BLOCK
        pairs = jnp.minimum((left + 2 * CHUNK - 1) // (2 * CHUNK), chunks // 2)

        def pair_body(p, carry):
            wide = wide_ref[q * (chunks // 2) + p]

            @pl.when(wide == 0)
            def _():
                process(q, (2 * p, 2 * p + 1), 1)

            @pl.when(wide != 0)
            def _():
                for i in range(2):
                    process(q, (2 * p + i,), 2)

            return carry

        lax.fori_loop(0, pairs, pair_body, 0)
        row_id = lax.broadcasted_iota(jnp.int32, (ATOM_BLOCK, 128), 0)
        out_ref[pl.ds(pl.multiple_of(q * ATOM_BLOCK, ATOM_BLOCK), ATOM_BLOCK), :] = jnp.where(
            row_id < left, acc_s[...], 0.0
        ).astype(bf16)
        return carry

    lax.fori_loop(0, live_blocks, block_body, 0)


def attend(count, lists, units, wide, srcs, wq, wkv, w1, b1, w2):
    blocks = srcs[0].shape[0]
    channels = srcs[0].shape[2]
    smem = pl.BlockSpec(memory_space=pltpu.SMEM)
    vmem = pl.BlockSpec(memory_space=pltpu.VMEM)
    hbm = pl.BlockSpec(memory_space=pl.ANY)
    f32 = jnp.float32
    return pl.pallas_call(
        attend_kernel,
        out_shape=jax.ShapeDtypeStruct((blocks * ATOM_BLOCK, channels), jnp.bfloat16),
        in_specs=[smem] * 4 + [hbm] * 9 + [vmem] * 5,
        out_specs=vmem,
        scratch_shapes=[
            pltpu.VMEM((2, KEY_BLOCKS, ROWS, channels), jnp.bfloat16),
            pltpu.SemaphoreType.DMA((2, KEY_BLOCKS)),
            pltpu.VMEM((DUMMY + 8, 128), f32),
            pltpu.VMEM((DUMMY + 8, 128), f32),
            pltpu.VMEM((DUMMY + 8, 128), f32),
            pltpu.VMEM((ATOM_BLOCK, 128), f32),
            pltpu.VMEM((ATOM_BLOCK, 128), f32),
            pltpu.VMEM((ATOM_BLOCK, 128), f32),
        ],
        name="attend",
    )(count, lists, units, wide, *srcs, wq, wkv, w1, b1, w2)


def make_weights(w_query, w_key, w_value, w_radial, b_radial, w_head):
    basis, radial = w_radial.shape
    eye = jnp.eye(CHUNK, dtype=jnp.bfloat16)
    w1 = (w_radial.T * jnp.bfloat16(0.5))[:, None, :, None] * eye[None, :, None, :]
    w1 = w1.reshape(radial * CHUNK, basis * CHUNK)
    w2 = w_head.T[:, None, :, None] * eye[None, :, None, :]
    w2 = w2.reshape(HEADS * CHUNK, radial * CHUNK)
    b1 = jnp.broadcast_to((0.5 * b_radial)[:, None, None], (radial, CHUNK, 128))
    return (
        w_query, jnp.concatenate([w_key, w_value], 1), w1,
        b1.reshape(radial * CHUNK, 128), w2,
    )


def shift(x, axis, by):
    size = lax.axis_size(axis)
    return lax.ppermute(x, axis, [(i, (i + by) % size) for i in range(size)])


def shards(
    features, positions, counts, neighbours, w_query, w_key, w_value, w_radial, b_radial, w_head
):
    blocks = features.shape[2] // ATOM_BLOCK
    row = lax.axis_index("gx")
    rows = lax.axis_size("gx")
    line = counts[:, 0]
    count = line[row]
    own = make_payload(features[0, 0], positions[0, 0], count)
    lines = [shift(own, "gy", 1), own, shift(own, "gy", -1)]
    count_lines = jnp.stack([shift(line, "gy", 1), line, shift(line, "gy", -1)], 0)
    srcs = (
        [shift(x, "gx", 1) for x in lines] + lines + [shift(x, "gx", -1) for x in lines]
    )
    near = jnp.stack([(row - 1) % rows, row, (row + 1) % rows])
    counts9 = count_lines[:, near].T.reshape(9)
    lists = neighbours[0, 0]
    units, wide = make_units(counts9, count, lists)
    out = attend(
        count[None], lists.reshape(-1), units, wide, srcs,
        *make_weights(w_query, w_key, w_value, w_radial, b_radial, w_head),
    )
    return out[None, None]


def solution(mesh):
    in_specs = (
        P("gx", "gy", None, None),
        P("gx", "gy", None, None),
        P(None, "gy"),
        P("gx", "gy", None, None),
        P(), P(), P(), P(), P(), P(),
    )
    out_specs = P("gx", "gy", None, None)
    return jax.shard_map(shards, mesh=mesh, in_specs=in_specs, out_specs=out_specs, check_vma=False)
```

```python
import math

import jax
import jax.numpy as jnp
from jax import lax
from jax.experimental import pallas as pl
from jax.experimental.pallas import tpu as pltpu
from jax.sharding import PartitionSpec as P

HEADS = 8
ATOM_BLOCK = 128
KEY_BLOCKS = 4
CUTOFF = 6.0
SHARPNESS = 4.0
MASKED = -1e30
LENGTH = 576.0
FAR = float(2**20)
POS_ROWS = 16
ROWS = ATOM_BLOCK + POS_ROWS
CHUNK = 8
UNITS = 32


def make_payload(rows, pos, count):
    slots, channels = rows.shape
    blocks = slots // ATOM_BLOCK
    live = jnp.arange(slots, dtype=jnp.int32) < count
    pos = jnp.concatenate([pos[:2], jnp.where(live, pos[2], FAR)[None]], 0)
    hi = lax.reduce_precision(pos, 8, 7)
    rest = pos - hi
    mid = lax.reduce_precision(rest, 8, 7)
    low = rest - mid
    parts = jnp.stack([hi, mid, low], 1).reshape(9, blocks, ATOM_BLOCK).transpose(1, 0, 2)
    parts = jnp.pad(parts.astype(jnp.bfloat16), ((0, 0), (0, POS_ROWS - 9), (0, 0)))
    return jnp.concatenate([rows.reshape(blocks, ATOM_BLOCK, channels), parts], 1)


def make_units(counts9, own_count, lists):
    blocks = lists.shape[0]
    chunks = ATOM_BLOCK // CHUNK
    ck = counts9[lists // blocks].astype(jnp.float32)[:, None, :]
    t0 = (lists % blocks * ATOM_BLOCK)[:, None, :]
    first = (
        jnp.arange(blocks, dtype=jnp.int32)[:, None] * ATOM_BLOCK
        + jnp.arange(chunks, dtype=jnp.int32)[None, :] * CHUNK
    )[:, :, None]
    cq = own_count.astype(jnp.float32)
    reach = ck * (CUTOFF / LENGTH)
    below = first.astype(jnp.float32) * ck / cq - reach - 1.05
    above = (first + CHUNK).astype(jnp.float32) * ck / cq + reach + 0.05
    lo = jnp.floor(below).astype(jnp.int32) + 1 - t0
    hi = jnp.ceil(above).astype(jnp.int32) - 1 - t0
    lo = jnp.maximum(lo, 0)
    hi = jnp.minimum(hi, ATOM_BLOCK - 1)
    hi = jnp.minimum(hi, ck.astype(jnp.int32) - 1 - t0)
    size = jnp.where(first < own_count, jnp.maximum(hi - lo + 1, 0), 0)
    units = (size + 7) // 8
    start = jnp.minimum(lo, ATOM_BLOCK - 8 * units)
    ends = jnp.cumsum(units, axis=2)
    begins = ends - units
    index = jnp.arange(UNITS, dtype=jnp.int32)[None, None, None, :]
    inside = (index >= begins[..., None]) & (index < ends[..., None])
    source = jnp.arange(blocks * KEY_BLOCKS, dtype=jnp.int32).reshape(blocks, 1, KEY_BLOCKS)
    base = source * ATOM_BLOCK + start - 8 * begins
    dummy = blocks * KEY_BLOCKS * ATOM_BLOCK
    rows = jnp.sum(jnp.where(inside, base[..., None] + 8 * index, 0), axis=2)
    rows = jnp.where(index[:, :, 0] < ends[:, :, -1:], rows, dummy)
    pairs = blocks * chunks // 2
    rows = rows.reshape(pairs, 2, UNITS)
    wide = (ends[:, :, -1] > UNITS // 2).reshape(pairs, 2).any(-1)
    together = rows[:, :, : UNITS // 2].reshape(pairs, 1, UNITS)
    items = jnp.where(wide[:, None, None], rows, together)
    items = jnp.concatenate([items.reshape(-1), jnp.full((UNITS,), dummy, jnp.int32)])
    pair = jnp.arange(pairs, dtype=jnp.int32)
    number = jnp.where(wide, 2, 1) * (pair * (2 * CHUNK) < own_count)
    last = jnp.cumsum(number)
    slot = jnp.arange(2 * pairs + 6, dtype=jnp.int32)[:, None] - 3
    here = (slot >= (last - number)[None]) & (slot < last[None])
    which = 2 * pair[None] + slot - (last - number)[None]
    order = jnp.where(here.any(1), jnp.sum(jnp.where(here, which, 0), 1), 2 * pairs)
    info = jnp.stack([last[-1], own_count])
    flags = jnp.concatenate([wide.astype(jnp.int32), jnp.zeros((1,), jnp.int32)])
    return info, items, order, flags


def attend_kernel(info_ref, lists_ref, items_ref, order_ref, flags_ref, *refs):
    srcs = refs[:9]
    wq_ref, wkv_ref, w1_ref, b1_ref, w2_ref, out_ref = refs[9:15]
    xbuf, sems, kvp_s, q_s, qp_s, acc_s, basis_s, active_s, logit_s, coef_s, den_s, v_s = refs[15:]
    blocks = srcs[0].shape[0]
    slots = blocks * ATOM_BLOCK
    dummy = blocks * KEY_BLOCKS * ATOM_BLOCK
    count = info_ref[1]
    live_blocks = (count + ATOM_BLOCK - 1) // ATOM_BLOCK
    bf16 = jnp.bfloat16
    f32 = jnp.float32

    def fetch(q, slot):
        for e in range(KEY_BLOCKS):
            item = lists_ref[q * KEY_BLOCKS + e]
            brick = item // blocks
            block = item % blocks
            for n in range(9):
                @pl.when(brick == n)
                def _():
                    pltpu.make_async_copy(
                        srcs[n].at[block], xbuf.at[slot, e], sems.at[slot, e]
                    ).start()

    def await_block(slot):
        for e in range(KEY_BLOCKS):
            pltpu.make_async_copy(srcs[0].at[0], xbuf.at[slot, e], sems.at[slot, e]).wait()

    lane = lax.broadcasted_iota(jnp.int32, (CHUNK, 128), 1)
    head_of = lane // 16
    key_terms = []
    query_mask = []
    for a in range(3):
        r = lane % 16
        is_key = (lane < 64) & ((r // 3 == a) & (r < 9) | (r == 9 + a) & (a < 2))
        key_terms.append(jnp.where(is_key, -1.0, 0.0).astype(f32))
        query_mask.append((lane >= 64 + 3 * a) & (lane < 67 + 3 * a))
    sub2 = lax.broadcasted_iota(jnp.int32, (2 * CHUNK, 128), 0)
    lane2 = lax.broadcasted_iota(jnp.int32, (2 * CHUNK, 128), 1)
    head_masks = [
        jnp.where(lane2 // 16 == 2 * i + sub2 // CHUNK, 1.0, 0.0).astype(bf16) for i in range(4)
    ]

    kvp_s[0, pl.ds(dummy, 8), :] = jnp.zeros((8, 128), f32)
    kvp_s[1, pl.ds(dummy, 8), :] = jnp.zeros((8, 128), f32)
    kvp_s[2, pl.ds(dummy, 8), :] = jnp.where(
        lane == 6, FAR, jnp.where((lane >= 64) & (lane < 73), 1.0, 0.0)
    ).astype(f32)
    q_s[pl.ds(slots, 8), :] = jnp.zeros((8, 128), f32)
    qp_s[pl.ds(slots, 8), :] = jnp.zeros((8, 128), f32)
    for ref in (basis_s, active_s, logit_s, coef_s, den_s, v_s):
        ref[...] = jnp.zeros_like(ref)

    fetch(0, 0)

    def project(q, carry):
        slot = q % 2
        await_block(slot)

        @pl.when(q + 1 < live_blocks)
        def _():
            fetch(q + 1, 1 - slot)

        mats = []
        sub = lax.broadcasted_iota(jnp.int32, (POS_ROWS, 128), 0)
        for e in range(KEY_BLOCKS):
            brick = lists_ref[q * KEY_BLOCKS + e] // blocks
            shift_x = ((brick // 3 - 1).astype(f32)) * CUTOFF
            shift_y = ((brick % 3 - 1).astype(f32)) * CUTOFF
            m = xbuf[slot, e, ATOM_BLOCK:, :].astype(f32)
            mats.append(jnp.where(sub == 9, shift_x, jnp.where(sub == 10, shift_y, m)))
        mats.append(xbuf[slot, 0, ATOM_BLOCK:, :].astype(f32))
        mats.append(jnp.zeros((48, 128), f32))
        turned = jnp.transpose(jnp.concatenate(mats, 0))
        wide_lane = lax.broadcasted_iota(jnp.int32, (128, 128), 1)
        ones = jnp.where((wide_lane >= 64) & (wide_lane < 73), 1.0, 0.0).astype(f32)
        own = pl.ds(pl.multiple_of(q * ATOM_BLOCK, ATOM_BLOCK), ATOM_BLOCK)
        qp_s[own, :] = turned
        for e in range(KEY_BLOCKS):
            at = pl.ds(
                pl.multiple_of((q * KEY_BLOCKS + e) * ATOM_BLOCK, ATOM_BLOCK), ATOM_BLOCK
            )
            kvp_s[2, at, :] = jnp.where(wide_lane // 16 == e, turned, ones)
            x = xbuf[slot, e, :ATOM_BLOCK, :]
            kv = jnp.dot(x, wkv_ref[...], preferred_element_type=f32)
            kv = kv.astype(bf16).astype(f32)
            kvp_s[0, at, :] = kv[:, :128]
            kvp_s[1, at, :] = kv[:, 128:]
        query = jnp.dot(xbuf[slot, 0, :ATOM_BLOCK, :], wq_ref[...], preferred_element_type=f32)
        q_s[own, :] = query.astype(bf16).astype(f32) * 0.25
        return carry

    lax.fori_loop(0, live_blocks, project, 0)

    contract_last = (((1,), (1,)), ((), ()))
    top_half = w1_ref.shape[0] // 2

    def query_rows(item):
        pair = item // 2
        wide = flags_ref[pair]
        first = jnp.where(wide != 0, item, 2 * pair)
        second = jnp.where(wide != 0, item, 2 * pair + 1)
        first = jnp.minimum(first * CHUNK, slots)
        second = jnp.minimum(second * CHUNK, slots)
        return wide, (pl.multiple_of(first, CHUNK), pl.multiple_of(second, CHUNK))


    def stage_a(item, slot):
        _, starts = query_rows(item)
        scale = math.sqrt(SHARPNESS * math.log2(math.e))
        found = []
        for half in range(2):
            base = item * UNITS + half * (UNITS // 2)
            parts = [[], [], []]
            for j in range(UNITS // 2):
                row = items_ref[base + j]
                for n in range(3):
                    parts[n].append(kvp_s[n, pl.ds(row, 8), :])
            keys, values, places = [jnp.concatenate(x, 0).astype(bf16) for x in parts]
            v_s[pl.ds(pl.multiple_of(lax.rem(slot, 4) * 256 + 128 * half, 128), 128), :] = values
            qp = qp_s[pl.ds(starts[half], CHUNK), :]
            lhs = [jnp.where(query_mask[a], qp, key_terms[a]) for a in range(3)]
            lhs.append(jnp.zeros((8, 128), f32))
            diff = lax.dot_general(
                jnp.concatenate(lhs, 0).astype(bf16), places, contract_last,
                preferred_element_type=f32,
            )
            qc = q_s[pl.ds(starts[half], CHUNK), :]
            qq = jnp.concatenate([qc, qc], 0).astype(bf16)
            q_exp = jnp.concatenate([qq * m for m in head_masks], 0)
            logit = lax.dot_general(q_exp, keys, contract_last, preferred_element_type=f32)
            found.append((diff, logit))
        yield
        for half in range(2):
            at = slice(128 * half, 128 * (half + 1))
            diff, logit = found[half]
            dx, dy, dz = diff[0:8], diff[8:16], diff[16:24]
            r2 = dx * dx + dy * dy + dz * dz
            valid = r2 < CUTOFF * CUTOFF
            inside = 1.0 - r2 * (1.0 / (CUTOFF * CUTOFF))
            env = jnp.where(valid, 2.0 * jnp.log(jnp.where(valid, inside, 1.0)), MASKED)
            r = jnp.sqrt(r2) * scale
            yield
            at_l = pl.multiple_of(lax.rem(slot, 4) * 64, 64)
            for k in range(0, 16, 2):
                two = []
                for kk in (k, k + 1):
                    t = r - (CUTOFF / 15 * kk) * scale
                    two.append(jnp.exp2(-(t * t)))
                basis_s[8 * k : 8 * k + 16, at] = jnp.concatenate(two, 0).astype(bf16)
                h = k // 2
                logit_s[pl.ds(at_l + 8 * h, 8), at] = logit[8 * h : 8 * h + 8] + env
                yield

    def stage_b(hidden, base):
        for t in range(0, hidden.shape[0], 16):
            bias = b1_ref[base + t : base + t + 16, :]
            x = hidden[t : t + 16] + jnp.concatenate([bias, bias], 1)
            active_s[base + t : base + t + 16, :] = (x + x * jnp.tanh(x)).astype(bf16)
            yield

    def stage_c(item, logits, filt):
        wide, _ = query_rows(item)
        dens = [[], []]
        held = [None, None]
        for h in range(HEADS):
            rows = [logits[8 * h : 8 * h + 8, 128 * i : 128 * i + 128] for i in range(2)]
            tops = [jnp.max(row, axis=1, keepdims=True) for row in rows]
            both = jnp.maximum(tops[0], tops[1])
            yield
            for i in range(2):
                top = jnp.where(wide != 0, both, tops[i])
                expo = jnp.exp(rows[i] - top)
                coef = expo * filt[8 * h : 8 * h + 8, 128 * i : 128 * (i + 1)]
                if h % 2:
                    coef_s[8 * h - 8 : 8 * h + 8, 128 * i : 128 * (i + 1)] = jnp.concatenate(
                        [held[i], coef], 0
                    ).astype(bf16)
                held[i] = coef
                dens[i].append(jnp.sum(expo, axis=1, keepdims=True))
            yield
        for i in range(2):
            den = jnp.broadcast_to(dens[i][0], (8, 128))
            for h in range(1, HEADS):
                den = jnp.where(head_of == h, dens[i][h], den)
            den_s[:, 128 * i : 128 * (i + 1)] = den
            yield

    def stage_d(item, nums, dens):
        wide, starts = query_rows(item)
        yield
        yield
        yield
        res = []
        for i in range(2):
            one = nums[i][0:8]
            for h in range(1, HEADS):
                one = jnp.where(head_of == h, nums[i][8 * h : 8 * h + 8], one)
            res.append(one)
            yield
        for i in range(2):
            num = jnp.where(wide != 0, res[0] + res[1], res[i])
            den = jnp.where(wide != 0, dens[0] + dens[1], dens[i])
            acc_s[pl.ds(starts[i], CHUNK), :] = num / jnp.maximum(den, 1.0)
            yield

    def in_turns(*turns):
        turns = list(turns)
        while turns:
            for turn in list(turns):
                if next(turn, turns) is turns:
                    turns.remove(turn)

    def step(i, carry):
        basis = basis_s[...]
        logits = logit_s[pl.ds(pl.multiple_of(lax.rem(i + 1, 4) * 64, 64), 64), :]
        coef = coef_s[...]
        dens = [den_s[:, 128 * n : 128 * (n + 1)] for n in range(2)]
        active = active_s[...]
        at_v = pl.multiple_of(lax.rem(i, 4) * 256, 256)
        values = [v_s[pl.ds(at_v + 128 * n, 128), :] for n in range(2)]
        first = jnp.dot(w1_ref[:top_half], basis, preferred_element_type=f32)
        begin = stage_a(order_ref[i + 3], i + 3)
        next(begin)
        filt = [
            jnp.dot(
                w2_ref[:, top_half * n : top_half * (n + 1)],
                active[top_half * n : top_half * (n + 1)],
                preferred_element_type=f32,
            )
            for n in range(2)
        ]
        filt = filt[0] + filt[1]
        nums = [
            jnp.dot(coef[:, 128 * n : 128 * (n + 1)], values[n], preferred_element_type=f32)
            for n in range(2)
        ]
        in_turns(stage_b(first, 0), stage_d(order_ref[i], nums, dens))
        second = jnp.dot(w1_ref[top_half:], basis, preferred_element_type=f32)
        in_turns(
            begin, stage_c(order_ref[i + 1], logits, filt), stage_b(second, top_half)
        )
        return carry

    lax.fori_loop(0, info_ref[0] + 3, step, 0)

    def finish(q, carry):
        at = pl.ds(pl.multiple_of(q * ATOM_BLOCK, ATOM_BLOCK), ATOM_BLOCK)
        row_id = lax.broadcasted_iota(jnp.int32, (ATOM_BLOCK, 128), 0) + q * ATOM_BLOCK
        out_ref[at, :] = jnp.where(row_id < count, acc_s[at, :], 0.0).astype(bf16)
        return carry

    lax.fori_loop(0, blocks, finish, 0)


def attend(tables, lists, srcs, wq, wkv, w1, b1, w2):
    blocks = srcs[0].shape[0]
    channels = srcs[0].shape[2]
    smem = pl.BlockSpec(memory_space=pltpu.SMEM)
    vmem = pl.BlockSpec(memory_space=pltpu.VMEM)
    hbm = pl.BlockSpec(memory_space=pl.ANY)
    f32 = jnp.float32
    slots = blocks * ATOM_BLOCK
    info, items, order, flags = tables
    return pl.pallas_call(
        attend_kernel,
        out_shape=jax.ShapeDtypeStruct((slots, channels), jnp.bfloat16),
        in_specs=[smem] * 5 + [hbm] * 9 + [vmem] * 5,
        out_specs=vmem,
        scratch_shapes=[
            pltpu.VMEM((2, KEY_BLOCKS, ROWS, channels), jnp.bfloat16),
            pltpu.SemaphoreType.DMA((2, KEY_BLOCKS)),
            pltpu.VMEM((3, slots * KEY_BLOCKS + 8, 128), f32),
            pltpu.VMEM((slots + 8, 128), f32),
            pltpu.VMEM((slots + 8, 128), f32),
            pltpu.VMEM((slots + 8, 128), f32),
            pltpu.VMEM((128, 256), jnp.bfloat16),
            pltpu.VMEM((512, 256), jnp.bfloat16),
            pltpu.VMEM((256, 256), f32),
            pltpu.VMEM((64, 256), jnp.bfloat16),
            pltpu.VMEM((8, 256), f32),
            pltpu.VMEM((1024, 128), jnp.bfloat16),
        ],
        name="attend",
    )(info, lists, items, order, flags, *srcs, wq, wkv, w1, b1, w2)


def make_weights(w_query, w_key, w_value, w_radial, b_radial, w_head):
    basis, radial = w_radial.shape
    eye = jnp.eye(CHUNK, dtype=jnp.bfloat16)
    w1 = (w_radial.T * jnp.bfloat16(0.5))[:, None, :, None] * eye[None, :, None, :]
    w1 = w1.reshape(radial * CHUNK, basis * CHUNK)
    w2 = w_head.T[:, None, :, None] * eye[None, :, None, :]
    w2 = w2.reshape(HEADS * CHUNK, radial * CHUNK)
    b1 = jnp.broadcast_to((0.5 * b_radial)[:, None, None], (radial, CHUNK, 128))
    return (
        w_query, jnp.concatenate([w_key, w_value], 1), w1,
        b1.reshape(radial * CHUNK, 128), w2,
    )


def shift(x, axis, by):
    size = lax.axis_size(axis)
    return lax.ppermute(x, axis, [(i, (i + by) % size) for i in range(size)])


def shards(
    features, positions, counts, neighbours, w_query, w_key, w_value, w_radial, b_radial, w_head
):
    blocks = features.shape[2] // ATOM_BLOCK
    row = lax.axis_index("gx")
    rows = lax.axis_size("gx")
    line = counts[:, 0]
    count = line[row]
    own = make_payload(features[0, 0], positions[0, 0], count)
    lines = [shift(own, "gy", 1), own, shift(own, "gy", -1)]
    count_lines = jnp.stack([shift(line, "gy", 1), line, shift(line, "gy", -1)], 0)
    srcs = (
        [shift(x, "gx", 1) for x in lines] + lines + [shift(x, "gx", -1) for x in lines]
    )
    near = jnp.stack([(row - 1) % rows, row, (row + 1) % rows])
    counts9 = count_lines[:, near].T.reshape(9)
    lists = neighbours[0, 0]
    out = attend(
        make_units(counts9, count, lists), lists.reshape(-1), srcs,
        *make_weights(w_query, w_key, w_value, w_radial, b_radial, w_head),
    )
    return out[None, None]


def solution(mesh):
    in_specs = (
        P("gx", "gy", None, None),
        P("gx", "gy", None, None),
        P(None, "gy"),
        P("gx", "gy", None, None),
        P(), P(), P(), P(), P(), P(),
    )
    out_specs = P("gx", "gy", None, None)
    return jax.shard_map(shards, mesh=mesh, in_specs=in_specs, out_specs=out_specs, check_vma=False)
```

```python
import math

import jax
import jax.numpy as jnp
from jax import lax
from jax.experimental import pallas as pl
from jax.experimental.pallas import tpu as pltpu
from jax.sharding import PartitionSpec as P

HEADS = 8
ATOM_BLOCK = 128
KEY_BLOCKS = 4
CUTOFF = 6.0
SHARPNESS = 4.0
MASKED = -1e30
LENGTH = 576.0
FAR = float(2**20)
POS_ROWS = 16
ROWS = ATOM_BLOCK + POS_ROWS
CHUNK = 8
LIGHT_BLOCKS = 7
UNITS = 32


def make_payload(rows, pos, count, first, last):
    channels = rows.shape[1]
    at = slice(first * ATOM_BLOCK, last * ATOM_BLOCK)
    live = jnp.arange(at.start, at.stop, dtype=jnp.int32) < count
    pos = pos[:, at]
    pos = jnp.concatenate([pos[:2], jnp.where(live, pos[2], FAR)[None]], 0)
    hi = lax.reduce_precision(pos, 8, 7)
    rest = pos - hi
    mid = lax.reduce_precision(rest, 8, 7)
    low = rest - mid
    parts = jnp.stack([hi, mid, low], 1).reshape(9, last - first, ATOM_BLOCK).transpose(1, 0, 2)
    parts = jnp.pad(parts.astype(jnp.bfloat16), ((0, 0), (0, POS_ROWS - 9), (0, 0)))
    return jnp.concatenate([rows[at].reshape(last - first, ATOM_BLOCK, channels), parts], 1)


def make_where(lists):
    blocks = lists.shape[0]
    brick = lists // blocks
    block = lists % blocks
    light = block < LIGHT_BLOCKS
    source = jnp.where(light, brick, 9 + brick % 3)
    place = jnp.where(light, block, block - LIGHT_BLOCKS)
    return jnp.stack([source, place, brick // 3 - 1, brick % 3 - 1], -1).reshape(-1)


def make_units(counts9, own_count, lists):
    blocks = lists.shape[0]
    chunks = ATOM_BLOCK // CHUNK
    ck = counts9[lists // blocks].astype(jnp.float32)[:, None, :]
    t0 = (lists % blocks * ATOM_BLOCK)[:, None, :]
    first = (
        jnp.arange(blocks, dtype=jnp.int32)[:, None] * ATOM_BLOCK
        + jnp.arange(chunks, dtype=jnp.int32)[None, :] * CHUNK
    )[:, :, None]
    cq = own_count.astype(jnp.float32)
    reach = ck * (CUTOFF / LENGTH)
    below = first.astype(jnp.float32) * ck / cq - reach - 1.05
    above = (first + CHUNK).astype(jnp.float32) * ck / cq + reach + 0.05
    lo = jnp.floor(below).astype(jnp.int32) + 1 - t0
    hi = jnp.ceil(above).astype(jnp.int32) - 1 - t0
    lo = jnp.maximum(lo, 0)
    hi = jnp.minimum(hi, ATOM_BLOCK - 1)
    hi = jnp.minimum(hi, ck.astype(jnp.int32) - 1 - t0)
    size = jnp.where(first < own_count, jnp.maximum(hi - lo + 1, 0), 0)
    units = (size + 7) // 8
    start = jnp.minimum(lo, ATOM_BLOCK - 8 * units)
    ends = jnp.cumsum(units, axis=2)
    begins = ends - units
    index = jnp.arange(UNITS, dtype=jnp.int32)[None, None, None, :]
    inside = (index >= begins[..., None]) & (index < ends[..., None])
    source = jnp.arange(blocks * KEY_BLOCKS, dtype=jnp.int32).reshape(blocks, 1, KEY_BLOCKS)
    base = source * ATOM_BLOCK + start - 8 * begins
    dummy = blocks * KEY_BLOCKS * ATOM_BLOCK
    rows = jnp.sum(jnp.where(inside, base[..., None] + 8 * index, 0), axis=2)
    rows = jnp.where(index[:, :, 0] < ends[:, :, -1:], rows, dummy)
    pairs = blocks * chunks // 2
    rows = rows.reshape(pairs, 2, UNITS)
    wide = (ends[:, :, -1] > UNITS // 2).reshape(pairs, 2).any(-1)
    together = rows[:, :, : UNITS // 2].reshape(pairs, 1, UNITS)
    items = jnp.where(wide[:, None, None], rows, together)
    items = jnp.concatenate([items.reshape(-1), jnp.full((UNITS,), dummy, jnp.int32)])
    pair = jnp.arange(pairs, dtype=jnp.int32)
    number = jnp.where(wide, 2, 1) * (pair * (2 * CHUNK) < own_count)
    last = jnp.cumsum(number)
    slot = jnp.arange(2 * pairs + 6, dtype=jnp.int32)[:, None] - 3
    here = (slot >= (last - number)[None]) & (slot < last[None])
    which = 2 * pair[None] + slot - (last - number)[None]
    order = jnp.where(here.any(1), jnp.sum(jnp.where(here, which, 0), 1), 2 * pairs)
    info = jnp.stack([last[-1], own_count])
    flags = jnp.concatenate([wide.astype(jnp.int32), jnp.zeros((1,), jnp.int32)])
    return info, items, order, flags


def attend_kernel(info_ref, where_ref, items_ref, order_ref, flags_ref, *refs):
    srcs = refs[:12]
    wq_ref, wkv_ref, w1_ref, b1_ref, w2_ref, out_ref = refs[12:18]
    xbuf, sems, kvp_s, q_s, qp_s, acc_s, basis_s, active_s, logit_s, coef_s, den_s, v_s = refs[18:]
    blocks = out_ref.shape[0] // ATOM_BLOCK
    slots = blocks * ATOM_BLOCK
    dummy = blocks * KEY_BLOCKS * ATOM_BLOCK
    count = info_ref[1]
    live_blocks = (count + ATOM_BLOCK - 1) // ATOM_BLOCK
    bf16 = jnp.bfloat16
    f32 = jnp.float32

    def fetch(q, carry):
        for e in range(KEY_BLOCKS):
            entry = 4 * (q * KEY_BLOCKS + e)
            source = where_ref[entry]
            block = where_ref[entry + 1]

            def among(low, high):
                if high - low == 1:
                    pltpu.make_async_copy(
                        srcs[low].at[block], xbuf.at[q, e], sems.at[q, e]
                    ).start()
                    return
                middle = (low + high) // 2
                pl.when(source < middle)(lambda: among(low, middle))
                pl.when(source >= middle)(lambda: among(middle, high))

            among(0, 12)
        return carry

    lax.fori_loop(0, live_blocks, fetch, 0)

    lane = lax.broadcasted_iota(jnp.int32, (CHUNK, 128), 1)
    head_of = lane // 16
    key_terms = []
    query_mask = []
    for a in range(3):
        r = lane % 16
        is_key = (lane < 64) & ((r // 3 == a) & (r < 9) | (r == 9 + a) & (a < 2))
        key_terms.append(jnp.where(is_key, -1.0, 0.0).astype(f32))
        query_mask.append((lane >= 64 + 3 * a) & (lane < 67 + 3 * a))
    sub2 = lax.broadcasted_iota(jnp.int32, (2 * CHUNK, 128), 0)
    lane2 = lax.broadcasted_iota(jnp.int32, (2 * CHUNK, 128), 1)
    head_masks = [
        jnp.where(lane2 // 16 == 2 * i + sub2 // CHUNK, 1.0, 0.0).astype(bf16) for i in range(4)
    ]

    kvp_s[0, pl.ds(dummy, 8), :] = jnp.zeros((8, 128), f32)
    kvp_s[1, pl.ds(dummy, 8), :] = jnp.zeros((8, 128), f32)
    kvp_s[2, pl.ds(dummy, 8), :] = jnp.where(
        lane == 6, FAR, jnp.where((lane >= 64) & (lane < 73), 1.0, 0.0)
    ).astype(f32)
    q_s[pl.ds(slots, 8), :] = jnp.zeros((8, 128), f32)
    qp_s[pl.ds(slots, 8), :] = jnp.zeros((8, 128), f32)
    for ref in (basis_s, active_s, logit_s, coef_s, den_s, v_s):
        ref[...] = jnp.zeros_like(ref)

    def project(q, carry):
        for e in range(KEY_BLOCKS):
            pltpu.make_async_copy(srcs[0].at[0], xbuf.at[q, e], sems.at[q, e]).wait()

        mats = []
        sub = lax.broadcasted_iota(jnp.int32, (POS_ROWS, 128), 0)
        for e in range(KEY_BLOCKS):
            entry = 4 * (q * KEY_BLOCKS + e)
            shift_x = where_ref[entry + 2].astype(f32) * CUTOFF
            shift_y = where_ref[entry + 3].astype(f32) * CUTOFF
            m = xbuf[q, e, ATOM_BLOCK:, :].astype(f32)
            mats.append(jnp.where(sub == 9, shift_x, jnp.where(sub == 10, shift_y, m)))
        mats.append(xbuf[q, 0, ATOM_BLOCK:, :].astype(f32))
        mats.append(jnp.zeros((48, 128), f32))
        turned = jnp.transpose(jnp.concatenate(mats, 0))
        wide_lane = lax.broadcasted_iota(jnp.int32, (128, 128), 1)
        ones = jnp.where((wide_lane >= 64) & (wide_lane < 73), 1.0, 0.0).astype(f32)
        own = pl.ds(pl.multiple_of(q * ATOM_BLOCK, ATOM_BLOCK), ATOM_BLOCK)
        qp_s[own, :] = turned
        for e in range(KEY_BLOCKS):
            at = pl.ds(
                pl.multiple_of((q * KEY_BLOCKS + e) * ATOM_BLOCK, ATOM_BLOCK), ATOM_BLOCK
            )
            kvp_s[2, at, :] = jnp.where(wide_lane // 16 == e, turned, ones)
            x = xbuf[q, e, :ATOM_BLOCK, :]
            kv = jnp.dot(x, wkv_ref[...], preferred_element_type=f32)
            kv = kv.astype(bf16).astype(f32)
            kvp_s[0, at, :] = kv[:, :128]
            kvp_s[1, at, :] = kv[:, 128:]
        query = jnp.dot(xbuf[q, 0, :ATOM_BLOCK, :], wq_ref[...], preferred_element_type=f32)
        q_s[own, :] = query.astype(bf16).astype(f32) * 0.25
        return carry

    lax.fori_loop(0, live_blocks, project, 0)

    contract_last = (((1,), (1,)), ((), ()))
    top_half = w1_ref.shape[0] // 2

    def query_rows(item):
        pair = lax.shift_right_logical(item, 1)
        wide = flags_ref[pair]
        first = jnp.where(wide != 0, item, 2 * pair)
        second = jnp.where(wide != 0, item, 2 * pair + 1)
        first = jnp.minimum(first * CHUNK, slots)
        second = jnp.minimum(second * CHUNK, slots)
        return wide, (pl.multiple_of(first, CHUNK), pl.multiple_of(second, CHUNK))


    def stage_a(item, slot):
        _, starts = query_rows(item)
        scale = math.sqrt(SHARPNESS * math.log2(math.e))
        found = []
        for half in range(2):
            base = item * UNITS + half * (UNITS // 2)
            parts = [[], [], []]
            for j in range(UNITS // 2):
                row = items_ref[base + j]
                for n in range(3):
                    parts[n].append(kvp_s[n, pl.ds(row, 8), :])
            keys, values, places = [jnp.concatenate(x, 0).astype(bf16) for x in parts]
            v_s[pl.ds(pl.multiple_of((slot & 3) * 256 + 128 * half, 128), 128), :] = values
            qp = qp_s[pl.ds(starts[half], CHUNK), :]
            lhs = [jnp.where(query_mask[a], qp, key_terms[a]) for a in range(3)]
            lhs.append(jnp.zeros((8, 128), f32))
            diff = lax.dot_general(
                jnp.concatenate(lhs, 0).astype(bf16), places, contract_last,
                preferred_element_type=f32,
            )
            qc = q_s[pl.ds(starts[half], CHUNK), :]
            qq = jnp.concatenate([qc, qc], 0).astype(bf16)
            q_exp = jnp.concatenate([qq * m for m in head_masks], 0)
            logit = lax.dot_general(q_exp, keys, contract_last, preferred_element_type=f32)
            found.append((diff, logit))
        yield
        for half in range(2):
            at = slice(128 * half, 128 * (half + 1))
            diff, logit = found[half]
            dx, dy, dz = diff[0:8], diff[8:16], diff[16:24]
            r2 = dx * dx + dy * dy + dz * dz
            valid = r2 < CUTOFF * CUTOFF
            inside = 1.0 - r2 * (1.0 / (CUTOFF * CUTOFF))
            env = jnp.where(valid, 2.0 * jnp.log(jnp.where(valid, inside, 1.0)), MASKED)
            r = jnp.sqrt(r2) * scale
            yield
            at_l = pl.multiple_of((slot & 3) * 64, 64)
            for k in range(0, 16, 2):
                two = []
                for kk in (k, k + 1):
                    t = r - (CUTOFF / 15 * kk) * scale
                    two.append(jnp.exp2(-(t * t)))
                basis_s[8 * k : 8 * k + 16, at] = jnp.concatenate(two, 0).astype(bf16)
                h = k // 2
                logit_s[pl.ds(at_l + 8 * h, 8), at] = logit[8 * h : 8 * h + 8] + env
                yield

    def stage_b(hidden, base):
        for t in range(0, hidden.shape[0], 16):
            bias = b1_ref[base + t : base + t + 16, :]
            x = hidden[t : t + 16] + jnp.concatenate([bias, bias], 1)
            active_s[base + t : base + t + 16, :] = (x + x * jnp.tanh(x)).astype(bf16)
            yield

    def stage_c(item, logits, filt):
        wide, _ = query_rows(item)
        dens = [[], []]
        held = [None, None]
        for h in range(HEADS):
            rows = [logits[8 * h : 8 * h + 8, 128 * i : 128 * i + 128] for i in range(2)]
            tops = [jnp.max(row, axis=1, keepdims=True) for row in rows]
            both = jnp.maximum(tops[0], tops[1])
            yield
            for i in range(2):
                top = jnp.where(wide != 0, both, tops[i])
                expo = jnp.exp(rows[i] - top)
                coef = expo * filt[8 * h : 8 * h + 8, 128 * i : 128 * (i + 1)]
                if h % 2:
                    coef_s[8 * h - 8 : 8 * h + 8, 128 * i : 128 * (i + 1)] = jnp.concatenate(
                        [held[i], coef], 0
                    ).astype(bf16)
                held[i] = coef
                dens[i].append(jnp.sum(expo, axis=1, keepdims=True))
            yield
        for i in range(2):
            den = jnp.broadcast_to(dens[i][0], (8, 128))
            for h in range(1, HEADS):
                den = jnp.where(head_of == h, dens[i][h], den)
            den_s[:, 128 * i : 128 * (i + 1)] = den
            yield

    def stage_d(item, nums, dens):
        wide, starts = query_rows(item)
        yield
        yield
        yield
        res = []
        for i in range(2):
            one = nums[i][0:8]
            for h in range(1, HEADS):
                one = jnp.where(head_of == h, nums[i][8 * h : 8 * h + 8], one)
            res.append(one)
            yield
        for i in range(2):
            num = jnp.where(wide != 0, res[0] + res[1], res[i])
            den = jnp.where(wide != 0, dens[0] + dens[1], dens[i])
            acc_s[pl.ds(starts[i], CHUNK), :] = num / jnp.maximum(den, 1.0)
            yield

    def in_turns(*turns):
        turns = list(turns)
        while turns:
            for turn in list(turns):
                if next(turn, turns) is turns:
                    turns.remove(turn)

    def step(i, carry):
        basis = basis_s[...]
        logits = logit_s[pl.ds(pl.multiple_of(((i + 1) & 3) * 64, 64), 64), :]
        coef = coef_s[...]
        dens = [den_s[:, 128 * n : 128 * (n + 1)] for n in range(2)]
        active = active_s[...]
        at_v = pl.multiple_of((i & 3) * 256, 256)
        values = [v_s[pl.ds(at_v + 128 * n, 128), :] for n in range(2)]
        first = jnp.dot(w1_ref[:top_half], basis, preferred_element_type=f32)
        begin = stage_a(order_ref[i + 3], i + 3)
        next(begin)
        filt = [
            jnp.dot(
                w2_ref[:, top_half * n : top_half * (n + 1)],
                active[top_half * n : top_half * (n + 1)],
                preferred_element_type=f32,
            )
            for n in range(2)
        ]
        filt = filt[0] + filt[1]
        nums = [
            jnp.dot(coef[:, 128 * n : 128 * (n + 1)], values[n], preferred_element_type=f32)
            for n in range(2)
        ]
        in_turns(stage_b(first, 0), stage_d(order_ref[i], nums, dens))
        second = jnp.dot(w1_ref[top_half:], basis, preferred_element_type=f32)
        in_turns(
            begin, stage_c(order_ref[i + 1], logits, filt), stage_b(second, top_half)
        )
        return carry

    lax.fori_loop(0, info_ref[0] + 3, step, 0)

    def finish(q, carry):
        at = pl.ds(pl.multiple_of(q * ATOM_BLOCK, ATOM_BLOCK), ATOM_BLOCK)
        row_id = lax.broadcasted_iota(jnp.int32, (ATOM_BLOCK, 128), 0) + q * ATOM_BLOCK
        out_ref[at, :] = jnp.where(row_id < count, acc_s[at, :], 0.0).astype(bf16)
        return carry

    lax.fori_loop(0, blocks, finish, 0)


def attend(tables, where, srcs, wq, wkv, w1, b1, w2):
    blocks = where.shape[0] // (4 * KEY_BLOCKS)
    channels = srcs[0].shape[2]
    smem = pl.BlockSpec(memory_space=pltpu.SMEM)
    vmem = pl.BlockSpec(memory_space=pltpu.VMEM)
    hbm = pl.BlockSpec(memory_space=pl.ANY)
    f32 = jnp.float32
    slots = blocks * ATOM_BLOCK
    info, items, order, flags = tables
    return pl.pallas_call(
        attend_kernel,
        out_shape=jax.ShapeDtypeStruct((slots, channels), jnp.bfloat16),
        in_specs=[smem] * 5 + [hbm] * 12 + [vmem] * 5,
        out_specs=vmem,
        scratch_shapes=[
            pltpu.VMEM((blocks, KEY_BLOCKS, ROWS, channels), jnp.bfloat16),
            pltpu.SemaphoreType.DMA((blocks, KEY_BLOCKS)),
            pltpu.VMEM((3, slots * KEY_BLOCKS + 8, 128), f32),
            pltpu.VMEM((slots + 8, 128), f32),
            pltpu.VMEM((slots + 8, 128), f32),
            pltpu.VMEM((slots + 8, 128), f32),
            pltpu.VMEM((128, 256), jnp.bfloat16),
            pltpu.VMEM((512, 256), jnp.bfloat16),
            pltpu.VMEM((256, 256), f32),
            pltpu.VMEM((64, 256), jnp.bfloat16),
            pltpu.VMEM((8, 256), f32),
            pltpu.VMEM((1024, 128), jnp.bfloat16),
        ],
        name="attend",
    )(info, where, items, order, flags, *srcs, wq, wkv, w1, b1, w2)


def make_weights(w_query, w_key, w_value, w_radial, b_radial, w_head):
    basis, radial = w_radial.shape
    eye = jnp.eye(CHUNK, dtype=jnp.bfloat16)
    w1 = (w_radial.T * jnp.bfloat16(0.5))[:, None, :, None] * eye[None, :, None, :]
    w1 = w1.reshape(radial * CHUNK, basis * CHUNK)
    w2 = w_head.T[:, None, :, None] * eye[None, :, None, :]
    w2 = w2.reshape(HEADS * CHUNK, radial * CHUNK)
    b1 = jnp.broadcast_to((0.5 * b_radial)[:, None, None], (radial, CHUNK, 128))
    return (
        w_query, jnp.concatenate([w_key, w_value], 1), w1,
        b1.reshape(radial * CHUNK, 128), w2,
    )


def shift(x, axis, by):
    size = lax.axis_size(axis)
    return lax.ppermute(x, axis, [(i, (i + by) % size) for i in range(size)])


def shards(
    features, positions, counts, neighbours, w_query, w_key, w_value, w_radial, b_radial, w_head
):
    row = lax.axis_index("gx")
    rows = lax.axis_size("gx")
    line = counts[:, 0]
    count = line[row]
    rows_own, pos_own = features[0, 0], positions[0, 0]
    blocks_own = rows_own.shape[0] // ATOM_BLOCK
    light = make_payload(rows_own, pos_own, count, 0, LIGHT_BLOCKS)
    extra = make_payload(rows_own, pos_own, count, LIGHT_BLOCKS, blocks_own)
    count_lines = jnp.stack([shift(line, "gy", 1), line, shift(line, "gy", -1)], 0)
    lines = [shift(light, "gy", 1), light, shift(light, "gy", -1)]
    dense = line > LIGHT_BLOCKS * ATOM_BLOCK
    extra = jnp.where(
        dense[(row - 1) % rows],
        shift(extra, "gx", 1),
        jnp.where(dense[(row + 1) % rows], shift(extra, "gx", -1), extra),
    )
    srcs = (
        [shift(x, "gx", 1) for x in lines] + lines + [shift(x, "gx", -1) for x in lines]
        + [shift(extra, "gy", 1), extra, shift(extra, "gy", -1)]
    )
    near = jnp.stack([(row - 1) % rows, row, (row + 1) % rows])
    counts9 = count_lines[:, near].T.reshape(9)
    lists = neighbours[0, 0]
    out = attend(
        make_units(counts9, count, lists), make_where(lists), srcs,
        *make_weights(w_query, w_key, w_value, w_radial, b_radial, w_head),
    )
    return out[None, None]


def solution(mesh):
    in_specs = (
        P("gx", "gy", None, None),
        P("gx", "gy", None, None),
        P(None, "gy"),
        P("gx", "gy", None, None),
        P(), P(), P(), P(), P(), P(),
    )
    out_specs = P("gx", "gy", None, None)
    return jax.shard_map(shards, mesh=mesh, in_specs=in_specs, out_specs=out_specs, check_vma=False)
```

```python
import math

import jax
import jax.numpy as jnp
from jax import lax
from jax.experimental import pallas as pl
from jax.experimental.pallas import tpu as pltpu
from jax.sharding import PartitionSpec as P

HEADS = 8
ATOM_BLOCK = 128
KEY_BLOCKS = 4
CUTOFF = 6.0
SHARPNESS = 4.0
MASKED = -1e30
LENGTH = 576.0
FAR = float(2**20)
POS_ROWS = 16
ROWS = ATOM_BLOCK + POS_ROWS
CHUNK = 8
LIGHT_BLOCKS = 7
UNITS = 32
SOURCES = 6


def make_payload(rows, pos, count, line, first, last):
    channels = rows.shape[1]
    at = slice(first * ATOM_BLOCK, last * ATOM_BLOCK)
    live = jnp.arange(at.start, at.stop, dtype=jnp.int32) < count
    pos = pos[:, at]
    pos = jnp.concatenate([pos[:2], jnp.where(live, pos[2], FAR)[None]], 0)
    hi = lax.reduce_precision(pos, 8, 7)
    rest = pos - hi
    mid = lax.reduce_precision(rest, 8, 7)
    low = rest - mid
    parts = jnp.stack([hi, mid, low], 1).reshape(9, last - first, ATOM_BLOCK).transpose(1, 0, 2)
    terms = jnp.concatenate([line // 16, line % 16]).astype(jnp.float32)
    terms = jnp.pad(terms, (0, ATOM_BLOCK - terms.shape[0]))
    terms = jnp.broadcast_to(terms, (last - first, 1, ATOM_BLOCK))
    parts = jnp.concatenate([parts, jnp.zeros_like(parts[:, :2]), terms], 1)
    parts = jnp.pad(parts, ((0, 0), (0, POS_ROWS - 12), (0, 0))).astype(jnp.bfloat16)
    return jnp.concatenate([rows[at].reshape(last - first, ATOM_BLOCK, channels), parts], 1)


def make_where(lists):
    blocks = lists.shape[0]
    brick = lists // blocks
    block = lists % blocks
    light = block < LIGHT_BLOCKS
    source = jnp.where(light, brick // 3, 3 + brick % 3)
    place = jnp.where(light, brick % 3 * LIGHT_BLOCKS + block, block - LIGHT_BLOCKS)
    return jnp.stack([source, place, brick // 3 - 1, brick % 3 - 1], -1).reshape(-1)


def make_units(counts9, own_count, lists):
    blocks = lists.shape[0]
    chunks = ATOM_BLOCK // CHUNK
    ck = counts9[lists // blocks].astype(jnp.float32)[:, None, :]
    t0 = (lists % blocks * ATOM_BLOCK)[:, None, :]
    first = (
        jnp.arange(blocks, dtype=jnp.int32)[:, None] * ATOM_BLOCK
        + jnp.arange(chunks, dtype=jnp.int32)[None, :] * CHUNK
    )[:, :, None]
    cq = own_count.astype(jnp.float32)
    reach = ck * (CUTOFF / LENGTH)
    below = first.astype(jnp.float32) * ck / cq - reach - 1.05
    above = (first + CHUNK).astype(jnp.float32) * ck / cq + reach + 0.05
    lo = jnp.floor(below).astype(jnp.int32) + 1 - t0
    hi = jnp.ceil(above).astype(jnp.int32) - 1 - t0
    lo = jnp.maximum(lo, 0)
    hi = jnp.minimum(hi, ATOM_BLOCK - 1)
    hi = jnp.minimum(hi, ck.astype(jnp.int32) - 1 - t0)
    size = jnp.where(first < own_count, jnp.maximum(hi - lo + 1, 0), 0)
    units = (size + 7) // 8
    start = jnp.minimum(lo, ATOM_BLOCK - 8 * units)
    ends = jnp.cumsum(units, axis=2)
    begins = ends - units
    index = jnp.arange(UNITS, dtype=jnp.int32)[None, None, None, :]
    inside = (index >= begins[..., None]) & (index < ends[..., None])
    source = jnp.arange(blocks * KEY_BLOCKS, dtype=jnp.int32).reshape(blocks, 1, KEY_BLOCKS)
    base = source * ATOM_BLOCK + start - 8 * begins
    dummy = blocks * KEY_BLOCKS * ATOM_BLOCK
    rows = jnp.sum(jnp.where(inside, base[..., None] + 8 * index, 0), axis=2)
    rows = jnp.where(index[:, :, 0] < ends[:, :, -1:], rows, dummy)
    pairs = blocks * chunks // 2
    rows = rows.reshape(pairs, 2, UNITS)
    wide = (ends[:, :, -1] > UNITS // 2).reshape(pairs, 2).any(-1)
    together = rows[:, :, : UNITS // 2].reshape(pairs, 1, UNITS)
    items = jnp.where(wide[:, None, None], rows, together)
    items = jnp.concatenate([items.reshape(-1), jnp.full((UNITS,), dummy, jnp.int32)])
    pair = jnp.arange(pairs, dtype=jnp.int32)
    number = jnp.where(wide, 2, 1) * (pair * (2 * CHUNK) < own_count)
    last = jnp.cumsum(number)
    slot = jnp.arange(2 * pairs + 6, dtype=jnp.int32)[:, None] - 3
    here = (slot >= (last - number)[None]) & (slot < last[None])
    which = 2 * pair[None] + slot - (last - number)[None]
    order = jnp.where(here.any(1), jnp.sum(jnp.where(here, which, 0), 1), 2 * pairs)
    info = jnp.stack([last[-1], own_count])
    flags = jnp.concatenate([wide.astype(jnp.int32), jnp.zeros((1,), jnp.int32)])
    return info, items, order, flags


def attend_kernel(info_ref, where_ref, items_ref, order_ref, flags_ref, *refs):
    srcs = refs[:SOURCES]
    wq_ref, wkv_ref, w1_ref, b1_ref, w2_ref, out_ref = refs[SOURCES : SOURCES + 6]
    xbuf, sems, kvp_s, q_s, qp_s, acc_s, basis_s, active_s, logit_s, coef_s, den_s, v_s = refs[SOURCES + 6 :]
    blocks = out_ref.shape[0] // ATOM_BLOCK
    slots = blocks * ATOM_BLOCK
    dummy = blocks * KEY_BLOCKS * ATOM_BLOCK
    count = info_ref[1]
    live_blocks = (count + ATOM_BLOCK - 1) // ATOM_BLOCK
    bf16 = jnp.bfloat16
    f32 = jnp.float32

    def fetch(q, carry):
        for e in range(KEY_BLOCKS):
            entry = 4 * (q * KEY_BLOCKS + e)
            source = where_ref[entry]
            block = where_ref[entry + 1]

            def among(low, high):
                if high - low == 1:
                    pltpu.make_async_copy(
                        srcs[low].at[block], xbuf.at[q, e], sems.at[q, e]
                    ).start()
                    return
                middle = (low + high) // 2
                pl.when(source < middle)(lambda: among(low, middle))
                pl.when(source >= middle)(lambda: among(middle, high))

            among(0, SOURCES)
        return carry

    lax.fori_loop(0, live_blocks, fetch, 0)

    lane = lax.broadcasted_iota(jnp.int32, (CHUNK, 128), 1)
    head_of = lane // 16
    key_terms = []
    query_mask = []
    for a in range(3):
        r = lane % 16
        is_key = (lane < 64) & ((r // 3 == a) & (r < 9) | (r == 9 + a) & (a < 2))
        key_terms.append(jnp.where(is_key, -1.0, 0.0).astype(f32))
        query_mask.append((lane >= 64 + 3 * a) & (lane < 67 + 3 * a))
    sub2 = lax.broadcasted_iota(jnp.int32, (2 * CHUNK, 128), 0)
    lane2 = lax.broadcasted_iota(jnp.int32, (2 * CHUNK, 128), 1)
    head_masks = [
        jnp.where(lane2 // 16 == 2 * i + sub2 // CHUNK, 1.0, 0.0).astype(bf16) for i in range(4)
    ]

    kvp_s[0, pl.ds(dummy, 8), :] = jnp.zeros((8, 128), f32)
    kvp_s[1, pl.ds(dummy, 8), :] = jnp.zeros((8, 128), f32)
    kvp_s[2, pl.ds(dummy, 8), :] = jnp.where(
        lane == 6, FAR, jnp.where((lane >= 64) & (lane < 73), 1.0, 0.0)
    ).astype(f32)
    q_s[pl.ds(slots, 8), :] = jnp.zeros((8, 128), f32)
    qp_s[pl.ds(slots, 8), :] = jnp.zeros((8, 128), f32)
    for ref in (basis_s, active_s, logit_s, coef_s, den_s, v_s):
        ref[...] = jnp.zeros_like(ref)

    def project(q, carry):
        for e in range(KEY_BLOCKS):
            pltpu.make_async_copy(srcs[0].at[0], xbuf.at[q, e], sems.at[q, e]).wait()

        mats = []
        sub = lax.broadcasted_iota(jnp.int32, (POS_ROWS, 128), 0)
        for e in range(KEY_BLOCKS):
            entry = 4 * (q * KEY_BLOCKS + e)
            shift_x = where_ref[entry + 2].astype(f32) * CUTOFF
            shift_y = where_ref[entry + 3].astype(f32) * CUTOFF
            m = xbuf[q, e, ATOM_BLOCK:, :].astype(f32)
            mats.append(jnp.where(sub == 9, shift_x, jnp.where(sub == 10, shift_y, m)))
        mats.append(xbuf[q, 0, ATOM_BLOCK:, :].astype(f32))
        mats.append(jnp.zeros((48, 128), f32))
        turned = jnp.transpose(jnp.concatenate(mats, 0))
        wide_lane = lax.broadcasted_iota(jnp.int32, (128, 128), 1)
        ones = jnp.where((wide_lane >= 64) & (wide_lane < 73), 1.0, 0.0).astype(f32)
        own = pl.ds(pl.multiple_of(q * ATOM_BLOCK, ATOM_BLOCK), ATOM_BLOCK)
        qp_s[own, :] = turned
        for e in range(KEY_BLOCKS):
            at = pl.ds(
                pl.multiple_of((q * KEY_BLOCKS + e) * ATOM_BLOCK, ATOM_BLOCK), ATOM_BLOCK
            )
            kvp_s[2, at, :] = jnp.where(wide_lane // 16 == e, turned, ones)
            x = xbuf[q, e, :ATOM_BLOCK, :]
            kv = jnp.dot(x, wkv_ref[...], preferred_element_type=f32)
            kv = kv.astype(bf16).astype(f32)
            kvp_s[0, at, :] = kv[:, :128]
            kvp_s[1, at, :] = kv[:, 128:]
        query = jnp.dot(xbuf[q, 0, :ATOM_BLOCK, :], wq_ref[...], preferred_element_type=f32)
        q_s[own, :] = query.astype(bf16).astype(f32) * 0.25
        return carry

    lax.fori_loop(0, live_blocks, project, 0)

    contract_last = (((1,), (1,)), ((), ()))
    top_half = w1_ref.shape[0] // 2

    def query_rows(item):
        pair = lax.shift_right_logical(item, 1)
        wide = flags_ref[pair]
        first = jnp.where(wide != 0, item, 2 * pair)
        second = jnp.where(wide != 0, item, 2 * pair + 1)
        first = jnp.minimum(first * CHUNK, slots)
        second = jnp.minimum(second * CHUNK, slots)
        return wide, (pl.multiple_of(first, CHUNK), pl.multiple_of(second, CHUNK))


    def stage_a(item, slot):
        _, starts = query_rows(item)
        scale = math.sqrt(SHARPNESS * math.log2(math.e))
        found = []
        for half in range(2):
            base = item * UNITS + half * (UNITS // 2)
            parts = [[], [], []]
            for j in range(UNITS // 2):
                row = items_ref[base + j]
                for n in range(3):
                    parts[n].append(kvp_s[n, pl.ds(row, 8), :])
            keys, values, places = [jnp.concatenate(x, 0).astype(bf16) for x in parts]
            v_s[pl.ds(pl.multiple_of((slot & 3) * 256 + 128 * half, 128), 128), :] = values
            qp = qp_s[pl.ds(starts[half], CHUNK), :]
            lhs = [jnp.where(query_mask[a], qp, key_terms[a]) for a in range(3)]
            lhs.append(jnp.zeros((8, 128), f32))
            diff = lax.dot_general(
                jnp.concatenate(lhs, 0).astype(bf16), places, contract_last,
                preferred_element_type=f32,
            )
            qc = q_s[pl.ds(starts[half], CHUNK), :]
            qq = jnp.concatenate([qc, qc], 0).astype(bf16)
            q_exp = jnp.concatenate([qq * m for m in head_masks], 0)
            logit = lax.dot_general(q_exp, keys, contract_last, preferred_element_type=f32)
            found.append((diff, logit))
        yield
        for half in range(2):
            at = slice(128 * half, 128 * (half + 1))
            diff, logit = found[half]
            dx, dy, dz = diff[0:8], diff[8:16], diff[16:24]
            r2 = dx * dx + dy * dy + dz * dz
            valid = r2 < CUTOFF * CUTOFF
            inside = 1.0 - r2 * (1.0 / (CUTOFF * CUTOFF))
            env = jnp.where(valid, 2.0 * jnp.log(jnp.where(valid, inside, 1.0)), MASKED)
            r = jnp.sqrt(r2) * scale
            yield
            at_l = pl.multiple_of((slot & 3) * 64, 64)
            for k in range(0, 16, 2):
                two = []
                for kk in (k, k + 1):
                    t = r - (CUTOFF / 15 * kk) * scale
                    two.append(jnp.exp2(-(t * t)))
                basis_s[8 * k : 8 * k + 16, at] = jnp.concatenate(two, 0).astype(bf16)
                h = k // 2
                logit_s[pl.ds(at_l + 8 * h, 8), at] = logit[8 * h : 8 * h + 8] + env
                yield

    def stage_b(hidden, base):
        for t in range(0, hidden.shape[0], 16):
            bias = b1_ref[base + t : base + t + 16, :]
            x = hidden[t : t + 16] + jnp.concatenate([bias, bias], 1)
            active_s[base + t : base + t + 16, :] = (x + x * jnp.tanh(x)).astype(bf16)
            yield

    def stage_c(item, logits, filt):
        wide, _ = query_rows(item)
        dens = [[], []]
        held = [None, None]
        for h in range(HEADS):
            rows = [logits[8 * h : 8 * h + 8, 128 * i : 128 * i + 128] for i in range(2)]
            tops = [jnp.max(row, axis=1, keepdims=True) for row in rows]
            both = jnp.maximum(tops[0], tops[1])
            yield
            for i in range(2):
                top = jnp.where(wide != 0, both, tops[i])
                expo = jnp.exp(rows[i] - top)
                coef = expo * filt[8 * h : 8 * h + 8, 128 * i : 128 * (i + 1)]
                if h % 2:
                    coef_s[8 * h - 8 : 8 * h + 8, 128 * i : 128 * (i + 1)] = jnp.concatenate(
                        [held[i], coef], 0
                    ).astype(bf16)
                held[i] = coef
                dens[i].append(jnp.sum(expo, axis=1, keepdims=True))
            yield
        for i in range(2):
            den = jnp.broadcast_to(dens[i][0], (8, 128))
            for h in range(1, HEADS):
                den = jnp.where(head_of == h, dens[i][h], den)
            den_s[:, 128 * i : 128 * (i + 1)] = den
            yield

    def stage_d(item, nums, dens):
        wide, starts = query_rows(item)
        yield
        yield
        yield
        res = []
        for i in range(2):
            one = nums[i][0:8]
            for h in range(1, HEADS):
                one = jnp.where(head_of == h, nums[i][8 * h : 8 * h + 8], one)
            res.append(one)
            yield
        for i in range(2):
            num = jnp.where(wide != 0, res[0] + res[1], res[i])
            den = jnp.where(wide != 0, dens[0] + dens[1], dens[i])
            acc_s[pl.ds(starts[i], CHUNK), :] = num / jnp.maximum(den, 1.0)
            yield

    def in_turns(*turns):
        turns = list(turns)
        while turns:
            for turn in list(turns):
                if next(turn, turns) is turns:
                    turns.remove(turn)

    def step(i, carry):
        basis = basis_s[...]
        logits = logit_s[pl.ds(pl.multiple_of(((i + 1) & 3) * 64, 64), 64), :]
        coef = coef_s[...]
        dens = [den_s[:, 128 * n : 128 * (n + 1)] for n in range(2)]
        active = active_s[...]
        at_v = pl.multiple_of((i & 3) * 256, 256)
        values = [v_s[pl.ds(at_v + 128 * n, 128), :] for n in range(2)]
        first = jnp.dot(w1_ref[:top_half], basis, preferred_element_type=f32)
        begin = stage_a(order_ref[i + 3], i + 3)
        next(begin)
        filt = [
            jnp.dot(
                w2_ref[:, top_half * n : top_half * (n + 1)],
                active[top_half * n : top_half * (n + 1)],
                preferred_element_type=f32,
            )
            for n in range(2)
        ]
        filt = filt[0] + filt[1]
        nums = [
            jnp.dot(coef[:, 128 * n : 128 * (n + 1)], values[n], preferred_element_type=f32)
            for n in range(2)
        ]
        in_turns(stage_b(first, 0), stage_d(order_ref[i], nums, dens))
        second = jnp.dot(w1_ref[top_half:], basis, preferred_element_type=f32)
        in_turns(
            begin, stage_c(order_ref[i + 1], logits, filt), stage_b(second, top_half)
        )
        return carry

    lax.fori_loop(0, info_ref[0] + 3, step, 0)

    def finish(q, carry):
        at = pl.ds(pl.multiple_of(q * ATOM_BLOCK, ATOM_BLOCK), ATOM_BLOCK)
        row_id = lax.broadcasted_iota(jnp.int32, (ATOM_BLOCK, 128), 0) + q * ATOM_BLOCK
        out_ref[at, :] = jnp.where(row_id < count, acc_s[at, :], 0.0).astype(bf16)
        return carry

    lax.fori_loop(0, blocks, finish, 0)


def attend(tables, where, srcs, wq, wkv, w1, b1, w2):
    blocks = where.shape[0] // (4 * KEY_BLOCKS)
    channels = srcs[0].shape[2]
    smem = pl.BlockSpec(memory_space=pltpu.SMEM)
    vmem = pl.BlockSpec(memory_space=pltpu.VMEM)
    hbm = pl.BlockSpec(memory_space=pl.ANY)
    f32 = jnp.float32
    slots = blocks * ATOM_BLOCK
    info, items, order, flags = tables
    return pl.pallas_call(
        attend_kernel,
        out_shape=jax.ShapeDtypeStruct((slots, channels), jnp.bfloat16),
        in_specs=[smem] * 5 + [hbm] * SOURCES + [vmem] * 5,
        out_specs=vmem,
        scratch_shapes=[
            pltpu.VMEM((blocks, KEY_BLOCKS, ROWS, channels), jnp.bfloat16),
            pltpu.SemaphoreType.DMA((blocks, KEY_BLOCKS)),
            pltpu.VMEM((3, slots * KEY_BLOCKS + 8, 128), f32),
            pltpu.VMEM((slots + 8, 128), f32),
            pltpu.VMEM((slots + 8, 128), f32),
            pltpu.VMEM((slots + 8, 128), f32),
            pltpu.VMEM((128, 256), jnp.bfloat16),
            pltpu.VMEM((512, 256), jnp.bfloat16),
            pltpu.VMEM((256, 256), f32),
            pltpu.VMEM((64, 256), jnp.bfloat16),
            pltpu.VMEM((8, 256), f32),
            pltpu.VMEM((1024, 128), jnp.bfloat16),
        ],
        name="attend",
    )(info, where, items, order, flags, *srcs, wq, wkv, w1, b1, w2)


def make_weights(w_query, w_key, w_value, w_radial, b_radial, w_head):
    basis, radial = w_radial.shape
    eye = jnp.eye(CHUNK, dtype=jnp.bfloat16)
    w1 = (w_radial.T * jnp.bfloat16(0.5))[:, None, :, None] * eye[None, :, None, :]
    w1 = w1.reshape(radial * CHUNK, basis * CHUNK)
    w2 = w_head.T[:, None, :, None] * eye[None, :, None, :]
    w2 = w2.reshape(HEADS * CHUNK, radial * CHUNK)
    b1 = jnp.broadcast_to((0.5 * b_radial)[:, None, None], (radial, CHUNK, 128))
    return (
        w_query, jnp.concatenate([w_key, w_value], 1), w1,
        b1.reshape(radial * CHUNK, 128), w2,
    )


def shift(x, axis, by):
    size = lax.axis_size(axis)
    return lax.ppermute(x, axis, [(i, (i + by) % size) for i in range(size)])


def shards(
    features, positions, counts, neighbours, w_query, w_key, w_value, w_radial, b_radial, w_head
):
    row = lax.axis_index("gx")
    rows = lax.axis_size("gx")
    line = counts[:, 0]
    count = line[row]
    rows_own, pos_own = features[0, 0], positions[0, 0]
    blocks_own = rows_own.shape[0] // ATOM_BLOCK
    light = make_payload(rows_own, pos_own, count, line, 0, LIGHT_BLOCKS)
    extra = make_payload(rows_own, pos_own, count, line, LIGHT_BLOCKS, blocks_own)
    dense = line > LIGHT_BLOCKS * ATOM_BLOCK
    extra = jnp.where(
        dense[(row - 1) % rows],
        shift(extra, "gx", 1),
        jnp.where(dense[(row + 1) % rows], shift(extra, "gx", -1), extra),
    )
    low, high = shift(light, "gy", 1), shift(light, "gy", -1)
    low, high, extra = lax.optimization_barrier((low, high, extra))
    column = jnp.concatenate([low, light, high], 0)
    srcs = [
        shift(column, "gx", 1), column, shift(column, "gx", -1),
        shift(extra, "gy", 1), extra, shift(extra, "gy", -1),
    ]

    def counts_of(x):
        terms = x[0, ATOM_BLOCK + 11, : 2 * rows].astype(jnp.int32)
        return terms[:rows] * 16 + terms[rows:]

    count_lines = jnp.stack([counts_of(low), line, counts_of(high)], 0)
    near = jnp.stack([(row - 1) % rows, row, (row + 1) % rows])
    counts9 = count_lines[:, near].T.reshape(9)
    lists = neighbours[0, 0]
    out = attend(
        make_units(counts9, count, lists), make_where(lists), srcs,
        *make_weights(w_query, w_key, w_value, w_radial, b_radial, w_head),
    )
    return out[None, None]


def solution(mesh):
    in_specs = (
        P("gx", "gy", None, None),
        P("gx", "gy", None, None),
        P(None, "gy"),
        P("gx", "gy", None, None),
        P(), P(), P(), P(), P(), P(),
    )
    out_specs = P("gx", "gy", None, None)
    return jax.shard_map(shards, mesh=mesh, in_specs=in_specs, out_specs=out_specs, check_vma=False)
```

```python
import math

import jax
import jax.numpy as jnp
from jax import lax
from jax.experimental import pallas as pl
from jax.experimental.pallas import tpu as pltpu
from jax.sharding import PartitionSpec as P

HEADS = 8
ATOM_BLOCK = 128
KEY_BLOCKS = 4
CUTOFF = 6.0
SHARPNESS = 4.0
MASKED = -1e30
LENGTH = 576.0
FAR = float(2**20)
POS_ROWS = 16
ROWS = ATOM_BLOCK + POS_ROWS
CHUNK = 8
LIGHT_BLOCKS = 7
UNITS = 32
SOURCES = 6


def payload_kernel(scalars_ref, rows_ref, pos_ref, light_ref, extra_ref):
    f32 = jnp.float32
    bf16 = jnp.bfloat16
    count = scalars_ref[0]
    lane = lax.broadcasted_iota(jnp.int32, (1, ATOM_BLOCK), 1)
    high_count = jnp.broadcast_to((count // 16 * 16).astype(f32), (1, ATOM_BLOCK))
    low_count = jnp.broadcast_to((count % 16).astype(f32), (1, ATOM_BLOCK))
    zeros = jnp.zeros((2, ATOM_BLOCK), f32)
    for q in range(rows_ref.shape[0] // ATOM_BLOCK):
        light = q < LIGHT_BLOCKS
        out = light_ref.at[q] if light else extra_ref.at[q - LIGHT_BLOCKS]
        at = slice(q * ATOM_BLOCK, (q + 1) * ATOM_BLOCK)
        out[:ATOM_BLOCK, :] = rows_ref[at, :]
        pos = pos_ref[:, at]
        pos = jnp.concatenate(
            [pos[:2], jnp.where(lane + q * ATOM_BLOCK < count, pos[2:3], FAR)], 0
        )
        hi = pos.astype(bf16).astype(f32)
        rest = pos - hi
        mid = rest.astype(bf16).astype(f32)
        begin = jnp.full((1, ATOM_BLOCK), float(q * ATOM_BLOCK), f32)
        terms = [hi, mid, rest - mid, zeros, high_count, low_count, begin, zeros]
        out[ATOM_BLOCK:, :] = jnp.concatenate(terms, 0).astype(bf16)


def make_payload(scalars, rows, pos):
    blocks = rows.shape[0] // ATOM_BLOCK
    return pl.pallas_call(
        payload_kernel,
        out_shape=[
            jax.ShapeDtypeStruct((n, ROWS, rows.shape[1]), jnp.bfloat16)
            for n in (LIGHT_BLOCKS, blocks - LIGHT_BLOCKS)
        ],
        in_specs=[pl.BlockSpec(memory_space=pltpu.SMEM)]
        + [pl.BlockSpec(memory_space=pltpu.VMEM)] * 2,
        out_specs=[pl.BlockSpec(memory_space=pltpu.VMEM)] * 2,
        name="payload",
    )(scalars, rows, pos)


def weights_kernel(key_ref, value_ref, radial_ref, bias_ref, head_ref, kv_ref, w1_ref, b1_ref, w2_ref):
    f32 = jnp.float32
    bf16 = jnp.bfloat16

    def split(shape, axis):
        index = lax.broadcasted_iota(jnp.int32, shape, axis)
        return lax.shift_right_logical(index, 3), index & (CHUNK - 1)

    def pick(condition):
        return jnp.where(condition, 1.0, 0.0).astype(bf16)

    def index(shape, axis):
        return lax.broadcasted_iota(jnp.int32, shape, axis)

    basis, radial = radial_ref.shape
    width, tall, heads = basis * CHUNK, radial * CHUNK, HEADS * CHUNK
    kv_ref[:, : key_ref.shape[1]] = key_ref[...]
    kv_ref[:, key_ref.shape[1] :] = value_ref[...]
    first = (((0,), (0,)), ((), ()))
    spread = pick(split((basis, width), 1)[0] == index((basis, width), 0))
    w1 = lax.dot_general(radial_ref[...], spread, first, preferred_element_type=f32)
    rows = pick(split((tall, radial), 0)[0] == index((tall, radial), 1))
    w1 = jnp.dot(rows, w1.astype(bf16), preferred_element_type=f32)
    same = split((tall, width), 0)[1] == split((tall, width), 1)[1]
    w1_ref[...] = jnp.where(same, 0.5 * w1, 0.0).astype(bf16)
    spread = pick(split((radial, tall), 1)[0] == index((radial, tall), 0))
    w2 = lax.dot_general(head_ref[...], spread, first, preferred_element_type=f32)
    rows = pick(split((heads, HEADS), 0)[0] == index((heads, HEADS), 1))
    w2 = jnp.dot(rows, w2.astype(bf16), preferred_element_type=f32)
    same = split((heads, tall), 0)[1] == split((heads, tall), 1)[1]
    w2_ref[...] = jnp.where(same, w2, 0.0).astype(bf16)
    here = split((tall, radial), 0)[0] == index((tall, radial), 1)
    bias = jnp.sum(jnp.where(here, 0.5 * bias_ref[...], 0.0), axis=1, keepdims=True)
    b1_ref[...] = jnp.broadcast_to(bias, b1_ref.shape)


def make_weights(w_key, w_value, w_radial, b_radial, w_head):
    basis, radial = w_radial.shape
    channels = w_key.shape[0]
    bf16 = jnp.bfloat16
    return pl.pallas_call(
        weights_kernel,
        out_shape=[
            jax.ShapeDtypeStruct((channels, 2 * channels), bf16),
            jax.ShapeDtypeStruct((radial * CHUNK, basis * CHUNK), bf16),
            jax.ShapeDtypeStruct((radial * CHUNK, 128), jnp.float32),
            jax.ShapeDtypeStruct((HEADS * CHUNK, radial * CHUNK), bf16),
        ],
        in_specs=[pl.BlockSpec(memory_space=pltpu.VMEM)] * 5,
        out_specs=[pl.BlockSpec(memory_space=pltpu.VMEM)] * 4,
        name="weights",
    )(w_key, w_value, w_radial, b_radial[None], w_head)


def attend_kernel(info_ref, lists_ref, *refs):
    srcs = refs[:SOURCES]
    wq_ref, wkv_ref, w1_ref, b1_ref, w2_ref, out_ref = refs[SOURCES : SOURCES + 6]
    xbuf, sems, kvp_s, q_s, qp_s, acc_s, basis_s, active_s, logit_s, coef_s, den_s, v_s, table_v, table_sem, items_ref, order_ref = refs[SOURCES + 6 :]
    blocks = out_ref.shape[0] // ATOM_BLOCK
    slots = blocks * ATOM_BLOCK
    dummy = blocks * KEY_BLOCKS * ATOM_BLOCK
    count = info_ref[0]
    chunks = ATOM_BLOCK // CHUNK
    none = blocks * chunks
    live_blocks = (count + ATOM_BLOCK - 1) // ATOM_BLOCK
    bf16 = jnp.bfloat16
    f32 = jnp.float32

    def listed(q, e):
        item = lists_ref[q, e]
        brick = lax.shift_right_logical(item, 4)
        part = lax.shift_right_logical(brick * 11, 5)
        return item, item & (blocks - 1), part, brick - 3 * part

    def fetch(q, carry):
        for e in range(KEY_BLOCKS):
            _, block, part, side = listed(q, e)
            light = block < LIGHT_BLOCKS
            source = jnp.where(light, part, 3 + side)
            block = jnp.where(light, side * LIGHT_BLOCKS + block, block - LIGHT_BLOCKS)

            def among(low, high):
                if high - low == 1:
                    pltpu.make_async_copy(
                        srcs[low].at[block], xbuf.at[q, e], sems.at[q, e]
                    ).start()
                    return
                middle = (low + high) // 2
                pl.when(source < middle)(lambda: among(low, middle))
                pl.when(source >= middle)(lambda: among(middle, high))

            among(0, SOURCES)
        return carry

    lax.fori_loop(0, live_blocks, fetch, 0)

    lane = lax.broadcasted_iota(jnp.int32, (CHUNK, 128), 1)
    head_of = lane // 16
    key_terms = []
    query_mask = []
    for a in range(3):
        r = lane % 16
        is_key = (lane < 64) & ((r % 3 == a) & (r < 9) | (r == 9 + a) & (a < 2))
        key_terms.append(jnp.where(is_key, -1.0, 0.0).astype(f32))
        query_mask.append((lane >= 64) & (lane < 73) & ((lane - 64) % 3 == a))
    sub2 = lax.broadcasted_iota(jnp.int32, (2 * CHUNK, 128), 0)
    lane2 = lax.broadcasted_iota(jnp.int32, (2 * CHUNK, 128), 1)
    head_masks = [
        jnp.where(lane2 // 16 == 2 * i + sub2 // CHUNK, 1.0, 0.0).astype(bf16) for i in range(4)
    ]

    kvp_s[0, pl.ds(dummy, 8), :] = jnp.zeros((8, 128), f32)
    kvp_s[1, pl.ds(dummy, 8), :] = jnp.zeros((8, 128), f32)
    kvp_s[2, pl.ds(dummy, 8), :] = jnp.where(
        lane == 2, FAR, jnp.where((lane >= 64) & (lane < 73), 1.0, 0.0)
    ).astype(f32)
    q_s[pl.ds(slots, 8), :] = jnp.zeros((8, 128), f32)
    qp_s[pl.ds(slots, 8), :] = jnp.zeros((8, 128), f32)
    for ref in (basis_s, active_s, logit_s, coef_s, den_s, v_s):
        ref[...] = jnp.zeros_like(ref)

    def project(q, carry):
        for e in range(KEY_BLOCKS):
            pltpu.make_async_copy(srcs[0].at[0], xbuf.at[q, e], sems.at[q, e]).wait()

        unit = lax.broadcasted_iota(jnp.int32, (chunks, 128), 1).astype(f32)
        chunk_id = lax.broadcasted_iota(jnp.int32, (chunks, 128), 0)
        first = (q * ATOM_BLOCK + CHUNK * chunk_id).astype(f32)
        rows = jnp.full((chunks, 128), float(dummy), f32)
        ends = jnp.zeros((chunks, 128), f32)
        mats = []
        sub = lax.broadcasted_iota(jnp.int32, (POS_ROWS, 128), 0)
        for e in range(KEY_BLOCKS):
            _, _, part, side = listed(q, e)
            shift_x = (part - 1).astype(f32) * CUTOFF
            shift_y = (side - 1).astype(f32) * CUTOFF
            m = xbuf[q, e, ATOM_BLOCK:, :].astype(f32)
            key_count = m[11:12] + m[12:13]
            ratio = key_count / count.astype(f32)
            reach = key_count * (CUTOFF / LENGTH)
            begin = m[13:14]
            low = jnp.floor(first * ratio - reach - 1.05) + 1.0 - begin
            high = jnp.ceil((first + CHUNK) * ratio + reach + 0.05) - 1.0 - begin
            low = jnp.maximum(low, 0.0)
            high = jnp.minimum(high, jnp.minimum(key_count - 1.0 - begin, ATOM_BLOCK - 1.0))
            size = jnp.where(first < count.astype(f32), jnp.maximum(high - low + 1.0, 0.0), 0.0)
            units = jnp.floor((size + 7.0) * 0.125)
            low = jnp.minimum(low, ATOM_BLOCK - 8.0 * units)
            base = ((q * KEY_BLOCKS + e) * ATOM_BLOCK).astype(f32)
            rows = jnp.where(
                (unit >= ends) & (unit < ends + units), base + low + 8.0 * (unit - ends), rows
            )
            ends = ends + units
            mats.append(jnp.where(sub == 9, shift_x, jnp.where(sub == 10, shift_y, m)))
        mats.append(xbuf[q, 0, ATOM_BLOCK:, :].astype(f32))
        mats.append(jnp.zeros((48, 128), f32))
        turned = jnp.transpose(jnp.concatenate(mats, 0))
        wide_lane = lax.broadcasted_iota(jnp.int32, (128, 128), 1)
        ones = jnp.where((wide_lane >= 64) & (wide_lane < 73), 1.0, 0.0).astype(f32)
        own = pl.ds(pl.multiple_of(q * ATOM_BLOCK, ATOM_BLOCK), ATOM_BLOCK)
        qp_s[own, :] = turned
        for e in range(KEY_BLOCKS):
            at = pl.ds(
                pl.multiple_of((q * KEY_BLOCKS + e) * ATOM_BLOCK, ATOM_BLOCK), ATOM_BLOCK
            )
            kvp_s[2, at, :] = jnp.where(wide_lane // 16 == e, turned, ones)
            x = xbuf[q, e, :ATOM_BLOCK, :]
            kv = jnp.dot(x, wkv_ref[...], preferred_element_type=f32)
            kv = kv.astype(bf16).astype(f32)
            kvp_s[0, at, :] = kv[:, :128]
            kvp_s[1, at, :] = kv[:, 128:]
        query = jnp.dot(xbuf[q, 0, :ATOM_BLOCK, :], wq_ref[...], preferred_element_type=f32)
        q_s[own, :] = query.astype(bf16).astype(f32) * 0.25
        wide = jnp.where(ends > UNITS // 2, 1.0, 0.0)
        even = chunk_id % 2 == 0
        wide = jnp.maximum(
            wide, jnp.where(even, pltpu.roll(wide, chunks - 1, 0), pltpu.roll(wide, 1, 0))
        )
        following = pltpu.roll(pltpu.roll(rows, chunks - 1, 0), UNITS // 2, 1)
        joined = (wide < 0.5) & (unit >= UNITS // 2)
        rows = jnp.where(joined, following, rows)
        rows = jnp.where(unit == UNITS, wide, rows)
        at = pl.ds(pl.multiple_of(q * chunks, chunks), chunks)
        table_v[at, :] = rows.astype(jnp.int32)
        pltpu.make_async_copy(table_v.at[at], items_ref.at[at], table_sem.at[q]).start()
        return carry

    end = pl.ds(none, 8)
    table_v[end, :] = jnp.where(lane == UNITS, 0, dummy)
    last = pltpu.make_async_copy(table_v.at[end], items_ref.at[end], table_sem.at[blocks])
    last.start()
    lax.fori_loop(0, live_blocks, project, 0)
    last.wait()

    def await_table(q, carry):
        at = pl.ds(pl.multiple_of(q * chunks, chunks), chunks)
        pltpu.make_async_copy(table_v.at[at], items_ref.at[at], table_sem.at[q]).wait()
        return carry

    lax.fori_loop(0, live_blocks, await_table, 0)

    def enlist(p, n):
        order_ref[n] = 2 * p
        order_ref[n + 1] = 2 * p + 1
        return n + 1 + items_ref[2 * p, UNITS]

    for n in range(3):
        order_ref[n] = none
    total = lax.fori_loop(
        0, lax.shift_right_logical(count + 2 * CHUNK - 1, 4), enlist, 3
    )
    for n in range(3):
        order_ref[total + n] = none

    contract_last = (((1,), (1,)), ((), ()))
    top_half = w1_ref.shape[0] // 2

    def query_rows(item):
        pair = lax.shift_right_logical(item, 1)
        wide = items_ref[item, UNITS]
        first = jnp.where(wide != 0, item, 2 * pair)
        second = jnp.where(wide != 0, item, 2 * pair + 1)
        first = jnp.minimum(first * CHUNK, slots)
        second = jnp.minimum(second * CHUNK, slots)
        return wide, (pl.multiple_of(first, CHUNK), pl.multiple_of(second, CHUNK))


    def stage_a(item, slot):
        _, starts = query_rows(item)
        scale = math.sqrt(SHARPNESS * math.log2(math.e))
        found = []
        for half in range(2):
            parts = [[], [], []]
            for j in range(UNITS // 2):
                row = items_ref[item, half * (UNITS // 2) + j]
                for n in range(3):
                    parts[n].append(kvp_s[n, pl.ds(row, 8), :])
            keys, values, places = [jnp.concatenate(x, 0).astype(bf16) for x in parts]
            v_s[pl.ds(pl.multiple_of((slot & 3) * 256 + 128 * half, 128), 128), :] = values
            qp = qp_s[pl.ds(starts[half], CHUNK), :]
            lhs = [jnp.where(query_mask[a], qp, key_terms[a]) for a in range(3)]
            lhs.append(jnp.zeros((8, 128), f32))
            diff = lax.dot_general(
                jnp.concatenate(lhs, 0).astype(bf16), places, contract_last,
                preferred_element_type=f32,
            )
            qc = q_s[pl.ds(starts[half], CHUNK), :]
            qq = jnp.concatenate([qc, qc], 0).astype(bf16)
            q_exp = jnp.concatenate([qq * m for m in head_masks], 0)
            logit = lax.dot_general(q_exp, keys, contract_last, preferred_element_type=f32)
            found.append((diff, logit))
        yield
        for half in range(2):
            at = slice(128 * half, 128 * (half + 1))
            diff, logit = found[half]
            dx, dy, dz = diff[0:8], diff[8:16], diff[16:24]
            r2 = dx * dx + dy * dy + dz * dz
            valid = r2 < CUTOFF * CUTOFF
            inside = 1.0 - r2 * (1.0 / (CUTOFF * CUTOFF))
            env = jnp.where(valid, 2.0 * jnp.log(jnp.where(valid, inside, 1.0)), MASKED)
            r = jnp.sqrt(r2) * scale
            yield
            at_l = pl.multiple_of((slot & 3) * 64, 64)
            for k in range(0, 16, 2):
                two = []
                for kk in (k, k + 1):
                    t = r - (CUTOFF / 15 * kk) * scale
                    two.append(jnp.exp2(-(t * t)))
                basis_s[8 * k : 8 * k + 16, at] = jnp.concatenate(two, 0).astype(bf16)
                h = k // 2
                logit_s[pl.ds(at_l + 8 * h, 8), at] = logit[8 * h : 8 * h + 8] + env
                yield

    def stage_b(hidden, base):
        for t in range(0, hidden.shape[0], 16):
            bias = b1_ref[base + t : base + t + 16, :]
            x = hidden[t : t + 16] + jnp.concatenate([bias, bias], 1)
            active_s[base + t : base + t + 16, :] = (x + x * jnp.tanh(x)).astype(bf16)
            yield

    def stage_c(item, logits, filt):
        wide, _ = query_rows(item)
        dens = [[], []]
        held = [None, None]
        for h in range(HEADS):
            rows = [logits[8 * h : 8 * h + 8, 128 * i : 128 * i + 128] for i in range(2)]
            tops = [jnp.max(row, axis=1, keepdims=True) for row in rows]
            both = jnp.maximum(tops[0], tops[1])
            yield
            for i in range(2):
                top = jnp.where(wide != 0, both, tops[i])
                expo = jnp.exp(rows[i] - top)
                coef = expo * filt[8 * h : 8 * h + 8, 128 * i : 128 * (i + 1)]
                if h % 2:
                    coef_s[8 * h - 8 : 8 * h + 8, 128 * i : 128 * (i + 1)] = jnp.concatenate(
                        [held[i], coef], 0
                    ).astype(bf16)
                held[i] = coef
                dens[i].append(jnp.sum(expo, axis=1, keepdims=True))
            yield
        for i in range(2):
            den = jnp.broadcast_to(dens[i][0], (8, 128))
            for h in range(1, HEADS):
                den = jnp.where(head_of == h, dens[i][h], den)
            den_s[:, 128 * i : 128 * (i + 1)] = den
            yield

    def stage_d(item, nums, dens):
        wide, starts = query_rows(item)
        yield
        yield
        yield
        res = []
        for i in range(2):
            one = nums[i][0:8]
            for h in range(1, HEADS):
                one = jnp.where(head_of == h, nums[i][8 * h : 8 * h + 8], one)
            res.append(one)
            yield
        for i in range(2):
            num = jnp.where(wide != 0, res[0] + res[1], res[i])
            den = jnp.where(wide != 0, dens[0] + dens[1], dens[i])
            acc_s[pl.ds(starts[i], CHUNK), :] = num / jnp.maximum(den, 1.0)
            yield

    def in_turns(*turns):
        turns = list(turns)
        while turns:
            for turn in list(turns):
                if next(turn, turns) is turns:
                    turns.remove(turn)

    def step(i, carry):
        basis = basis_s[...]
        logits = logit_s[pl.ds(pl.multiple_of(((i + 1) & 3) * 64, 64), 64), :]
        coef = coef_s[...]
        dens = [den_s[:, 128 * n : 128 * (n + 1)] for n in range(2)]
        active = active_s[...]
        at_v = pl.multiple_of((i & 3) * 256, 256)
        values = [v_s[pl.ds(at_v + 128 * n, 128), :] for n in range(2)]
        first = jnp.dot(w1_ref[:top_half], basis, preferred_element_type=f32)
        begin = stage_a(order_ref[i + 3], i + 3)
        next(begin)
        filt = [
            jnp.dot(
                w2_ref[:, top_half * n : top_half * (n + 1)],
                active[top_half * n : top_half * (n + 1)],
                preferred_element_type=f32,
            )
            for n in range(2)
        ]
        filt = filt[0] + filt[1]
        nums = [
            jnp.dot(coef[:, 128 * n : 128 * (n + 1)], values[n], preferred_element_type=f32)
            for n in range(2)
        ]
        in_turns(stage_b(first, 0), stage_d(order_ref[i], nums, dens))
        second = jnp.dot(w1_ref[top_half:], basis, preferred_element_type=f32)
        in_turns(
            begin, stage_c(order_ref[i + 1], logits, filt), stage_b(second, top_half)
        )
        return carry

    lax.fori_loop(0, total, step, 0)

    def finish(q, carry):
        at = pl.ds(pl.multiple_of(q * ATOM_BLOCK, ATOM_BLOCK), ATOM_BLOCK)
        row_id = lax.broadcasted_iota(jnp.int32, (ATOM_BLOCK, 128), 0) + q * ATOM_BLOCK
        out_ref[at, :] = jnp.where(row_id < count, acc_s[at, :], 0.0).astype(bf16)
        return carry

    lax.fori_loop(0, blocks, finish, 0)


def attend(scalars, lists, srcs, wq, wkv, w1, b1, w2):
    blocks = lists.shape[0]
    channels = srcs[0].shape[2]
    smem = pl.BlockSpec(memory_space=pltpu.SMEM)
    vmem = pl.BlockSpec(memory_space=pltpu.VMEM)
    hbm = pl.BlockSpec(memory_space=pl.ANY)
    f32 = jnp.float32
    slots = blocks * ATOM_BLOCK
    table = (slots // CHUNK + 8, 128)
    return pl.pallas_call(
        attend_kernel,
        out_shape=jax.ShapeDtypeStruct((slots, channels), jnp.bfloat16),
        in_specs=[smem] * 2 + [hbm] * SOURCES + [vmem] * 5,
        out_specs=vmem,
        scratch_shapes=[
            pltpu.VMEM((blocks, KEY_BLOCKS, ROWS, channels), jnp.bfloat16),
            pltpu.SemaphoreType.DMA((blocks, KEY_BLOCKS)),
            pltpu.VMEM((3, slots * KEY_BLOCKS + 8, 128), f32),
            pltpu.VMEM((slots + 8, 128), f32),
            pltpu.VMEM((slots + 8, 128), f32),
            pltpu.VMEM((slots + 8, 128), f32),
            pltpu.VMEM((128, 256), jnp.bfloat16),
            pltpu.VMEM((512, 256), jnp.bfloat16),
            pltpu.VMEM((256, 256), f32),
            pltpu.VMEM((64, 256), jnp.bfloat16),
            pltpu.VMEM((8, 256), f32),
            pltpu.VMEM((1024, 128), jnp.bfloat16),
            pltpu.VMEM(table, jnp.int32),
            pltpu.SemaphoreType.DMA((blocks + 1,)),
            pltpu.SMEM(table, jnp.int32),
            pltpu.SMEM((slots // CHUNK + 8,), jnp.int32),
        ],
        name="attend",
    )(scalars, lists, *srcs, wq, wkv, w1, b1, w2)


def shift(x, axis, by):
    size = lax.axis_size(axis)
    return lax.ppermute(x, axis, [(i, (i + by) % size) for i in range(size)])


def shards(
    features, positions, counts, neighbours, w_query, w_key, w_value, w_radial, b_radial, w_head
):
    row = lax.axis_index("gx")
    rows = lax.axis_size("gx")
    line = counts[:, 0]
    scalars = line[row][None]
    light, extra = make_payload(scalars, features[0, 0], positions[0, 0])
    dense = line > LIGHT_BLOCKS * ATOM_BLOCK
    extra = jnp.where(
        dense[(row - 1) % rows],
        shift(extra, "gx", 1),
        jnp.where(dense[(row + 1) % rows], shift(extra, "gx", -1), extra),
    )
    low, high = shift(light, "gy", 1), shift(light, "gy", -1)
    low, high, extra = lax.optimization_barrier((low, high, extra))
    column = jnp.concatenate([low, light, high], 0)
    srcs = [
        shift(column, "gx", 1), column, shift(column, "gx", -1),
        shift(extra, "gy", 1), extra, shift(extra, "gy", -1),
    ]
    wkv, w1, b1, w2 = make_weights(w_key, w_value, w_radial, b_radial, w_head)
    out = attend(scalars, neighbours[0, 0], srcs, w_query, wkv, w1, b1, w2)
    return out[None, None]


def solution(mesh):
    in_specs = (
        P("gx", "gy", None, None),
        P("gx", "gy", None, None),
        P(None, "gy"),
        P("gx", "gy", None, None),
        P(), P(), P(), P(), P(), P(),
    )
    out_specs = P("gx", "gy", None, None)
    return jax.shard_map(shards, mesh=mesh, in_specs=in_specs, out_specs=out_specs, check_vma=False)
```

```python
import math

import jax
import jax.numpy as jnp
from jax import lax
from jax.experimental import pallas as pl
from jax.experimental.pallas import tpu as pltpu
from jax.sharding import PartitionSpec as P

HEADS = 8
ATOM_BLOCK = 128
KEY_BLOCKS = 4
CUTOFF = 6.0
SHARPNESS = 4.0
MASKED = -1e30
LENGTH = 576.0
FAR = float(2**20)
POS_ROWS = 16
ROWS = ATOM_BLOCK + POS_ROWS
CHUNK = 8
LIGHT_BLOCKS = 7
UNITS = 32
SOURCES = 6


def payload_kernel(scalars_ref, rows_ref, pos_ref, light_ref, extra_ref):
    f32 = jnp.float32
    bf16 = jnp.bfloat16
    count = scalars_ref[0]
    lane = lax.broadcasted_iota(jnp.int32, (1, ATOM_BLOCK), 1)
    high_count = jnp.broadcast_to((count // 16 * 16).astype(f32), (1, ATOM_BLOCK))
    low_count = jnp.broadcast_to((count % 16).astype(f32), (1, ATOM_BLOCK))
    zeros = jnp.zeros((2, ATOM_BLOCK), f32)
    for q in range(rows_ref.shape[0] // ATOM_BLOCK):
        light = q < LIGHT_BLOCKS
        out = light_ref.at[q] if light else extra_ref.at[q - LIGHT_BLOCKS]
        at = slice(q * ATOM_BLOCK, (q + 1) * ATOM_BLOCK)
        out[:ATOM_BLOCK, :] = rows_ref[at, :]
        pos = pos_ref[:, at]
        pos = jnp.concatenate(
            [pos[:2], jnp.where(lane + q * ATOM_BLOCK < count, pos[2:3], FAR)], 0
        )
        hi = pos.astype(bf16).astype(f32)
        rest = pos - hi
        mid = rest.astype(bf16).astype(f32)
        begin = jnp.full((1, ATOM_BLOCK), float(q * ATOM_BLOCK), f32)
        terms = [hi, mid, rest - mid, zeros, high_count, low_count, begin, zeros]
        out[ATOM_BLOCK:, :] = jnp.concatenate(terms, 0).astype(bf16)


def make_payload(scalars, rows, pos):
    blocks = rows.shape[0] // ATOM_BLOCK
    return pl.pallas_call(
        payload_kernel,
        out_shape=[
            jax.ShapeDtypeStruct((n, ROWS, rows.shape[1]), jnp.bfloat16)
            for n in (LIGHT_BLOCKS, blocks - LIGHT_BLOCKS)
        ],
        in_specs=[pl.BlockSpec(memory_space=pltpu.SMEM)]
        + [pl.BlockSpec(memory_space=pltpu.VMEM)] * 2,
        out_specs=[pl.BlockSpec(memory_space=pltpu.VMEM)] * 2,
        name="payload",
    )(scalars, rows, pos)


def weights_kernel(key_ref, value_ref, radial_ref, bias_ref, head_ref, kv_ref, w1_ref, b1_ref, w2_ref):
    f32 = jnp.float32
    bf16 = jnp.bfloat16

    def split(shape, axis):
        index = lax.broadcasted_iota(jnp.int32, shape, axis)
        return lax.shift_right_logical(index, 3), index & (CHUNK - 1)

    def pick(condition):
        return jnp.where(condition, 1.0, 0.0).astype(bf16)

    def index(shape, axis):
        return lax.broadcasted_iota(jnp.int32, shape, axis)

    basis, radial = radial_ref.shape
    width, tall, heads = basis * CHUNK, radial * CHUNK, HEADS * CHUNK
    kv_ref[:, : key_ref.shape[1]] = key_ref[...]
    kv_ref[:, key_ref.shape[1] :] = value_ref[...]
    first = (((0,), (0,)), ((), ()))
    spread = pick(split((basis, width), 1)[0] == index((basis, width), 0))
    w1 = lax.dot_general(radial_ref[...], spread, first, preferred_element_type=f32)
    rows = pick(split((tall, radial), 0)[0] == index((tall, radial), 1))
    w1 = jnp.dot(rows, w1.astype(bf16), preferred_element_type=f32)
    same = split((tall, width), 0)[1] == split((tall, width), 1)[1]
    w1_ref[...] = jnp.where(same, 0.5 * w1, 0.0).astype(bf16)
    spread = pick(split((radial, tall), 1)[0] == index((radial, tall), 0))
    w2 = lax.dot_general(head_ref[...], spread, first, preferred_element_type=f32)
    rows = pick(split((heads, HEADS), 0)[0] == index((heads, HEADS), 1))
    w2 = jnp.dot(rows, w2.astype(bf16), preferred_element_type=f32)
    same = split((heads, tall), 0)[1] == split((heads, tall), 1)[1]
    w2_ref[...] = jnp.where(same, w2, 0.0).astype(bf16)
    here = split((tall, radial), 0)[0] == index((tall, radial), 1)
    bias = jnp.sum(jnp.where(here, 0.5 * bias_ref[...], 0.0), axis=1, keepdims=True)
    b1_ref[...] = jnp.broadcast_to(bias, b1_ref.shape)


def make_weights(w_key, w_value, w_radial, b_radial, w_head):
    basis, radial = w_radial.shape
    channels = w_key.shape[0]
    bf16 = jnp.bfloat16
    return pl.pallas_call(
        weights_kernel,
        out_shape=[
            jax.ShapeDtypeStruct((channels, 2 * channels), bf16),
            jax.ShapeDtypeStruct((radial * CHUNK, basis * CHUNK), bf16),
            jax.ShapeDtypeStruct((radial * CHUNK, 128), jnp.float32),
            jax.ShapeDtypeStruct((HEADS * CHUNK, radial * CHUNK), bf16),
        ],
        in_specs=[pl.BlockSpec(memory_space=pltpu.VMEM)] * 5,
        out_specs=[pl.BlockSpec(memory_space=pltpu.VMEM)] * 4,
        name="weights",
    )(w_key, w_value, w_radial, b_radial[None], w_head)


def attend_kernel(info_ref, lists_ref, *refs):
    srcs = refs[:SOURCES]
    wq_ref, wkv_ref, w1_ref, b1_ref, w2_ref, out_ref = refs[SOURCES : SOURCES + 6]
    xbuf, sems, kvp_s, q_s, qp_s, acc_s, basis_s, active_s, logit_s, coef_s, den_s, v_s, r2_s, env_s, table_v, table_sem, items_ref, order_ref = refs[SOURCES + 6 :]
    blocks = out_ref.shape[0] // ATOM_BLOCK
    slots = blocks * ATOM_BLOCK
    dummy = blocks * KEY_BLOCKS * ATOM_BLOCK
    count = info_ref[0]
    chunks = ATOM_BLOCK // CHUNK
    none = blocks * chunks
    live_blocks = (count + ATOM_BLOCK - 1) // ATOM_BLOCK
    bf16 = jnp.bfloat16
    f32 = jnp.float32

    def listed(q, e):
        item = lists_ref[q, e]
        brick = lax.shift_right_logical(item, 4)
        part = lax.shift_right_logical(brick * 11, 5)
        return item, item & (blocks - 1), part, brick - 3 * part

    def fetch(q, carry):
        for e in range(KEY_BLOCKS):
            _, block, part, side = listed(q, e)
            light = block < LIGHT_BLOCKS
            source = jnp.where(light, part, 3 + side)
            block = jnp.where(light, side * LIGHT_BLOCKS + block, block - LIGHT_BLOCKS)

            def among(low, high):
                if high - low == 1:
                    pltpu.make_async_copy(
                        srcs[low].at[block], xbuf.at[q, e], sems.at[q, e]
                    ).start()
                    return
                middle = (low + high) // 2
                pl.when(source < middle)(lambda: among(low, middle))
                pl.when(source >= middle)(lambda: among(middle, high))

            among(0, SOURCES)
        return carry

    lax.fori_loop(0, live_blocks, fetch, 0)

    lane = lax.broadcasted_iota(jnp.int32, (CHUNK, 128), 1)
    head_of = lane // 16
    sub2 = lax.broadcasted_iota(jnp.int32, (2 * CHUNK, 128), 0)
    lane2 = lax.broadcasted_iota(jnp.int32, (2 * CHUNK, 128), 1)
    head_masks = [
        jnp.where(lane2 // 16 == 2 * i + sub2 // CHUNK, 1.0, 0.0).astype(bf16) for i in range(4)
    ]

    kvp_s[0, pl.ds(dummy, 8), :] = jnp.zeros((8, 128), f32)
    kvp_s[1, pl.ds(dummy, 8), :] = jnp.zeros((8, 128), f32)
    kvp_s[2, pl.ds(dummy, 8), :] = jnp.where(
        lane % 64 == 2, FAR, 0.0
    ).astype(f32)
    q_s[pl.ds(slots, 8), :] = jnp.zeros((8, 128), f32)
    qp_s[pl.ds(slots, 8), :] = jnp.zeros((8, 128), f32)
    for ref in (basis_s, active_s, logit_s, coef_s, den_s, v_s, r2_s, env_s):
        ref[...] = jnp.zeros_like(ref)

    def project(q, carry):
        for e in range(KEY_BLOCKS):
            pltpu.make_async_copy(srcs[0].at[0], xbuf.at[q, e], sems.at[q, e]).wait()

        unit = lax.broadcasted_iota(jnp.int32, (chunks, 128), 1).astype(f32)
        chunk_id = lax.broadcasted_iota(jnp.int32, (chunks, 128), 0)
        first = (q * ATOM_BLOCK + CHUNK * chunk_id).astype(f32)
        rows = jnp.full((chunks, 128), float(dummy), f32)
        ends = jnp.zeros((chunks, 128), f32)
        mats = []
        for e in range(KEY_BLOCKS):
            _, _, part, side = listed(q, e)
            shift_x = (part - 1).astype(f32) * CUTOFF
            shift_y = (side - 1).astype(f32) * CUTOFF
            m = xbuf[q, e, ATOM_BLOCK:, :].astype(f32)
            key_count = m[11:12] + m[12:13]
            ratio = key_count / count.astype(f32)
            reach = key_count * (CUTOFF / LENGTH)
            begin = m[13:14]
            low = jnp.floor(first * ratio - reach - 1.05) + 1.0 - begin
            high = jnp.ceil((first + CHUNK) * ratio + reach + 0.05) - 1.0 - begin
            low = jnp.maximum(low, 0.0)
            high = jnp.minimum(high, jnp.minimum(key_count - 1.0 - begin, ATOM_BLOCK - 1.0))
            size = jnp.where(first < count.astype(f32), jnp.maximum(high - low + 1.0, 0.0), 0.0)
            units = jnp.floor((size + 7.0) * 0.125)
            low = jnp.minimum(low, ATOM_BLOCK - 8.0 * units)
            base = ((q * KEY_BLOCKS + e) * ATOM_BLOCK).astype(f32)
            rows = jnp.where(
                (unit >= ends) & (unit < ends + units), base + low + 8.0 * (unit - ends), rows
            )
            ends = ends + units
            place = (m[0:3] + m[3:6]) + m[6:9]
            axis = lax.broadcasted_iota(jnp.int32, (3, 128), 0)
            place = place + jnp.where(axis == 0, shift_x, jnp.where(axis == 1, shift_y, 0.0))
            mats.append(jnp.concatenate([place, jnp.zeros((13, 128), f32)], 0))
        turned = jnp.transpose(jnp.concatenate(mats + mats, 0))
        own = pl.ds(pl.multiple_of(q * ATOM_BLOCK, ATOM_BLOCK), ATOM_BLOCK)
        qp_s[own, :] = turned
        for e in range(KEY_BLOCKS):
            at = pl.ds(
                pl.multiple_of((q * KEY_BLOCKS + e) * ATOM_BLOCK, ATOM_BLOCK), ATOM_BLOCK
            )
            kvp_s[2, at, :] = pltpu.roll(turned, 128 - 16 * e, 1) if e else turned
            x = xbuf[q, e, :ATOM_BLOCK, :]
            kv = jnp.dot(x, wkv_ref[...], preferred_element_type=f32)
            kv = kv.astype(bf16).astype(f32)
            kvp_s[0, at, :] = kv[:, :128]
            kvp_s[1, at, :] = kv[:, 128:]
        query = jnp.dot(xbuf[q, 0, :ATOM_BLOCK, :], wq_ref[...], preferred_element_type=f32)
        q_s[own, :] = query.astype(bf16).astype(f32) * 0.25
        wide = jnp.where(ends > UNITS // 2, 1.0, 0.0)
        even = chunk_id % 2 == 0
        wide = jnp.maximum(
            wide, jnp.where(even, pltpu.roll(wide, chunks - 1, 0), pltpu.roll(wide, 1, 0))
        )
        following = pltpu.roll(pltpu.roll(rows, chunks - 1, 0), UNITS // 2, 1)
        joined = (wide < 0.5) & (unit >= UNITS // 2)
        rows = jnp.where(joined, following, rows)
        rows = jnp.where(unit == UNITS, wide, rows)
        at = pl.ds(pl.multiple_of(q * chunks, chunks), chunks)
        table_v[at, :] = rows.astype(jnp.int32)
        pltpu.make_async_copy(table_v.at[at], items_ref.at[at], table_sem.at[q]).start()
        return carry

    end = pl.ds(none, 8)
    table_v[end, :] = jnp.where(lane == UNITS, 0, dummy)
    last = pltpu.make_async_copy(table_v.at[end], items_ref.at[end], table_sem.at[blocks])
    last.start()
    lax.fori_loop(0, live_blocks, project, 0)
    last.wait()

    def await_table(q, carry):
        at = pl.ds(pl.multiple_of(q * chunks, chunks), chunks)
        pltpu.make_async_copy(table_v.at[at], items_ref.at[at], table_sem.at[q]).wait()
        return carry

    lax.fori_loop(0, live_blocks, await_table, 0)

    def enlist(p, n):
        order_ref[n] = 2 * p
        order_ref[n + 1] = 2 * p + 1
        return n + 1 + items_ref[2 * p, UNITS]

    for n in range(4):
        order_ref[n] = none
    total = lax.fori_loop(
        0, lax.shift_right_logical(count + 2 * CHUNK - 1, 4), enlist, 4
    )
    for n in range(4):
        order_ref[total + n] = none

    contract_last = (((1,), (1,)), ((), ()))
    top_half = w1_ref.shape[0] // 2

    def query_rows(item):
        pair = lax.shift_right_logical(item, 1)
        wide = items_ref[item, UNITS]
        first = jnp.where(wide != 0, item, 2 * pair)
        second = jnp.where(wide != 0, item, 2 * pair + 1)
        first = jnp.minimum(first * CHUNK, slots)
        second = jnp.minimum(second * CHUNK, slots)
        return wide, (pl.multiple_of(first, CHUNK), pl.multiple_of(second, CHUNK))


    def stage_a(item, slot):
        _, starts = query_rows(item)
        places = []
        for half in range(2):
            at = slice(128 * half, 128 * (half + 1))
            parts = [[], [], []]
            for j in range(UNITS // 2):
                row = items_ref[item, half * (UNITS // 2) + j]
                for n in range(3):
                    parts[n].append(kvp_s[n, pl.ds(row, 8), :])
            places.append(parts[2])
            keys = jnp.concatenate(parts[0], 0).astype(bf16)
            v_s[pl.ds(pl.multiple_of((slot & 7) * 256 + 128 * half, 128), 128), :] = (
                jnp.concatenate(parts[1], 0).astype(bf16)
            )
            qc = q_s[pl.ds(starts[half], CHUNK), :]
            qq = jnp.concatenate([qc, qc], 0).astype(bf16)
            q_exp = jnp.concatenate([qq * m for m in head_masks], 0)
            logit_s[pl.ds(pl.multiple_of((slot & 3) * 64, 64), 64), at] = lax.dot_general(
                q_exp, keys, contract_last, preferred_element_type=f32
            )
            yield
        turned = jnp.transpose(
            jnp.concatenate([jnp.where(lane < 64, x, y) for x, y in zip(*places)], 0)
        )
        yield
        for half in range(2):
            at = slice(128 * half, 128 * (half + 1))
            qp = qp_s[pl.ds(starts[half], CHUNK), :]
            r2 = 0.0
            for a in range(3):
                diff = qp[:, a : a + 1] - turned[64 * half + a : 64 * half + a + 1, :]
                r2 = r2 + diff * diff
            r2_s[:, at] = r2
            yield

    def stage_g(r2_both, slot):
        scale = math.sqrt(SHARPNESS * math.log2(math.e))
        for half in range(2):
            at = slice(128 * half, 128 * (half + 1))
            r2 = r2_both[:, at]
            valid = r2 < CUTOFF * CUTOFF
            inside = 1.0 - r2 * (1.0 / (CUTOFF * CUTOFF))
            env_s[pl.ds(pl.multiple_of((slot & 3) * 8, 8), 8), at] = jnp.where(
                valid, 2.0 * jnp.log(jnp.where(valid, inside, 1.0)), MASKED
            )
            r = jnp.sqrt(r2) * scale
            yield
            for k in range(0, 16, 2):
                two = []
                for kk in (k, k + 1):
                    t = r - (CUTOFF / 15 * kk) * scale
                    two.append(jnp.exp2(-(t * t)))
                basis_s[8 * k : 8 * k + 16, at] = jnp.concatenate(two, 0).astype(bf16)
                yield

    def stage_b(hidden, base):
        for t in range(0, hidden.shape[0], 16):
            bias = b1_ref[base + t : base + t + 16, :]
            x = hidden[t : t + 16] + jnp.concatenate([bias, bias], 1)
            active_s[base + t : base + t + 16, :] = (x + x * jnp.tanh(x)).astype(bf16)
            yield

    def stage_c(item, logits, env, expos):
        wide, _ = query_rows(item)
        dens = [[], []]
        for h in range(HEADS):
            rows = [
                logits[8 * h : 8 * h + 8, 128 * i : 128 * i + 128] + env[:, 128 * i : 128 * i + 128]
                for i in range(2)
            ]
            tops = [jnp.max(row, axis=1, keepdims=True) for row in rows]
            both = jnp.maximum(tops[0], tops[1])
            yield
            for i in range(2):
                top = jnp.where(wide != 0, both, tops[i])
                expo = jnp.exp(rows[i] - top)
                expos[i].append(expo)
                dens[i].append(jnp.sum(expo, axis=1, keepdims=True))
            yield
        for i in range(2):
            den = jnp.broadcast_to(dens[i][0], (8, 128))
            for h in range(1, HEADS):
                den = jnp.where(head_of == h, dens[i][h], den)
            den_s[:, 128 * i : 128 * (i + 1)] = den
            yield

    def stage_e(expos, filt):
        for h in range(0, HEADS, 2):
            for i in range(2):
                at = slice(128 * i, 128 * (i + 1))
                two = [expos[i][h + n] * filt[8 * (h + n) : 8 * (h + n) + 8, at] for n in range(2)]
                coef_s[8 * h : 8 * h + 16, at] = jnp.concatenate(two, 0).astype(bf16)
            yield

    def stage_d(item, nums, dens):
        wide, starts = query_rows(item)
        yield
        yield
        yield
        res = []
        for i in range(2):
            one = nums[i][0:8]
            for h in range(1, HEADS):
                one = jnp.where(head_of == h, nums[i][8 * h : 8 * h + 8], one)
            res.append(one)
            yield
        for i in range(2):
            num = jnp.where(wide != 0, res[0] + res[1], res[i])
            den = jnp.where(wide != 0, dens[0] + dens[1], dens[i])
            acc_s[pl.ds(starts[i], CHUNK), :] = num / jnp.maximum(den, 1.0)
            yield

    def in_turns(*turns):
        turns = list(turns)
        while turns:
            for turn in list(turns):
                if next(turn, turns) is turns:
                    turns.remove(turn)

    def step(i, carry):
        basis = basis_s[...]
        r2 = r2_s[...]
        logits = logit_s[pl.ds(pl.multiple_of(((i + 1) & 3) * 64, 64), 64), :]
        env = env_s[pl.ds(pl.multiple_of(((i + 1) & 3) * 8, 8), 8), :]
        coef = coef_s[...]
        dens = [den_s[:, 128 * n : 128 * (n + 1)] for n in range(2)]
        active = active_s[...]
        at_v = pl.multiple_of((i & 7) * 256, 256)
        values = [v_s[pl.ds(at_v + 128 * n, 128), :] for n in range(2)]
        filt = [
            jnp.dot(
                w2_ref[:, top_half * n : top_half * (n + 1)],
                active[top_half * n : top_half * (n + 1)],
                preferred_element_type=f32,
            )
            for n in range(2)
        ]
        filt = filt[0] + filt[1]
        nums = [
            jnp.dot(coef[:, 128 * n : 128 * (n + 1)], values[n], preferred_element_type=f32)
            for n in range(2)
        ]
        first = jnp.dot(w1_ref[:top_half], basis, preferred_element_type=f32)
        second = jnp.dot(w1_ref[top_half:], basis, preferred_element_type=f32)
        expos = [[], []]
        in_turns(stage_c(order_ref[i + 1], logits, env, expos), stage_d(order_ref[i], nums, dens), stage_g(r2, i + 3))
        in_turns(stage_b(first, 0), stage_b(second, top_half), stage_a(order_ref[i + 4], i + 4), stage_e(expos, filt))
        return carry

    lax.fori_loop(0, total, step, 0)

    def finish(q, carry):
        at = pl.ds(pl.multiple_of(q * ATOM_BLOCK, ATOM_BLOCK), ATOM_BLOCK)
        row_id = lax.broadcasted_iota(jnp.int32, (ATOM_BLOCK, 128), 0) + q * ATOM_BLOCK
        out_ref[at, :] = jnp.where(row_id < count, acc_s[at, :], 0.0).astype(bf16)
        return carry

    lax.fori_loop(0, blocks, finish, 0)


def attend(scalars, lists, srcs, wq, wkv, w1, b1, w2):
    blocks = lists.shape[0]
    channels = srcs[0].shape[2]
    smem = pl.BlockSpec(memory_space=pltpu.SMEM)
    vmem = pl.BlockSpec(memory_space=pltpu.VMEM)
    hbm = pl.BlockSpec(memory_space=pl.ANY)
    f32 = jnp.float32
    slots = blocks * ATOM_BLOCK
    table = (slots // CHUNK + 8, 128)
    return pl.pallas_call(
        attend_kernel,
        out_shape=jax.ShapeDtypeStruct((slots, channels), jnp.bfloat16),
        in_specs=[smem] * 2 + [hbm] * SOURCES + [vmem] * 5,
        out_specs=vmem,
        scratch_shapes=[
            pltpu.VMEM((blocks, KEY_BLOCKS, ROWS, channels), jnp.bfloat16),
            pltpu.SemaphoreType.DMA((blocks, KEY_BLOCKS)),
            pltpu.VMEM((3, slots * KEY_BLOCKS + 8, 128), f32),
            pltpu.VMEM((slots + 8, 128), f32),
            pltpu.VMEM((slots + 8, 128), f32),
            pltpu.VMEM((slots + 8, 128), f32),
            pltpu.VMEM((128, 256), jnp.bfloat16),
            pltpu.VMEM((512, 256), jnp.bfloat16),
            pltpu.VMEM((256, 256), f32),
            pltpu.VMEM((64, 256), jnp.bfloat16),
            pltpu.VMEM((8, 256), f32),
            pltpu.VMEM((2048, 128), jnp.bfloat16),
            pltpu.VMEM((8, 256), f32),
            pltpu.VMEM((32, 256), f32),
            pltpu.VMEM(table, jnp.int32),
            pltpu.SemaphoreType.DMA((blocks + 1,)),
            pltpu.SMEM(table, jnp.int32),
            pltpu.SMEM((slots // CHUNK + 8,), jnp.int32),
        ],
        name="attend",
    )(scalars, lists, *srcs, wq, wkv, w1, b1, w2)


def shift(x, axis, by):
    size = lax.axis_size(axis)
    return lax.ppermute(x, axis, [(i, (i + by) % size) for i in range(size)])


def shards(
    features, positions, counts, neighbours, w_query, w_key, w_value, w_radial, b_radial, w_head
):
    row = lax.axis_index("gx")
    rows = lax.axis_size("gx")
    line = counts[:, 0]
    scalars = line[row][None]
    light, extra = make_payload(scalars, features[0, 0], positions[0, 0])
    dense = line > LIGHT_BLOCKS * ATOM_BLOCK
    extra = jnp.where(
        dense[(row - 1) % rows],
        shift(extra, "gx", 1),
        jnp.where(dense[(row + 1) % rows], shift(extra, "gx", -1), extra),
    )
    low, high = shift(light, "gy", 1), shift(light, "gy", -1)
    low, high, extra = lax.optimization_barrier((low, high, extra))
    column = jnp.concatenate([low, light, high], 0)
    srcs = [
        shift(column, "gx", 1), column, shift(column, "gx", -1),
        shift(extra, "gy", 1), extra, shift(extra, "gy", -1),
    ]
    wkv, w1, b1, w2 = make_weights(w_key, w_value, w_radial, b_radial, w_head)
    out = attend(scalars, neighbours[0, 0], srcs, w_query, wkv, w1, b1, w2)
    return out[None, None]


def solution(mesh):
    in_specs = (
        P("gx", "gy", None, None),
        P("gx", "gy", None, None),
        P(None, "gy"),
        P("gx", "gy", None, None),
        P(), P(), P(), P(), P(), P(),
    )
    out_specs = P("gx", "gy", None, None)
    return jax.shard_map(shards, mesh=mesh, in_specs=in_specs, out_specs=out_specs, check_vma=False)
```

```python
import math

import jax
import jax.numpy as jnp
from jax import lax
from jax.experimental import pallas as pl
from jax.experimental.pallas import tpu as pltpu
from jax.sharding import PartitionSpec as P

HEADS = 8
ATOM_BLOCK = 128
KEY_BLOCKS = 4
CUTOFF = 6.0
SHARPNESS = 4.0
MASKED = -1e30
LENGTH = 576.0
FAR = float(2**20)
POS_ROWS = 16
ROWS = ATOM_BLOCK + POS_ROWS
CHUNK = 8
LIGHT_BLOCKS = 7
UNITS = 32
SOURCES = 6


def payload_kernel(scalars_ref, rows_ref, pos_ref, light_ref, extra_ref):
    f32 = jnp.float32
    bf16 = jnp.bfloat16
    count = scalars_ref[0]
    lane = lax.broadcasted_iota(jnp.int32, (1, ATOM_BLOCK), 1)
    high_count = jnp.broadcast_to((count // 16 * 16).astype(f32), (1, ATOM_BLOCK))
    low_count = jnp.broadcast_to((count % 16).astype(f32), (1, ATOM_BLOCK))
    zeros = jnp.zeros((2, ATOM_BLOCK), f32)
    for q in range(rows_ref.shape[0] // ATOM_BLOCK):
        light = q < LIGHT_BLOCKS
        out = light_ref.at[q] if light else extra_ref.at[q - LIGHT_BLOCKS]
        at = slice(q * ATOM_BLOCK, (q + 1) * ATOM_BLOCK)
        out[:ATOM_BLOCK, :] = rows_ref[at, :]
        pos = pos_ref[:, at]
        pos = jnp.concatenate(
            [pos[:2], jnp.where(lane + q * ATOM_BLOCK < count, pos[2:3], FAR)], 0
        )
        hi = pos.astype(bf16).astype(f32)
        rest = pos - hi
        mid = rest.astype(bf16).astype(f32)
        begin = jnp.full((1, ATOM_BLOCK), float(q * ATOM_BLOCK), f32)
        terms = [hi, mid, rest - mid, zeros, high_count, low_count, begin, zeros]
        out[ATOM_BLOCK:, :] = jnp.concatenate(terms, 0).astype(bf16)


def make_payload(scalars, rows, pos):
    blocks = rows.shape[0] // ATOM_BLOCK
    return pl.pallas_call(
        payload_kernel,
        out_shape=[
            jax.ShapeDtypeStruct((n, ROWS, rows.shape[1]), jnp.bfloat16)
            for n in (LIGHT_BLOCKS, blocks - LIGHT_BLOCKS)
        ],
        in_specs=[pl.BlockSpec(memory_space=pltpu.SMEM)]
        + [pl.BlockSpec(memory_space=pltpu.VMEM)] * 2,
        out_specs=[pl.BlockSpec(memory_space=pltpu.VMEM)] * 2,
        name="payload",
    )(scalars, rows, pos)


def weights_kernel(key_ref, value_ref, radial_ref, bias_ref, head_ref, kv_ref, w1_ref, b1_ref, w2_ref):
    f32 = jnp.float32
    bf16 = jnp.bfloat16

    def split(shape, axis):
        index = lax.broadcasted_iota(jnp.int32, shape, axis)
        return lax.shift_right_logical(index, 3), index & (CHUNK - 1)

    def pick(condition):
        return jnp.where(condition, 1.0, 0.0).astype(bf16)

    def index(shape, axis):
        return lax.broadcasted_iota(jnp.int32, shape, axis)

    basis, radial = radial_ref.shape
    width, tall, heads = basis * CHUNK, radial * CHUNK, HEADS * CHUNK
    kv_ref[:, : key_ref.shape[1]] = key_ref[...]
    kv_ref[:, key_ref.shape[1] :] = value_ref[...]
    first = (((0,), (0,)), ((), ()))
    spread = pick(split((basis, width), 1)[0] == index((basis, width), 0))
    w1 = lax.dot_general(radial_ref[...], spread, first, preferred_element_type=f32)
    rows = pick(split((tall, radial), 0)[0] == index((tall, radial), 1))
    w1 = jnp.dot(rows, w1.astype(bf16), preferred_element_type=f32)
    same = split((tall, width), 0)[1] == split((tall, width), 1)[1]
    w1_ref[...] = jnp.where(same, 0.5 * w1, 0.0).astype(bf16)
    spread = pick(split((radial, tall), 1)[0] == index((radial, tall), 0))
    w2 = lax.dot_general(head_ref[...], spread, first, preferred_element_type=f32)
    rows = pick(split((heads, HEADS), 0)[0] == index((heads, HEADS), 1))
    w2 = jnp.dot(rows, w2.astype(bf16), preferred_element_type=f32)
    same = split((heads, tall), 0)[1] == split((heads, tall), 1)[1]
    w2_ref[...] = jnp.where(same, w2, 0.0).astype(bf16)
    here = split((tall, radial), 0)[0] == index((tall, radial), 1)
    bias = jnp.sum(jnp.where(here, 0.5 * bias_ref[...], 0.0), axis=1, keepdims=True)
    b1_ref[...] = jnp.broadcast_to(bias, b1_ref.shape)


def make_weights(w_key, w_value, w_radial, b_radial, w_head):
    basis, radial = w_radial.shape
    channels = w_key.shape[0]
    bf16 = jnp.bfloat16
    return pl.pallas_call(
        weights_kernel,
        out_shape=[
            jax.ShapeDtypeStruct((channels, 2 * channels), bf16),
            jax.ShapeDtypeStruct((radial * CHUNK, basis * CHUNK), bf16),
            jax.ShapeDtypeStruct((radial * CHUNK, 128), jnp.float32),
            jax.ShapeDtypeStruct((HEADS * CHUNK, radial * CHUNK), bf16),
        ],
        in_specs=[pl.BlockSpec(memory_space=pltpu.VMEM)] * 5,
        out_specs=[pl.BlockSpec(memory_space=pltpu.VMEM)] * 4,
        name="weights",
    )(w_key, w_value, w_radial, b_radial[None], w_head)


def attend_kernel(info_ref, lists_ref, *refs):
    srcs = refs[:SOURCES]
    wq_ref, wkv_ref, w1_ref, b1_ref, w2_ref, out_ref = refs[SOURCES : SOURCES + 6]
    xbuf, sems, kvp_s, q_s, qp_s, acc_s, basis_s, active_s, logit_s, coef_s, den_s, v_s, r2_s, env_s, table_v, table_sem, items_ref, order_ref = refs[SOURCES + 6 :]
    blocks = out_ref.shape[0] // ATOM_BLOCK
    slots = blocks * ATOM_BLOCK
    dummy = blocks * KEY_BLOCKS * ATOM_BLOCK
    count = info_ref[0]
    chunks = ATOM_BLOCK // CHUNK
    none = blocks * chunks
    live_blocks = (count + ATOM_BLOCK - 1) // ATOM_BLOCK
    bf16 = jnp.bfloat16
    f32 = jnp.float32

    def listed(q, e):
        item = lists_ref[q, e]
        brick = lax.shift_right_logical(item, 4)
        part = lax.shift_right_logical(brick * 11, 5)
        return item, item & (blocks - 1), part, brick - 3 * part

    def fetch(q, carry):
        for e in range(KEY_BLOCKS):
            _, block, part, side = listed(q, e)
            light = block < LIGHT_BLOCKS
            source = jnp.where(light, part, 3 + side)
            block = jnp.where(light, side * LIGHT_BLOCKS + block, block - LIGHT_BLOCKS)

            def among(low, high):
                if high - low == 1:
                    pltpu.make_async_copy(
                        srcs[low].at[block], xbuf.at[q, e], sems.at[q, e]
                    ).start()
                    return
                middle = (low + high) // 2
                pl.when(source < middle)(lambda: among(low, middle))
                pl.when(source >= middle)(lambda: among(middle, high))

            among(0, SOURCES)
        return carry

    lax.fori_loop(0, live_blocks, fetch, 0)

    lane = lax.broadcasted_iota(jnp.int32, (CHUNK, 128), 1)
    head_of = lane // 16
    sub2 = lax.broadcasted_iota(jnp.int32, (2 * CHUNK, 128), 0)
    lane2 = lax.broadcasted_iota(jnp.int32, (2 * CHUNK, 128), 1)
    head_masks = [
        jnp.where(lane2 // 16 == 2 * i + sub2 // CHUNK, 1.0, 0.0).astype(bf16) for i in range(4)
    ]

    kvp_s[0, pl.ds(dummy, 8), :] = jnp.zeros((8, 128), f32)
    kvp_s[1, pl.ds(dummy, 8), :] = jnp.zeros((8, 128), f32)
    kvp_s[2, pl.ds(dummy, 8), :] = jnp.where(
        lane % 64 == 2, FAR, 0.0
    ).astype(f32)
    q_s[pl.ds(slots, 8), :] = jnp.zeros((8, 128), f32)
    qp_s[pl.ds(slots, 8), :] = jnp.zeros((8, 128), f32)
    for ref in (basis_s, active_s, logit_s, coef_s, den_s, v_s, r2_s, env_s):
        ref[...] = jnp.zeros_like(ref)

    def project(q, carry):
        for e in range(KEY_BLOCKS):
            pltpu.make_async_copy(srcs[0].at[0], xbuf.at[q, e], sems.at[q, e]).wait()

        unit = lax.broadcasted_iota(jnp.int32, (chunks, 128), 1).astype(f32)
        chunk_id = lax.broadcasted_iota(jnp.int32, (chunks, 128), 0)
        first = (q * ATOM_BLOCK + CHUNK * chunk_id).astype(f32)
        rows = jnp.full((chunks, 128), float(dummy), f32)
        ends = jnp.zeros((chunks, 128), f32)
        mats = []
        for e in range(KEY_BLOCKS):
            _, _, part, side = listed(q, e)
            shift_x = (part - 1).astype(f32) * CUTOFF
            shift_y = (side - 1).astype(f32) * CUTOFF
            m = xbuf[q, e, ATOM_BLOCK:, :].astype(f32)
            key_count = m[11:12] + m[12:13]
            ratio = key_count / count.astype(f32)
            reach = key_count * (CUTOFF / LENGTH)
            begin = m[13:14]
            low = jnp.floor(first * ratio - reach - 1.05) + 1.0 - begin
            high = jnp.ceil((first + CHUNK) * ratio + reach + 0.05) - 1.0 - begin
            low = jnp.maximum(low, 0.0)
            high = jnp.minimum(high, jnp.minimum(key_count - 1.0 - begin, ATOM_BLOCK - 1.0))
            size = jnp.where(first < count.astype(f32), jnp.maximum(high - low + 1.0, 0.0), 0.0)
            units = jnp.floor((size + 7.0) * 0.125)
            low = jnp.minimum(low, ATOM_BLOCK - 8.0 * units)
            base = ((q * KEY_BLOCKS + e) * ATOM_BLOCK).astype(f32)
            rows = jnp.where(
                (unit >= ends) & (unit < ends + units), base + low + 8.0 * (unit - ends), rows
            )
            ends = ends + units
            place = (m[0:3] + m[3:6]) + m[6:9]
            axis = lax.broadcasted_iota(jnp.int32, (3, 128), 0)
            place = place + jnp.where(axis == 0, shift_x, jnp.where(axis == 1, shift_y, 0.0))
            mats.append(jnp.concatenate([place, jnp.zeros((13, 128), f32)], 0))
        turned = jnp.transpose(jnp.concatenate(mats + mats, 0))
        own = pl.ds(pl.multiple_of(q * ATOM_BLOCK, ATOM_BLOCK), ATOM_BLOCK)
        qp_s[own, :] = turned
        for e in range(KEY_BLOCKS):
            at = pl.ds(
                pl.multiple_of((q * KEY_BLOCKS + e) * ATOM_BLOCK, ATOM_BLOCK), ATOM_BLOCK
            )
            kvp_s[2, at, :] = pltpu.roll(turned, 128 - 16 * e, 1) if e else turned
            x = xbuf[q, e, :ATOM_BLOCK, :]
            kv = jnp.dot(x, wkv_ref[...], preferred_element_type=f32)
            kv = kv.astype(bf16).astype(f32)
            kvp_s[0, at, :] = kv[:, :128]
            kvp_s[1, at, :] = kv[:, 128:]
        query = jnp.dot(xbuf[q, 0, :ATOM_BLOCK, :], wq_ref[...], preferred_element_type=f32)
        q_s[own, :] = query.astype(bf16).astype(f32) * 0.25
        wide = jnp.where(ends > UNITS // 2, 1.0, 0.0)
        even = chunk_id % 2 == 0
        wide = jnp.maximum(
            wide, jnp.where(even, pltpu.roll(wide, chunks - 1, 0), pltpu.roll(wide, 1, 0))
        )
        following = pltpu.roll(pltpu.roll(rows, chunks - 1, 0), UNITS // 2, 1)
        joined = (wide < 0.5) & (unit >= UNITS // 2)
        rows = jnp.where(joined, following, rows)
        rows = jnp.where(unit == UNITS, wide, rows)
        at = pl.ds(pl.multiple_of(q * chunks, chunks), chunks)
        table_v[at, :] = rows.astype(jnp.int32)
        pltpu.make_async_copy(table_v.at[at], items_ref.at[at], table_sem.at[q]).start()
        return carry

    end = pl.ds(none, 8)
    table_v[end, :] = jnp.where(lane == UNITS, 0, dummy)
    last = pltpu.make_async_copy(table_v.at[end], items_ref.at[end], table_sem.at[blocks])
    last.start()
    lax.fori_loop(0, live_blocks, project, 0)
    last.wait()

    def await_table(q, carry):
        at = pl.ds(pl.multiple_of(q * chunks, chunks), chunks)
        pltpu.make_async_copy(table_v.at[at], items_ref.at[at], table_sem.at[q]).wait()
        return carry

    lax.fori_loop(0, live_blocks, await_table, 0)

    def enlist(p, n):
        order_ref[n] = 2 * p
        order_ref[n + 1] = 2 * p + 1
        return n + 1 + items_ref[2 * p, UNITS]

    for n in range(4):
        order_ref[n] = none
    total = lax.fori_loop(
        0, lax.shift_right_logical(count + 2 * CHUNK - 1, 4), enlist, 4
    )
    for n in range(4):
        order_ref[total + n] = none

    contract_last = (((1,), (1,)), ((), ()))
    top_half = w1_ref.shape[0] // 2

    def query_rows(item):
        pair = lax.shift_right_logical(item, 1)
        wide = items_ref[item, UNITS]
        first = jnp.where(wide != 0, item, 2 * pair)
        second = jnp.where(wide != 0, item, 2 * pair + 1)
        first = jnp.minimum(first * CHUNK, slots)
        second = jnp.minimum(second * CHUNK, slots)
        return wide, (pl.multiple_of(first, CHUNK), pl.multiple_of(second, CHUNK))


    def stage_a(item, slot):
        _, starts = query_rows(item)
        places = []
        for half in range(2):
            at = slice(128 * half, 128 * (half + 1))
            parts = [[], [], []]
            for j in range(UNITS // 2):
                row = items_ref[item, half * (UNITS // 2) + j]
                for n in range(3):
                    parts[n].append(kvp_s[n, pl.ds(row, 8), :])
            places.append(parts[2])
            keys = jnp.concatenate(parts[0], 0).astype(bf16)
            v_s[pl.ds(pl.multiple_of((slot & 7) * 256 + 128 * half, 128), 128), :] = (
                jnp.concatenate(parts[1], 0).astype(bf16)
            )
            qc = q_s[pl.ds(starts[half], CHUNK), :]
            qq = jnp.concatenate([qc, qc], 0).astype(bf16)
            q_exp = jnp.concatenate([qq * m for m in head_masks], 0)
            logit_s[pl.ds(pl.multiple_of((slot & 3) * 64, 64), 64), at] = lax.dot_general(
                q_exp, keys, contract_last, preferred_element_type=f32
            )
            yield
        turned = jnp.transpose(
            jnp.concatenate([jnp.where(lane < 64, x, y) for x, y in zip(*places)], 0)
        )
        yield
        for half in range(2):
            at = slice(128 * half, 128 * (half + 1))
            qp = qp_s[pl.ds(starts[half], CHUNK), :]
            r2 = 0.0
            for a in range(3):
                diff = qp[:, a : a + 1] - turned[64 * half + a : 64 * half + a + 1, :]
                r2 = r2 + diff * diff
            r2_s[:, at] = r2
            yield

    def stage_g(r2_both, slot):
        scale = math.sqrt(SHARPNESS * math.log2(math.e))
        for half in range(2):
            at = slice(128 * half, 128 * (half + 1))
            r2 = r2_both[:, at]
            valid = r2 < CUTOFF * CUTOFF
            inside = 1.0 - r2 * (1.0 / (CUTOFF * CUTOFF))
            env_s[pl.ds(pl.multiple_of((slot & 3) * 8, 8), 8), at] = jnp.where(
                valid, 2.0 * jnp.log(jnp.where(valid, inside, 1.0)), MASKED
            )
            r = jnp.sqrt(r2) * scale
            yield
            for k in range(0, 16, 2):
                two = []
                for kk in (k, k + 1):
                    t = r - (CUTOFF / 15 * kk) * scale
                    two.append(jnp.exp2(-(t * t)))
                basis_s[8 * k : 8 * k + 16, at] = jnp.concatenate(two, 0).astype(bf16)
                yield

    def stage_b(hidden, base):
        for t in range(0, hidden.shape[0], 16):
            bias = b1_ref[base + t : base + t + 16, :]
            x = hidden[t : t + 16] + jnp.concatenate([bias, bias], 1)
            active_s[base + t : base + t + 16, :] = (x + x * jnp.tanh(x)).astype(bf16)
            yield

    def stage_c(item, logits, env, expos):
        wide, _ = query_rows(item)
        dens = [[], []]
        for h in range(HEADS):
            rows = [
                logits[8 * h : 8 * h + 8, 128 * i : 128 * i + 128] + env[:, 128 * i : 128 * i + 128]
                for i in range(2)
            ]
            tops = [jnp.max(row, axis=1, keepdims=True) for row in rows]
            both = jnp.maximum(tops[0], tops[1])
            yield
            for i in range(2):
                top = jnp.where(wide != 0, both, tops[i])
                expo = jnp.exp(rows[i] - top)
                expos[i].append(expo)
                dens[i].append(jnp.sum(expo, axis=1, keepdims=True))
            yield
        for i in range(2):
            den = jnp.broadcast_to(dens[i][0], (8, 128))
            for h in range(1, HEADS):
                den = jnp.where(head_of == h, dens[i][h], den)
            den_s[:, 128 * i : 128 * (i + 1)] = den
            yield

    def stage_e(expos, filt):
        for h in range(0, HEADS, 2):
            for i in range(2):
                at = slice(128 * i, 128 * (i + 1))
                two = [expos[i][h + n] * filt[8 * (h + n) : 8 * (h + n) + 8, at] for n in range(2)]
                coef_s[8 * h : 8 * h + 16, at] = jnp.concatenate(two, 0).astype(bf16)
            yield

    def stage_d(item, nums, dens):
        wide, starts = query_rows(item)
        yield
        yield
        yield
        res = []
        for i in range(2):
            one = nums[i][0:8]
            for h in range(1, HEADS):
                one = jnp.where(head_of == h, nums[i][8 * h : 8 * h + 8], one)
            res.append(one)
            yield
        for i in range(2):
            num = jnp.where(wide != 0, res[0] + res[1], res[i])
            den = jnp.where(wide != 0, dens[0] + dens[1], dens[i])
            acc_s[pl.ds(starts[i], CHUNK), :] = num / jnp.maximum(den, 1.0)
            yield

    def in_turns(*turns):
        turns = list(turns)
        while turns:
            for turn in list(turns):
                if next(turn, turns) is turns:
                    turns.remove(turn)

    def step(i, carry):
        basis = basis_s[...]
        r2 = r2_s[...]
        logits = logit_s[pl.ds(pl.multiple_of(((i + 1) & 3) * 64, 64), 64), :]
        env = env_s[pl.ds(pl.multiple_of(((i + 1) & 3) * 8, 8), 8), :]
        coef = coef_s[...]
        dens = [den_s[:, 128 * n : 128 * (n + 1)] for n in range(2)]
        active = active_s[...]
        at_v = pl.multiple_of((i & 7) * 256, 256)
        values = [v_s[pl.ds(at_v + 128 * n, 128), :] for n in range(2)]
        filt = [
            jnp.dot(
                w2_ref[:, top_half * n : top_half * (n + 1)],
                active[top_half * n : top_half * (n + 1)],
                preferred_element_type=f32,
            )
            for n in range(2)
        ]
        filt = filt[0] + filt[1]
        nums = [
            jnp.dot(coef[:, 128 * n : 128 * (n + 1)], values[n], preferred_element_type=f32)
            for n in range(2)
        ]
        first = jnp.dot(w1_ref[:top_half], basis, preferred_element_type=f32)
        second = jnp.dot(w1_ref[top_half:], basis, preferred_element_type=f32)
        expos = [[], []]
        in_turns(stage_c(order_ref[i + 1], logits, env, expos), stage_d(order_ref[i], nums, dens), stage_g(r2, i + 3))
        in_turns(stage_b(first, 0), stage_b(second, top_half), stage_a(order_ref[i + 4], i + 4), stage_e(expos, filt))
        return carry

    lax.fori_loop(0, total, step, 0)

    def finish(q, carry):
        at = pl.ds(pl.multiple_of(q * ATOM_BLOCK, ATOM_BLOCK), ATOM_BLOCK)
        row_id = lax.broadcasted_iota(jnp.int32, (ATOM_BLOCK, 128), 0) + q * ATOM_BLOCK
        out_ref[at, :] = jnp.where(row_id < count, acc_s[at, :], 0.0).astype(bf16)
        return carry

    lax.fori_loop(0, blocks, finish, 0)


def attend(scalars, lists, srcs, wq, wkv, w1, b1, w2):
    blocks = lists.shape[0]
    channels = srcs[0].shape[2]
    smem = pl.BlockSpec(memory_space=pltpu.SMEM)
    vmem = pl.BlockSpec(memory_space=pltpu.VMEM)
    hbm = pl.BlockSpec(memory_space=pl.ANY)
    f32 = jnp.float32
    slots = blocks * ATOM_BLOCK
    table = (slots // CHUNK + 8, 128)
    return pl.pallas_call(
        attend_kernel,
        out_shape=jax.ShapeDtypeStruct((slots, channels), jnp.bfloat16),
        in_specs=[smem] * 2 + [hbm] * SOURCES + [vmem] * 5,
        out_specs=vmem,
        scratch_shapes=[
            pltpu.VMEM((blocks, KEY_BLOCKS, ROWS, channels), jnp.bfloat16),
            pltpu.SemaphoreType.DMA((blocks, KEY_BLOCKS)),
            pltpu.VMEM((3, slots * KEY_BLOCKS + 8, 128), f32),
            pltpu.VMEM((slots + 8, 128), f32),
            pltpu.VMEM((slots + 8, 128), f32),
            pltpu.VMEM((slots + 8, 128), f32),
            pltpu.VMEM((128, 256), jnp.bfloat16),
            pltpu.VMEM((512, 256), jnp.bfloat16),
            pltpu.VMEM((256, 256), f32),
            pltpu.VMEM((64, 256), jnp.bfloat16),
            pltpu.VMEM((8, 256), f32),
            pltpu.VMEM((2048, 128), jnp.bfloat16),
            pltpu.VMEM((8, 256), f32),
            pltpu.VMEM((32, 256), f32),
            pltpu.VMEM(table, jnp.int32),
            pltpu.SemaphoreType.DMA((blocks + 1,)),
            pltpu.SMEM(table, jnp.int32),
            pltpu.SMEM((slots // CHUNK + 8,), jnp.int32),
        ],
        name="attend",
    )(scalars, lists, *srcs, wq, wkv, w1, b1, w2)


def shift(x, axis, by):
    size = lax.axis_size(axis)
    return lax.ppermute(x, axis, [(i, (i + by) % size) for i in range(size)])


def shards(
    features, positions, counts, neighbours, w_query, w_key, w_value, w_radial, b_radial, w_head
):
    row = lax.axis_index("gx")
    rows = lax.axis_size("gx")
    line = counts[:, 0]
    scalars = line[row][None]
    light, extra = make_payload(scalars, features[0, 0], positions[0, 0])
    dense = line > LIGHT_BLOCKS * ATOM_BLOCK
    extra = jnp.where(
        dense[(row - 1) % rows],
        shift(extra, "gx", 1),
        jnp.where(dense[(row + 1) % rows], shift(extra, "gx", -1), extra),
    )
    low, high = shift(light, "gy", 1), shift(light, "gy", -1)
    further = [shift(extra, "gy", 1), extra, shift(extra, "gy", -1)]
    low, high, _ = lax.optimization_barrier((low, high, extra))
    column = jnp.concatenate([low, light, high], 0)
    srcs = [shift(column, "gx", 1), column, shift(column, "gx", -1)] + further
    wkv, w1, b1, w2 = make_weights(w_key, w_value, w_radial, b_radial, w_head)
    out = attend(scalars, neighbours[0, 0], srcs, w_query, wkv, w1, b1, w2)
    return out[None, None]


def solution(mesh):
    in_specs = (
        P("gx", "gy", None, None),
        P("gx", "gy", None, None),
        P(None, "gy"),
        P("gx", "gy", None, None),
        P(), P(), P(), P(), P(), P(),
    )
    out_specs = P("gx", "gy", None, None)
    return jax.shard_map(shards, mesh=mesh, in_specs=in_specs, out_specs=out_specs, check_vma=False)
```

```python
import math

import jax
import jax.numpy as jnp
from jax import lax
from jax.experimental import pallas as pl
from jax.experimental.pallas import tpu as pltpu
from jax.sharding import PartitionSpec as P

HEADS = 8
ATOM_BLOCK = 128
KEY_BLOCKS = 4
CUTOFF = 6.0
SHARPNESS = 4.0
MASKED = -1e30
LENGTH = 576.0
FAR = float(2**20)
POS_ROWS = 16
ROWS = ATOM_BLOCK + POS_ROWS
CHUNK = 8
LIGHT_BLOCKS = 7
UNITS = 32
SOURCES = 6


def payload_kernel(line_ref, row_ref, rows_ref, pos_ref, light_ref, extra_ref):
    f32 = jnp.float32
    bf16 = jnp.bfloat16
    count = line_ref[0, row_ref[0]]
    lane = lax.broadcasted_iota(jnp.int32, (1, ATOM_BLOCK), 1)
    high_count = jnp.broadcast_to((count // 16 * 16).astype(f32), (1, ATOM_BLOCK))
    low_count = jnp.broadcast_to((count % 16).astype(f32), (1, ATOM_BLOCK))
    zeros = jnp.zeros((2, ATOM_BLOCK), f32)
    for q in range(rows_ref.shape[0] // ATOM_BLOCK):
        light = q < LIGHT_BLOCKS
        out = light_ref.at[q] if light else extra_ref.at[q - LIGHT_BLOCKS]
        at = slice(q * ATOM_BLOCK, (q + 1) * ATOM_BLOCK)
        out[:ATOM_BLOCK, :] = rows_ref[at, :]
        pos = [pos_ref[a, :, at] for a in range(3)]
        pos[2] = jnp.where(lane + q * ATOM_BLOCK < count, pos[2], FAR)
        pos = jnp.concatenate(pos, 0)
        hi = pos.astype(bf16).astype(f32)
        rest = pos - hi
        mid = rest.astype(bf16).astype(f32)
        begin = jnp.full((1, ATOM_BLOCK), float(q * ATOM_BLOCK), f32)
        terms = [hi, mid, rest - mid, zeros, high_count, low_count, begin, zeros]
        out[ATOM_BLOCK:, :] = jnp.concatenate(terms, 0).astype(bf16)


def make_payload(line, row, rows, pos):
    blocks = rows.shape[0] // ATOM_BLOCK
    return pl.pallas_call(
        payload_kernel,
        out_shape=[
            jax.ShapeDtypeStruct((n, ROWS, rows.shape[1]), jnp.bfloat16)
            for n in (LIGHT_BLOCKS, blocks - LIGHT_BLOCKS)
        ],
        in_specs=[pl.BlockSpec(memory_space=pltpu.SMEM)] * 2
        + [pl.BlockSpec(memory_space=pltpu.VMEM)] * 2,
        out_specs=[pl.BlockSpec(memory_space=pltpu.VMEM)] * 2,
        name="payload",
    )(line, row, rows, pos)


def weights_kernel(key_ref, value_ref, radial_ref, bias_ref, head_ref, kv_ref, w1_ref, b1_ref, w2_ref):
    f32 = jnp.float32
    bf16 = jnp.bfloat16

    def split(shape, axis):
        index = lax.broadcasted_iota(jnp.int32, shape, axis)
        return lax.shift_right_logical(index, 3), index & (CHUNK - 1)

    def pick(condition):
        return jnp.where(condition, 1.0, 0.0).astype(bf16)

    def index(shape, axis):
        return lax.broadcasted_iota(jnp.int32, shape, axis)

    basis, radial = radial_ref.shape
    width, tall, heads = basis * CHUNK, radial * CHUNK, HEADS * CHUNK
    kv_ref[:, : key_ref.shape[1]] = key_ref[...]
    kv_ref[:, key_ref.shape[1] :] = value_ref[...]
    first = (((0,), (0,)), ((), ()))
    spread = pick(split((basis, width), 1)[0] == index((basis, width), 0))
    w1 = lax.dot_general(radial_ref[...], spread, first, preferred_element_type=f32)
    rows = pick(split((tall, radial), 0)[0] == index((tall, radial), 1))
    w1 = jnp.dot(rows, w1.astype(bf16), preferred_element_type=f32)
    same = split((tall, width), 0)[1] == split((tall, width), 1)[1]
    w1_ref[...] = jnp.where(same, 0.5 * w1, 0.0).astype(bf16)
    spread = pick(split((radial, tall), 1)[0] == index((radial, tall), 0))
    w2 = lax.dot_general(head_ref[...], spread, first, preferred_element_type=f32)
    rows = pick(split((heads, HEADS), 0)[0] == index((heads, HEADS), 1))
    w2 = jnp.dot(rows, w2.astype(bf16), preferred_element_type=f32)
    same = split((heads, tall), 0)[1] == split((heads, tall), 1)[1]
    w2_ref[...] = jnp.where(same, w2, 0.0).astype(bf16)
    here = split((tall, radial), 0)[0] == index((tall, radial), 1)
    bias = jnp.sum(jnp.where(here, 0.5 * bias_ref[...], 0.0), axis=1, keepdims=True)
    b1_ref[...] = jnp.broadcast_to(bias, b1_ref.shape)


def make_weights(w_key, w_value, w_radial, b_radial, w_head):
    basis, radial = w_radial.shape
    channels = w_key.shape[0]
    bf16 = jnp.bfloat16
    return pl.pallas_call(
        weights_kernel,
        out_shape=[
            jax.ShapeDtypeStruct((channels, 2 * channels), bf16),
            jax.ShapeDtypeStruct((radial * CHUNK, basis * CHUNK), bf16),
            jax.ShapeDtypeStruct((radial * CHUNK, 128), jnp.float32),
            jax.ShapeDtypeStruct((HEADS * CHUNK, radial * CHUNK), bf16),
        ],
        in_specs=[pl.BlockSpec(memory_space=pltpu.VMEM)] * 5,
        out_specs=[pl.BlockSpec(memory_space=pltpu.VMEM)] * 4,
        name="weights",
    )(w_key, w_value, w_radial, b_radial[None], w_head)


def attend_kernel(line_ref, row_ref, lists_ref, *refs):
    srcs = refs[:SOURCES]
    wq_ref, wkv_ref, w1_ref, b1_ref, w2_ref, out_ref = refs[SOURCES : SOURCES + 6]
    xbuf, sems, kvp_s, q_s, qp_s, acc_s, basis_s, active_s, logit_s, coef_s, den_s, v_s, r2_s, env_s, table_v, table_sem, items_ref, order_ref = refs[SOURCES + 6 :]
    blocks = out_ref.shape[0] // ATOM_BLOCK
    slots = blocks * ATOM_BLOCK
    dummy = blocks * KEY_BLOCKS * ATOM_BLOCK
    count = line_ref[0, row_ref[0]]
    chunks = ATOM_BLOCK // CHUNK
    none = blocks * chunks
    live_blocks = (count + ATOM_BLOCK - 1) // ATOM_BLOCK
    bf16 = jnp.bfloat16
    f32 = jnp.float32

    def listed(q, e):
        item = lists_ref[q, e]
        brick = lax.shift_right_logical(item, 4)
        part = lax.shift_right_logical(brick * 11, 5)
        return item, item & (blocks - 1), part, brick - 3 * part

    def fetch(q, carry):
        for e in range(KEY_BLOCKS):
            _, block, part, side = listed(q, e)
            light = block < LIGHT_BLOCKS
            source = jnp.where(light, part, 3 + side)
            block = jnp.where(light, side * LIGHT_BLOCKS + block, block - LIGHT_BLOCKS)

            def among(low, high):
                if high - low == 1:
                    pltpu.make_async_copy(
                        srcs[low].at[block], xbuf.at[q, e], sems.at[q, e]
                    ).start()
                    return
                middle = (low + high) // 2
                pl.when(source < middle)(lambda: among(low, middle))
                pl.when(source >= middle)(lambda: among(middle, high))

            if e == 0:
                pl.when(light)(lambda: among(1, 2))
                pl.when(jnp.logical_not(light))(lambda: among(4, 5))
            else:
                among(0, SOURCES)
        return carry

    lax.fori_loop(0, live_blocks, fetch, 0)

    lane = lax.broadcasted_iota(jnp.int32, (CHUNK, 128), 1)
    head_of = lane // 16
    sub2 = lax.broadcasted_iota(jnp.int32, (2 * CHUNK, 128), 0)
    lane2 = lax.broadcasted_iota(jnp.int32, (2 * CHUNK, 128), 1)
    head_masks = [
        jnp.where(lane2 // 16 == 2 * i + sub2 // CHUNK, 1.0, 0.0).astype(bf16) for i in range(4)
    ]

    kvp_s[0, pl.ds(dummy, 8), :] = jnp.zeros((8, 128), f32)
    kvp_s[1, pl.ds(dummy, 8), :] = jnp.zeros((8, 128), f32)
    kvp_s[2, pl.ds(dummy, 8), :] = jnp.where(
        lane % 64 == 2, FAR, 0.0
    ).astype(f32)
    q_s[pl.ds(slots, 8), :] = jnp.zeros((8, 128), f32)
    qp_s[pl.ds(slots, 8), :] = jnp.zeros((8, 128), f32)
    for ref in (basis_s, active_s, logit_s, coef_s, den_s, v_s, r2_s, env_s):
        ref[...] = jnp.zeros_like(ref)

    def project(q, carry):
        for e in range(KEY_BLOCKS):
            pltpu.make_async_copy(srcs[0].at[0], xbuf.at[q, e], sems.at[q, e]).wait()

        unit = lax.broadcasted_iota(jnp.int32, (chunks, 128), 1).astype(f32)
        chunk_id = lax.broadcasted_iota(jnp.int32, (chunks, 128), 0)
        first = (q * ATOM_BLOCK + CHUNK * chunk_id).astype(f32)
        rows = jnp.full((chunks, 128), float(dummy), f32)
        ends = jnp.zeros((chunks, 128), f32)
        mats = []
        for e in range(KEY_BLOCKS):
            _, _, part, side = listed(q, e)
            shift_x = (part - 1).astype(f32) * CUTOFF
            shift_y = (side - 1).astype(f32) * CUTOFF
            m = xbuf[q, e, ATOM_BLOCK:, :].astype(f32)
            key_count = m[11:12] + m[12:13]
            ratio = key_count / count.astype(f32)
            reach = key_count * (CUTOFF / LENGTH)
            begin = m[13:14]
            low = jnp.floor(first * ratio - reach - 1.05) + 1.0 - begin
            high = jnp.ceil((first + CHUNK) * ratio + reach + 0.05) - 1.0 - begin
            low = jnp.maximum(low, 0.0)
            high = jnp.minimum(high, jnp.minimum(key_count - 1.0 - begin, ATOM_BLOCK - 1.0))
            size = jnp.where(first < count.astype(f32), jnp.maximum(high - low + 1.0, 0.0), 0.0)
            units = jnp.floor((size + 7.0) * 0.125)
            low = jnp.minimum(low, ATOM_BLOCK - 8.0 * units)
            base = ((q * KEY_BLOCKS + e) * ATOM_BLOCK).astype(f32)
            rows = jnp.where(
                (unit >= ends) & (unit < ends + units), base + low + 8.0 * (unit - ends), rows
            )
            ends = ends + units
            place = (m[0:3] + m[3:6]) + m[6:9]
            axis = lax.broadcasted_iota(jnp.int32, (3, 128), 0)
            place = place + jnp.where(axis == 0, shift_x, jnp.where(axis == 1, shift_y, 0.0))
            mats.append(jnp.concatenate([place, jnp.zeros((13, 128), f32)], 0))
        turned = jnp.transpose(jnp.concatenate(mats + mats, 0))
        own = pl.ds(pl.multiple_of(q * ATOM_BLOCK, ATOM_BLOCK), ATOM_BLOCK)
        qp_s[own, :] = turned
        for e in range(KEY_BLOCKS):
            at = pl.ds(
                pl.multiple_of((q * KEY_BLOCKS + e) * ATOM_BLOCK, ATOM_BLOCK), ATOM_BLOCK
            )
            kvp_s[2, at, :] = pltpu.roll(turned, 128 - 16 * e, 1) if e else turned
            x = xbuf[q, e, :ATOM_BLOCK, :]
            kv = jnp.dot(x, wkv_ref[...], preferred_element_type=f32)
            kv = kv.astype(bf16).astype(f32)
            kvp_s[0, at, :] = kv[:, :128]
            kvp_s[1, at, :] = kv[:, 128:]
        query = jnp.dot(xbuf[q, 0, :ATOM_BLOCK, :], wq_ref[...], preferred_element_type=f32)
        q_s[own, :] = query.astype(bf16).astype(f32) * 0.25
        wide = jnp.where(ends > UNITS // 2, 1.0, 0.0)
        even = chunk_id % 2 == 0
        wide = jnp.maximum(
            wide, jnp.where(even, pltpu.roll(wide, chunks - 1, 0), pltpu.roll(wide, 1, 0))
        )
        following = pltpu.roll(pltpu.roll(rows, chunks - 1, 0), UNITS // 2, 1)
        joined = (wide < 0.5) & (unit >= UNITS // 2)
        rows = jnp.where(joined, following, rows)
        rows = jnp.where(unit == UNITS, wide, rows)
        at = pl.ds(pl.multiple_of(q * chunks, chunks), chunks)
        table_v[at, :] = rows.astype(jnp.int32)
        pltpu.make_async_copy(table_v.at[at], items_ref.at[at], table_sem.at[q]).start()
        return carry

    end = pl.ds(none, 8)
    table_v[end, :] = jnp.where(lane == UNITS, 0, dummy)
    last = pltpu.make_async_copy(table_v.at[end], items_ref.at[end], table_sem.at[blocks])
    last.start()
    lax.fori_loop(0, live_blocks, project, 0)
    last.wait()

    def await_table(q, carry):
        at = pl.ds(pl.multiple_of(q * chunks, chunks), chunks)
        pltpu.make_async_copy(table_v.at[at], items_ref.at[at], table_sem.at[q]).wait()
        return carry

    lax.fori_loop(0, live_blocks, await_table, 0)

    def enlist(p, n):
        order_ref[n] = 2 * p
        order_ref[n + 1] = 2 * p + 1
        return n + 1 + items_ref[2 * p, UNITS]

    for n in range(4):
        order_ref[n] = none
    total = lax.fori_loop(
        0, lax.shift_right_logical(count + 2 * CHUNK - 1, 4), enlist, 4
    )
    for n in range(4):
        order_ref[total + n] = none

    contract_last = (((1,), (1,)), ((), ()))
    top_half = w1_ref.shape[0] // 2

    def query_rows(item):
        pair = lax.shift_right_logical(item, 1)
        wide = items_ref[item, UNITS]
        first = jnp.where(wide != 0, item, 2 * pair)
        second = jnp.where(wide != 0, item, 2 * pair + 1)
        first = jnp.minimum(first * CHUNK, slots)
        second = jnp.minimum(second * CHUNK, slots)
        return wide, (pl.multiple_of(first, CHUNK), pl.multiple_of(second, CHUNK))


    def stage_a(item, slot):
        _, starts = query_rows(item)
        places = []
        for half in range(2):
            at = slice(128 * half, 128 * (half + 1))
            parts = [[], [], []]
            for j in range(UNITS // 2):
                row = items_ref[item, half * (UNITS // 2) + j]
                for n in range(3):
                    parts[n].append(kvp_s[n, pl.ds(row, 8), :])
            places.append(parts[2])
            keys = jnp.concatenate(parts[0], 0).astype(bf16)
            v_s[pl.ds(pl.multiple_of((slot & 7) * 256 + 128 * half, 128), 128), :] = (
                jnp.concatenate(parts[1], 0).astype(bf16)
            )
            qc = q_s[pl.ds(starts[half], CHUNK), :]
            qq = jnp.concatenate([qc, qc], 0).astype(bf16)
            q_exp = jnp.concatenate([qq * m for m in head_masks], 0)
            logit_s[pl.ds(pl.multiple_of((slot & 3) * 64, 64), 64), at] = lax.dot_general(
                q_exp, keys, contract_last, preferred_element_type=f32
            )
            yield
        turned = jnp.transpose(
            jnp.concatenate([jnp.where(lane < 64, x, y) for x, y in zip(*places)], 0)
        )
        yield
        for half in range(2):
            at = slice(128 * half, 128 * (half + 1))
            qp = qp_s[pl.ds(starts[half], CHUNK), :]
            r2 = 0.0
            for a in range(3):
                diff = qp[:, a : a + 1] - turned[64 * half + a : 64 * half + a + 1, :]
                r2 = r2 + diff * diff
            r2_s[:, at] = r2
            yield

    def stage_g(r2_both, slot):
        scale = math.sqrt(SHARPNESS * math.log2(math.e))
        for half in range(2):
            at = slice(128 * half, 128 * (half + 1))
            r2 = r2_both[:, at]
            valid = r2 < CUTOFF * CUTOFF
            inside = 1.0 - r2 * (1.0 / (CUTOFF * CUTOFF))
            env_s[pl.ds(pl.multiple_of((slot & 3) * 8, 8), 8), at] = jnp.where(
                valid, 2.0 * jnp.log(jnp.where(valid, inside, 1.0)), MASKED
            )
            r = jnp.sqrt(r2) * scale
            yield
            for k in range(0, 16, 2):
                two = []
                for kk in (k, k + 1):
                    t = r - (CUTOFF / 15 * kk) * scale
                    two.append(jnp.exp2(-(t * t)))
                basis_s[8 * k : 8 * k + 16, at] = jnp.concatenate(two, 0).astype(bf16)
                yield

    def stage_b(hidden, base):
        for t in range(0, hidden.shape[0], 16):
            bias = b1_ref[base + t : base + t + 16, :]
            x = hidden[t : t + 16] + jnp.concatenate([bias, bias], 1)
            active_s[base + t : base + t + 16, :] = (x + x * jnp.tanh(x)).astype(bf16)
            yield

    def stage_c(item, logits, env, expos):
        wide, _ = query_rows(item)
        dens = [[], []]
        for h in range(HEADS):
            rows = [
                logits[8 * h : 8 * h + 8, 128 * i : 128 * i + 128] + env[:, 128 * i : 128 * i + 128]
                for i in range(2)
            ]
            tops = [jnp.max(row, axis=1, keepdims=True) for row in rows]
            both = jnp.maximum(tops[0], tops[1])
            yield
            for i in range(2):
                top = jnp.where(wide != 0, both, tops[i])
                expo = jnp.exp(rows[i] - top)
                expos[i].append(expo)
                dens[i].append(jnp.sum(expo, axis=1, keepdims=True))
            yield
        for i in range(2):
            den = jnp.broadcast_to(dens[i][0], (8, 128))
            for h in range(1, HEADS):
                den = jnp.where(head_of == h, dens[i][h], den)
            den_s[:, 128 * i : 128 * (i + 1)] = den
            yield

    def stage_e(expos, filt):
        for h in range(0, HEADS, 2):
            for i in range(2):
                at = slice(128 * i, 128 * (i + 1))
                two = [expos[i][h + n] * filt[8 * (h + n) : 8 * (h + n) + 8, at] for n in range(2)]
                coef_s[8 * h : 8 * h + 16, at] = jnp.concatenate(two, 0).astype(bf16)
            yield

    def stage_d(item, nums, dens):
        wide, starts = query_rows(item)
        yield
        yield
        yield
        res = []
        for i in range(2):
            one = nums[i][0:8]
            for h in range(1, HEADS):
                one = jnp.where(head_of == h, nums[i][8 * h : 8 * h + 8], one)
            res.append(one)
            yield
        for i in range(2):
            num = jnp.where(wide != 0, res[0] + res[1], res[i])
            den = jnp.where(wide != 0, dens[0] + dens[1], dens[i])
            acc_s[pl.ds(starts[i], CHUNK), :] = num / jnp.maximum(den, 1.0)
            yield

    def in_turns(*turns):
        turns = list(turns)
        while turns:
            for turn in list(turns):
                if next(turn, turns) is turns:
                    turns.remove(turn)

    def step(i, carry):
        basis = basis_s[...]
        r2 = r2_s[...]
        logits = logit_s[pl.ds(pl.multiple_of(((i + 1) & 3) * 64, 64), 64), :]
        env = env_s[pl.ds(pl.multiple_of(((i + 1) & 3) * 8, 8), 8), :]
        coef = coef_s[...]
        dens = [den_s[:, 128 * n : 128 * (n + 1)] for n in range(2)]
        active = active_s[...]
        at_v = pl.multiple_of((i & 7) * 256, 256)
        values = [v_s[pl.ds(at_v + 128 * n, 128), :] for n in range(2)]
        filt = [
            jnp.dot(
                w2_ref[:, top_half * n : top_half * (n + 1)],
                active[top_half * n : top_half * (n + 1)],
                preferred_element_type=f32,
            )
            for n in range(2)
        ]
        filt = filt[0] + filt[1]
        nums = [
            jnp.dot(coef[:, 128 * n : 128 * (n + 1)], values[n], preferred_element_type=f32)
            for n in range(2)
        ]
        first = jnp.dot(w1_ref[:top_half], basis, preferred_element_type=f32)
        second = jnp.dot(w1_ref[top_half:], basis, preferred_element_type=f32)
        expos = [[], []]
        in_turns(stage_c(order_ref[i + 1], logits, env, expos), stage_d(order_ref[i], nums, dens), stage_g(r2, i + 3))
        in_turns(stage_b(first, 0), stage_b(second, top_half), stage_a(order_ref[i + 4], i + 4), stage_e(expos, filt))
        return carry

    lax.fori_loop(0, total, step, 0)

    def finish(q, carry):
        at = pl.ds(pl.multiple_of(q * ATOM_BLOCK, ATOM_BLOCK), ATOM_BLOCK)
        row_id = lax.broadcasted_iota(jnp.int32, (ATOM_BLOCK, 128), 0) + q * ATOM_BLOCK
        out_ref[at, :] = jnp.where(row_id < count, acc_s[at, :], 0.0).astype(bf16)
        return carry

    lax.fori_loop(0, blocks, finish, 0)


def attend(line, row, lists, srcs, wq, wkv, w1, b1, w2):
    blocks = lists.shape[0]
    channels = srcs[0].shape[2]
    smem = pl.BlockSpec(memory_space=pltpu.SMEM)
    vmem = pl.BlockSpec(memory_space=pltpu.VMEM)
    hbm = pl.BlockSpec(memory_space=pl.ANY)
    f32 = jnp.float32
    slots = blocks * ATOM_BLOCK
    table = (slots // CHUNK + 8, 128)
    return pl.pallas_call(
        attend_kernel,
        out_shape=jax.ShapeDtypeStruct((slots, channels), jnp.bfloat16),
        in_specs=[smem] * 3 + [hbm] * SOURCES + [vmem] * 5,
        out_specs=vmem,
        scratch_shapes=[
            pltpu.VMEM((blocks, KEY_BLOCKS, ROWS, channels), jnp.bfloat16),
            pltpu.SemaphoreType.DMA((blocks, KEY_BLOCKS)),
            pltpu.VMEM((3, slots * KEY_BLOCKS + 8, 128), f32),
            pltpu.VMEM((slots + 8, 128), f32),
            pltpu.VMEM((slots + 8, 128), f32),
            pltpu.VMEM((slots + 8, 128), f32),
            pltpu.VMEM((128, 256), jnp.bfloat16),
            pltpu.VMEM((512, 256), jnp.bfloat16),
            pltpu.VMEM((256, 256), f32),
            pltpu.VMEM((64, 256), jnp.bfloat16),
            pltpu.VMEM((8, 256), f32),
            pltpu.VMEM((2048, 128), jnp.bfloat16),
            pltpu.VMEM((8, 256), f32),
            pltpu.VMEM((32, 256), f32),
            pltpu.VMEM(table, jnp.int32),
            pltpu.SemaphoreType.DMA((blocks + 1,)),
            pltpu.SMEM(table, jnp.int32),
            pltpu.SMEM((slots // CHUNK + 8,), jnp.int32),
        ],
        name="attend",
    )(line, row, lists, *srcs, wq, wkv, w1, b1, w2)


def shift(x, axis, by):
    size = lax.axis_size(axis)
    return lax.ppermute(x, axis, [(i, (i + by) % size) for i in range(size)])


def shards(
    features, positions, counts, neighbours, w_query, w_key, w_value, w_radial, b_radial, w_head
):
    row = lax.axis_index("gx")
    rows = lax.axis_size("gx")
    line = counts[:, 0]
    place = (counts.T, row[None])
    light, extra = make_payload(*place, features[0, 0], positions.transpose(0, 2, 1, 3)[0])
    dense = line > LIGHT_BLOCKS * ATOM_BLOCK
    extra = jnp.where(
        dense[(row - 1) % rows],
        shift(extra, "gx", 1),
        jnp.where(dense[(row + 1) % rows], shift(extra, "gx", -1), extra),
    )
    low, high = shift(light, "gy", 1), shift(light, "gy", -1)
    further = [shift(extra, "gy", 1), extra, shift(extra, "gy", -1)]
    low, high, _ = lax.optimization_barrier((low, high, extra))
    column = jnp.concatenate([low, light, high], 0)
    srcs = [shift(column, "gx", 1), column, shift(column, "gx", -1)] + further
    wkv, w1, b1, w2 = make_weights(w_key, w_value, w_radial, b_radial, w_head)
    out = attend(*place, neighbours[0, 0], srcs, w_query, wkv, w1, b1, w2)
    return out[None, None]


def solution(mesh):
    in_specs = (
        P("gx", "gy", None, None),
        P("gx", "gy", None, None),
        P(None, "gy"),
        P("gx", "gy", None, None),
        P(), P(), P(), P(), P(), P(),
    )
    out_specs = P("gx", "gy", None, None)
    return jax.shard_map(shards, mesh=mesh, in_specs=in_specs, out_specs=out_specs, check_vma=False)
```

```python
import math

import jax
import jax.numpy as jnp
from jax import lax
from jax.experimental import pallas as pl
from jax.experimental.pallas import tpu as pltpu
from jax.sharding import PartitionSpec as P

HEADS = 8
ATOM_BLOCK = 128
KEY_BLOCKS = 4
CUTOFF = 6.0
SHARPNESS = 4.0
MASKED = -1e30
LENGTH = 576.0
FAR = float(2**20)
POS_ROWS = 16
ROWS = ATOM_BLOCK + POS_ROWS
CHUNK = 8
LIGHT_BLOCKS = 7
UNITS = 32
SOURCES = 6


def payload_kernel(line_ref, row_ref, rows_ref, pos_ref, light_ref, extra_ref):
    f32 = jnp.float32
    bf16 = jnp.bfloat16
    count = line_ref[0, row_ref[0]]
    lane = lax.broadcasted_iota(jnp.int32, (1, ATOM_BLOCK), 1)
    high_count = jnp.broadcast_to((count // 16 * 16).astype(f32), (1, ATOM_BLOCK))
    low_count = jnp.broadcast_to((count % 16).astype(f32), (1, ATOM_BLOCK))
    zeros = jnp.zeros((2, ATOM_BLOCK), f32)
    for q in range(rows_ref.shape[0] // ATOM_BLOCK):
        light = q < LIGHT_BLOCKS
        out = light_ref.at[q] if light else extra_ref.at[q - LIGHT_BLOCKS]
        at = slice(q * ATOM_BLOCK, (q + 1) * ATOM_BLOCK)
        out[:ATOM_BLOCK, :] = rows_ref[at, :]
        pos = [pos_ref[a, :, at] for a in range(3)]
        pos[2] = jnp.where(lane + q * ATOM_BLOCK < count, pos[2], FAR)
        pos = jnp.concatenate(pos, 0)
        hi = pos.astype(bf16).astype(f32)
        rest = pos - hi
        mid = rest.astype(bf16).astype(f32)
        begin = jnp.full((1, ATOM_BLOCK), float(q * ATOM_BLOCK), f32)
        terms = [hi, mid, rest - mid, zeros, high_count, low_count, begin, zeros]
        out[ATOM_BLOCK:, :] = jnp.concatenate(terms, 0).astype(bf16)


def make_payload(line, row, rows, pos):
    blocks = rows.shape[0] // ATOM_BLOCK
    return pl.pallas_call(
        payload_kernel,
        out_shape=[
            jax.ShapeDtypeStruct((n, ROWS, rows.shape[1]), jnp.bfloat16)
            for n in (LIGHT_BLOCKS, blocks - LIGHT_BLOCKS)
        ],
        in_specs=[pl.BlockSpec(memory_space=pltpu.SMEM)] * 2
        + [pl.BlockSpec(memory_space=pltpu.VMEM)] * 2,
        out_specs=[pl.BlockSpec(memory_space=pltpu.VMEM)] * 2,
        name="payload",
    )(line, row, rows, pos)


def weights_kernel(key_ref, value_ref, radial_ref, bias_ref, head_ref, kv_ref, w1_ref, b1_ref, w2_ref):
    f32 = jnp.float32
    bf16 = jnp.bfloat16

    def split(shape, axis):
        index = lax.broadcasted_iota(jnp.int32, shape, axis)
        return lax.shift_right_logical(index, 3), index & (CHUNK - 1)

    def pick(condition):
        return jnp.where(condition, 1.0, 0.0).astype(bf16)

    def index(shape, axis):
        return lax.broadcasted_iota(jnp.int32, shape, axis)

    basis, radial = radial_ref.shape
    width, tall, heads = basis * CHUNK, radial * CHUNK, HEADS * CHUNK
    kv_ref[:, : key_ref.shape[1]] = key_ref[...]
    kv_ref[:, key_ref.shape[1] :] = value_ref[...]
    first = (((0,), (0,)), ((), ()))
    spread = pick(split((basis, width), 1)[0] == index((basis, width), 0))
    w1 = lax.dot_general(radial_ref[...], spread, first, preferred_element_type=f32)
    rows = pick(split((tall, radial), 0)[0] == index((tall, radial), 1))
    w1 = jnp.dot(rows, w1.astype(bf16), preferred_element_type=f32)
    same = split((tall, width), 0)[1] == split((tall, width), 1)[1]
    w1_ref[...] = jnp.where(same, 0.5 * w1, 0.0).astype(bf16)
    spread = pick(split((radial, tall), 1)[0] == index((radial, tall), 0))
    w2 = lax.dot_general(head_ref[...], spread, first, preferred_element_type=f32)
    rows = pick(split((heads, HEADS), 0)[0] == index((heads, HEADS), 1))
    w2 = jnp.dot(rows, w2.astype(bf16), preferred_element_type=f32)
    same = split((heads, tall), 0)[1] == split((heads, tall), 1)[1]
    w2_ref[...] = jnp.where(same, w2, 0.0).astype(bf16)
    here = split((tall, radial), 0)[0] == index((tall, radial), 1)
    bias = jnp.sum(jnp.where(here, 0.5 * bias_ref[...], 0.0), axis=1, keepdims=True)
    b1_ref[...] = jnp.broadcast_to(bias, b1_ref.shape)


def make_weights(w_key, w_value, w_radial, b_radial, w_head):
    basis, radial = w_radial.shape
    channels = w_key.shape[0]
    bf16 = jnp.bfloat16
    return pl.pallas_call(
        weights_kernel,
        out_shape=[
            jax.ShapeDtypeStruct((channels, 2 * channels), bf16),
            jax.ShapeDtypeStruct((radial * CHUNK, basis * CHUNK), bf16),
            jax.ShapeDtypeStruct((radial * CHUNK, 128), jnp.float32),
            jax.ShapeDtypeStruct((HEADS * CHUNK, radial * CHUNK), bf16),
        ],
        in_specs=[pl.BlockSpec(memory_space=pltpu.VMEM)] * 5,
        out_specs=[pl.BlockSpec(memory_space=pltpu.VMEM)] * 4,
        name="weights",
    )(w_key, w_value, w_radial, b_radial[None], w_head)


def attend_kernel(line_ref, row_ref, lists_ref, *refs):
    srcs = refs[:SOURCES]
    wq_ref, wkv_ref, w1_ref, b1_ref, w2_ref, out_ref = refs[SOURCES : SOURCES + 6]
    xbuf, sems, kvp_s, q_s, qp_s, acc_s, basis_s, active_s, logit_s, coef_s, den_s, v_s, r2_s, env_s, table_v, table_sem, items_ref, order_ref = refs[SOURCES + 6 :]
    blocks = out_ref.shape[0] // ATOM_BLOCK
    slots = blocks * ATOM_BLOCK
    dummy = blocks * KEY_BLOCKS * ATOM_BLOCK
    count = line_ref[0, row_ref[0]]
    chunks = ATOM_BLOCK // CHUNK
    none = blocks * chunks
    live_blocks = (count + ATOM_BLOCK - 1) // ATOM_BLOCK
    bf16 = jnp.bfloat16
    f32 = jnp.float32

    def listed(q, e):
        item = lists_ref[q, e]
        brick = lax.shift_right_logical(item, 4)
        part = lax.shift_right_logical(brick * 11, 5)
        return item, item & (blocks - 1), part, brick - 3 * part

    def fetch(q, carry):
        for e in range(KEY_BLOCKS):
            _, block, part, side = listed(q, e)
            light = block < LIGHT_BLOCKS
            source = jnp.where(light, part, 3 + side)
            block = jnp.where(light, side * LIGHT_BLOCKS + block, block - LIGHT_BLOCKS)

            def among(low, high):
                if high - low == 1:
                    pltpu.make_async_copy(
                        srcs[low].at[block], xbuf.at[q, e], sems.at[q, e]
                    ).start()
                    return
                middle = (low + high) // 2
                pl.when(source < middle)(lambda: among(low, middle))
                pl.when(source >= middle)(lambda: among(middle, high))

            if e == 0:
                pl.when(light)(lambda: among(1, 2))
                pl.when(jnp.logical_not(light))(lambda: among(4, 5))
            else:
                among(0, SOURCES)
        return carry

    lax.fori_loop(0, live_blocks, fetch, 0)

    lane = lax.broadcasted_iota(jnp.int32, (CHUNK, 128), 1)
    head_of = lane // 16
    sub2 = lax.broadcasted_iota(jnp.int32, (2 * CHUNK, 128), 0)
    lane2 = lax.broadcasted_iota(jnp.int32, (2 * CHUNK, 128), 1)
    head_masks = [
        jnp.where(lane2 // 16 == 2 * i + sub2 // CHUNK, 1.0, 0.0).astype(bf16) for i in range(4)
    ]

    kvp_s[0, pl.ds(dummy, 8), :] = jnp.zeros((8, 128), f32)
    kvp_s[1, pl.ds(dummy, 8), :] = jnp.zeros((8, 128), f32)
    kvp_s[2, pl.ds(dummy, 8), :] = jnp.where(
        lane % 64 == 2, FAR, 0.0
    ).astype(f32)
    q_s[pl.ds(slots, 8), :] = jnp.zeros((8, 128), f32)
    qp_s[pl.ds(slots, 8), :] = jnp.zeros((8, 128), f32)
    for ref in (basis_s, active_s, logit_s, coef_s, den_s, v_s, r2_s, env_s):
        ref[...] = jnp.zeros_like(ref)

    def project(q, carry):
        for e in range(KEY_BLOCKS):
            pltpu.make_async_copy(srcs[0].at[0], xbuf.at[q, e], sems.at[q, e]).wait()

        unit = lax.broadcasted_iota(jnp.int32, (chunks, 128), 1).astype(f32)
        chunk_id = lax.broadcasted_iota(jnp.int32, (chunks, 128), 0)
        first = (q * ATOM_BLOCK + CHUNK * chunk_id).astype(f32)
        rows = jnp.full((chunks, 128), float(dummy), f32)
        ends = jnp.zeros((chunks, 128), f32)
        mats = []
        for e in range(KEY_BLOCKS):
            _, _, part, side = listed(q, e)
            shift_x = (part - 1).astype(f32) * CUTOFF
            shift_y = (side - 1).astype(f32) * CUTOFF
            m = xbuf[q, e, ATOM_BLOCK:, :].astype(f32)
            key_count = m[11:12] + m[12:13]
            ratio = key_count / count.astype(f32)
            reach = key_count * (CUTOFF / LENGTH)
            begin = m[13:14]
            low = jnp.floor(first * ratio - reach - 1.05) + 1.0 - begin
            high = jnp.ceil((first + CHUNK) * ratio + reach + 0.05) - 1.0 - begin
            low = jnp.maximum(low, 0.0)
            high = jnp.minimum(high, jnp.minimum(key_count - 1.0 - begin, ATOM_BLOCK - 1.0))
            size = jnp.where(first < count.astype(f32), jnp.maximum(high - low + 1.0, 0.0), 0.0)
            units = jnp.floor((size + 7.0) * 0.125)
            low = jnp.minimum(low, ATOM_BLOCK - 8.0 * units)
            base = ((q * KEY_BLOCKS + e) * ATOM_BLOCK).astype(f32)
            rows = jnp.where(
                (unit >= ends) & (unit < ends + units), base + low + 8.0 * (unit - ends), rows
            )
            ends = ends + units
            place = (m[0:3] + m[3:6]) + m[6:9]
            axis = lax.broadcasted_iota(jnp.int32, (3, 128), 0)
            place = place + jnp.where(axis == 0, shift_x, jnp.where(axis == 1, shift_y, 0.0))
            mats.append(jnp.concatenate([place, jnp.zeros((13, 128), f32)], 0))
        turned = jnp.transpose(jnp.concatenate(mats + mats, 0))
        own = pl.ds(pl.multiple_of(q * ATOM_BLOCK, ATOM_BLOCK), ATOM_BLOCK)
        qp_s[own, :] = turned
        for e in range(KEY_BLOCKS):
            at = pl.ds(
                pl.multiple_of((q * KEY_BLOCKS + e) * ATOM_BLOCK, ATOM_BLOCK), ATOM_BLOCK
            )
            kvp_s[2, at, :] = pltpu.roll(turned, 128 - 16 * e, 1) if e else turned
            x = xbuf[q, e, :ATOM_BLOCK, :]
            kv = jnp.dot(x, wkv_ref[...], preferred_element_type=f32)
            kv = kv.astype(bf16).astype(f32)
            kvp_s[0, at, :] = kv[:, :128]
            kvp_s[1, at, :] = kv[:, 128:]
        query = jnp.dot(xbuf[q, 0, :ATOM_BLOCK, :], wq_ref[...], preferred_element_type=f32)
        q_s[own, :] = query.astype(bf16).astype(f32) * 0.25
        wide = jnp.where(ends > UNITS // 2, 1.0, 0.0)
        even = chunk_id % 2 == 0
        wide = jnp.maximum(
            wide, jnp.where(even, pltpu.roll(wide, chunks - 1, 0), pltpu.roll(wide, 1, 0))
        )
        following = pltpu.roll(pltpu.roll(rows, chunks - 1, 0), UNITS // 2, 1)
        joined = (wide < 0.5) & (unit >= UNITS // 2)
        rows = jnp.where(joined, following, rows)
        rows = jnp.where(unit == UNITS, wide, rows)
        at = pl.ds(pl.multiple_of(q * chunks, chunks), chunks)
        table_v[at, :] = rows.astype(jnp.int32)
        pltpu.make_async_copy(table_v.at[at], items_ref.at[at], table_sem.at[q]).start()
        return carry

    end = pl.ds(none, 8)
    table_v[end, :] = jnp.where(lane == UNITS, 0, dummy)
    last = pltpu.make_async_copy(table_v.at[end], items_ref.at[end], table_sem.at[blocks])
    last.start()
    lax.fori_loop(0, live_blocks, project, 0)
    last.wait()

    def await_table(q, carry):
        at = pl.ds(pl.multiple_of(q * chunks, chunks), chunks)
        pltpu.make_async_copy(table_v.at[at], items_ref.at[at], table_sem.at[q]).wait()
        return carry

    lax.fori_loop(0, live_blocks, await_table, 0)

    def enlist(p, n):
        order_ref[n] = 2 * p
        order_ref[n + 1] = 2 * p + 1
        return n + 1 + items_ref[2 * p, UNITS]

    for n in range(4):
        order_ref[n] = none
    total = lax.fori_loop(
        0, lax.shift_right_logical(count + 2 * CHUNK - 1, 4), enlist, 4
    )
    for n in range(4):
        order_ref[total + n] = none

    contract_last = (((1,), (1,)), ((), ()))
    top_half = w1_ref.shape[0] // 2

    def query_rows(item):
        pair = lax.shift_right_logical(item, 1)
        wide = items_ref[item, UNITS]
        first = jnp.where(wide != 0, item, 2 * pair)
        second = jnp.where(wide != 0, item, 2 * pair + 1)
        first = jnp.minimum(first * CHUNK, slots)
        second = jnp.minimum(second * CHUNK, slots)
        return wide, (pl.multiple_of(first, CHUNK), pl.multiple_of(second, CHUNK))


    def stage_a(item, slot):
        _, starts = query_rows(item)
        places = []
        for half in range(2):
            at = slice(128 * half, 128 * (half + 1))
            parts = [[], [], []]
            for j in range(UNITS // 2):
                row = items_ref[item, half * (UNITS // 2) + j]
                for n in range(3):
                    parts[n].append(kvp_s[n, pl.ds(row, 8), :])
            places.append(parts[2])
            keys = jnp.concatenate(parts[0], 0).astype(bf16)
            v_s[pl.ds(pl.multiple_of((slot & 7) * 256 + 128 * half, 128), 128), :] = (
                jnp.concatenate(parts[1], 0).astype(bf16)
            )
            qc = q_s[pl.ds(starts[half], CHUNK), :]
            qq = jnp.concatenate([qc, qc], 0).astype(bf16)
            q_exp = jnp.concatenate([qq * m for m in head_masks], 0)
            logit_s[pl.ds(pl.multiple_of((slot & 3) * 64, 64), 64), at] = lax.dot_general(
                q_exp, keys, contract_last, preferred_element_type=f32
            )
            yield
        turned = jnp.transpose(
            jnp.concatenate([jnp.where(lane < 64, x, y) for x, y in zip(*places)], 0)
        )
        yield
        for half in range(2):
            at = slice(128 * half, 128 * (half + 1))
            qp = qp_s[pl.ds(starts[half], CHUNK), :]
            r2 = 0.0
            for a in range(3):
                diff = qp[:, a : a + 1] - turned[64 * half + a : 64 * half + a + 1, :]
                r2 = r2 + diff * diff
            r2_s[:, at] = r2
            yield

    def stage_g(r2_both, slot):
        scale = math.sqrt(SHARPNESS * math.log2(math.e))
        for half in range(2):
            at = slice(128 * half, 128 * (half + 1))
            r2 = r2_both[:, at]
            valid = r2 < CUTOFF * CUTOFF
            inside = 1.0 - r2 * (1.0 / (CUTOFF * CUTOFF))
            env_s[pl.ds(pl.multiple_of((slot & 3) * 8, 8), 8), at] = jnp.where(
                valid, 2.0 * jnp.log(jnp.where(valid, inside, 1.0)), MASKED
            )
            r = jnp.sqrt(r2) * scale
            yield
            for k in range(0, 16, 2):
                two = []
                for kk in (k, k + 1):
                    t = r - (CUTOFF / 15 * kk) * scale
                    two.append(jnp.exp2(-(t * t)))
                basis_s[8 * k : 8 * k + 16, at] = jnp.concatenate(two, 0).astype(bf16)
                yield

    def stage_b(hidden, base):
        for t in range(0, hidden.shape[0], 16):
            bias = b1_ref[base + t : base + t + 16, :]
            x = hidden[t : t + 16] + jnp.concatenate([bias, bias], 1)
            active_s[base + t : base + t + 16, :] = (x + x * jnp.tanh(x)).astype(bf16)
            yield

    def stage_c(item, logits, env, expos):
        wide, _ = query_rows(item)
        dens = [[], []]
        for h in range(HEADS):
            rows = [
                logits[8 * h : 8 * h + 8, 128 * i : 128 * i + 128] + env[:, 128 * i : 128 * i + 128]
                for i in range(2)
            ]
            tops = [jnp.max(row, axis=1, keepdims=True) for row in rows]
            both = jnp.maximum(tops[0], tops[1])
            yield
            for i in range(2):
                top = jnp.where(wide != 0, both, tops[i])
                expo = jnp.exp(rows[i] - top)
                expos[i].append(expo)
                dens[i].append(jnp.sum(expo, axis=1, keepdims=True))
            yield
        for i in range(2):
            den = jnp.broadcast_to(dens[i][0], (8, 128))
            for h in range(1, HEADS):
                den = jnp.where(head_of == h, dens[i][h], den)
            den_s[:, 128 * i : 128 * (i + 1)] = den
            yield

    def stage_e(expos, filt):
        for h in range(0, HEADS, 2):
            for i in range(2):
                at = slice(128 * i, 128 * (i + 1))
                two = [expos[i][h + n] * filt[8 * (h + n) : 8 * (h + n) + 8, at] for n in range(2)]
                coef_s[8 * h : 8 * h + 16, at] = jnp.concatenate(two, 0).astype(bf16)
            yield

    def stage_d(item, nums, dens):
        wide, starts = query_rows(item)
        yield
        yield
        yield
        res = []
        for i in range(2):
            one = nums[i][0:8]
            for h in range(1, HEADS):
                one = jnp.where(head_of == h, nums[i][8 * h : 8 * h + 8], one)
            res.append(one)
            yield
        for i in range(2):
            num = jnp.where(wide != 0, res[0] + res[1], res[i])
            den = jnp.where(wide != 0, dens[0] + dens[1], dens[i])
            acc_s[pl.ds(starts[i], CHUNK), :] = num / jnp.maximum(den, 1.0)
            yield

    def in_turns(*turns):
        turns = list(turns)
        while turns:
            for turn in list(turns):
                if next(turn, turns) is turns:
                    turns.remove(turn)

    def step(i, carry):
        basis = basis_s[...]
        r2 = r2_s[...]
        logits = logit_s[pl.ds(pl.multiple_of(((i + 1) & 3) * 64, 64), 64), :]
        env = env_s[pl.ds(pl.multiple_of(((i + 1) & 3) * 8, 8), 8), :]
        coef = coef_s[...]
        dens = [den_s[:, 128 * n : 128 * (n + 1)] for n in range(2)]
        active = active_s[...]
        at_v = pl.multiple_of((i & 7) * 256, 256)
        values = [v_s[pl.ds(at_v + 128 * n, 128), :] for n in range(2)]
        filt = [
            jnp.dot(
                w2_ref[:, top_half * n : top_half * (n + 1)],
                active[top_half * n : top_half * (n + 1)],
                preferred_element_type=f32,
            )
            for n in range(2)
        ]
        filt = filt[0] + filt[1]
        nums = [
            jnp.dot(coef[:, 128 * n : 128 * (n + 1)], values[n], preferred_element_type=f32)
            for n in range(2)
        ]
        first = jnp.dot(w1_ref[:top_half], basis, preferred_element_type=f32)
        second = jnp.dot(w1_ref[top_half:], basis, preferred_element_type=f32)
        expos = [[], []]
        in_turns(stage_c(order_ref[i + 1], logits, env, expos), stage_d(order_ref[i], nums, dens), stage_g(r2, i + 3))
        in_turns(stage_b(first, 0), stage_b(second, top_half), stage_a(order_ref[i + 4], i + 4), stage_e(expos, filt))
        return carry

    lax.fori_loop(0, total, step, 0)

    def finish(q, carry):
        at = pl.ds(pl.multiple_of(q * ATOM_BLOCK, ATOM_BLOCK), ATOM_BLOCK)
        row_id = lax.broadcasted_iota(jnp.int32, (ATOM_BLOCK, 128), 0) + q * ATOM_BLOCK
        out_ref[at, :] = jnp.where(row_id < count, acc_s[at, :], 0.0).astype(bf16)
        return carry

    lax.fori_loop(0, blocks, finish, 0)


def attend(line, row, lists, srcs, wq, wkv, w1, b1, w2):
    blocks = lists.shape[0]
    channels = srcs[0].shape[2]
    smem = pl.BlockSpec(memory_space=pltpu.SMEM)
    vmem = pl.BlockSpec(memory_space=pltpu.VMEM)
    hbm = pl.BlockSpec(memory_space=pl.ANY)
    f32 = jnp.float32
    slots = blocks * ATOM_BLOCK
    table = (slots // CHUNK + 8, 128)
    return pl.pallas_call(
        attend_kernel,
        out_shape=jax.ShapeDtypeStruct((slots, channels), jnp.bfloat16),
        in_specs=[smem] * 3 + [hbm] * SOURCES + [vmem] * 5,
        out_specs=vmem,
        scratch_shapes=[
            pltpu.VMEM((blocks, KEY_BLOCKS, ROWS, channels), jnp.bfloat16),
            pltpu.SemaphoreType.DMA((blocks, KEY_BLOCKS)),
            pltpu.VMEM((3, slots * KEY_BLOCKS + 8, 128), f32),
            pltpu.VMEM((slots + 8, 128), f32),
            pltpu.VMEM((slots + 8, 128), f32),
            pltpu.VMEM((slots + 8, 128), f32),
            pltpu.VMEM((128, 256), jnp.bfloat16),
            pltpu.VMEM((512, 256), jnp.bfloat16),
            pltpu.VMEM((256, 256), f32),
            pltpu.VMEM((64, 256), jnp.bfloat16),
            pltpu.VMEM((8, 256), f32),
            pltpu.VMEM((2048, 128), jnp.bfloat16),
            pltpu.VMEM((8, 256), f32),
            pltpu.VMEM((32, 256), f32),
            pltpu.VMEM(table, jnp.int32),
            pltpu.SemaphoreType.DMA((blocks + 1,)),
            pltpu.SMEM(table, jnp.int32),
            pltpu.SMEM((slots // CHUNK + 8,), jnp.int32),
        ],
        name="attend",
    )(line, row, lists, *srcs, wq, wkv, w1, b1, w2)


def shift(x, axis, by):
    size = lax.axis_size(axis)
    return lax.ppermute(x, axis, [(i, (i + by) % size) for i in range(size)])


def shards(
    features, positions, counts, neighbours, w_query, w_key, w_value, w_radial, b_radial, w_head
):
    row = lax.axis_index("gx")
    rows = lax.axis_size("gx")
    line = counts[:, 0]
    place = (counts.T, row[None])
    light, extra = make_payload(*place, features[0, 0], positions.transpose(0, 2, 1, 3)[0])
    dense = line > LIGHT_BLOCKS * ATOM_BLOCK
    before, after = shift(extra, "gx", 1), shift(extra, "gx", -1)
    extra = jnp.where(
        dense[(row - 1) % rows], before, jnp.where(dense[(row + 1) % rows], after, extra)
    )
    low, high = shift(light, "gy", 1), shift(light, "gy", -1)
    further = [shift(extra, "gy", 1), extra, shift(extra, "gy", -1)]
    column = jnp.concatenate([low, light, high], 0)
    srcs = [shift(column, "gx", 1), column, shift(column, "gx", -1)] + further
    wkv, w1, b1, w2 = make_weights(w_key, w_value, w_radial, b_radial, w_head)
    out = attend(*place, neighbours[0, 0], srcs, w_query, wkv, w1, b1, w2)
    return out[None, None]


def solution(mesh):
    in_specs = (
        P("gx", "gy", None, None),
        P("gx", "gy", None, None),
        P(None, "gy"),
        P("gx", "gy", None, None),
        P(), P(), P(), P(), P(), P(),
    )
    out_specs = P("gx", "gy", None, None)
    return jax.shard_map(shards, mesh=mesh, in_specs=in_specs, out_specs=out_specs, check_vma=False)
```
